32 devices in a mesh: dx: 4 (over y, core), dy: 4 (over z), band: 2 (over x).
Axes of the slice: x: 2, y: 2, z: 4, core: 2. Of those that a mesh axis runs over, the one named last changes fastest.
Arguments:
- states: float32 [24, 32, 8, 512], P('dx', 'dy', None, 'band'), may hold values from -6 to 6
- potential: float32 [24, 32, 8], P('dx', 'dy'), may hold values from -1 to 1
Outputs:
- orthonormal: float32 [24, 32, 8, 512], P('dx', 'dy', None, 'band')
The draws below stay inside these ranges and needn't reach their ends.
All inputs are finite; a program needn't handle non-finite values.
Results may differ from the reference program's by a relative error of at most 0.000073.
Values sent between devices are 32-bit elements; how exact they have to be, the bound alone decides.
No kernel may reach another device: no remote copies, remote signals or barrier semaphores. Data moves between devices by JAX's collectives and lax.ppermute only.
A program may use at most 64 MiB of HBM per device.

```python
import jax
import jax.numpy as jnp
from jax import lax

NZ = 8
NS = 512
DEGREE = 3
NX = 24
NY = 32


def block_levels(rng, dims, split, smallest, top_value):
    loudness, own = 1.0, jax.random.fold_in(rng, 6)
    for axis_at, blocks in split:
        heights = jnp.exp(jax.random.uniform(jax.random.fold_in(own, axis_at), (blocks,), jnp.float32, smallest / len(split), top_value / len(split)))
        loudness = loudness * jnp.repeat(heights, dims[axis_at] // blocks).reshape([-1 if axis == axis_at else 1 for axis in range(len(dims))])
    return loudness


def normal_values(key, shape, scale, limit, cuts=(), kind=jnp.bfloat16):
    entries = jax.random.normal(key, shape, jnp.float32) * scale
    if len(cuts) > 0:
        entries = block_levels(key, shape, cuts, -0.22, 0.18) * entries
    return jnp.clip(entries, min=-limit, max=limit).astype(kind)


def setup_inputs(seed: int = 0) -> dict:
    arg_keys = jax.random.split(jax.random.key(seed), 3)
    return {
        "states": normal_values(arg_keys[0], (NX, NY, NZ, NS), 1.0, 6.0, ((0, 4), (1, 4), (3, 2)), jnp.float32),
        "potential": jnp.clip(jax.random.uniform(arg_keys[1], (NX, NY, NZ), jnp.float32, -1.0, 1.0) * block_levels(arg_keys[1], (NX, NY, NZ), ((0, 4), (1, 4)), -0.4, 0.0), -1.0, 1.0),
    }


coeffs = (-5369.0 / 1800.0, 12.0 / 7.0, -15.0 / 56.0, 10.0 / 189.0, -1.0 / 112.0, 2.0 / 1925.0, -1.0 / 16632.0)
half_width = 5.0
centre_value = 7.0

def apply_ham(field, potential):
    lap = 3.0 * coeffs[0] * field
    for shift in range(1, 7):
        near = jnp.zeros_like(field)
        for axis in range(3):
            near = near + jnp.roll(field, shift, axis) + jnp.roll(field, -shift, axis)
        lap = lap + coeffs[shift] * near
    return -0.5 * lap + potential[..., None] * field

def reference(states, potential):
    prev = states
    cur = (apply_ham(states, potential) - centre_value * states) / half_width
    for step in range(1, DEGREE):
        nxt = 2.0 * (apply_ham(cur, potential) - centre_value * cur) / half_width - prev
        prev, cur = (cur, nxt)
    total = cur.shape[0] * cur.shape[1] * cur.shape[2]
    flat = cur.reshape(total, cur.shape[3])
    correlation = jnp.dot(flat.T.astype(jnp.float32), flat.astype(jnp.float32), precision=lax.Precision.HIGHEST, preferred_element_type=jnp.float32) / total
    factor = jnp.linalg.cholesky(correlation)
    eye = jnp.eye(correlation.shape[0], dtype=jnp.float32)
    inverse = jax.scipy.linalg.solve_triangular(factor, eye, lower=True)
    result = jnp.dot(flat.astype(jnp.float32), inverse.T.astype(jnp.float32), precision=lax.Precision.HIGHEST, preferred_element_type=jnp.float32)
    return result.reshape(cur.shape)
```

```python
import functools

import jax
import jax.numpy as jnp
from jax import lax
from jax.experimental import pallas as pl
from jax.experimental.pallas import tpu as pltpu
from jax.sharding import PartitionSpec as P

DEGREE = 3
LANES = 128
SUBLANES = 8
PANEL = 32

coeffs = (
    -5369.0 / 1800.0,
    12.0 / 7.0,
    -15.0 / 56.0,
    10.0 / 189.0,
    -1.0 / 112.0,
    2.0 / 1925.0,
    -1.0 / 16632.0,
)
WIDTH = len(coeffs) - 1
half_width = 5.0
centre_value = 7.0
VMEM = pl.BlockSpec(memory_space=pltpu.VMEM)
HIGHEST = lax.Precision.HIGHEST


def dot(a, b, dims):
    return lax.dot_general(a, b, (dims, ((), ())), precision=HIGHEST, preferred_element_type=jnp.float32)


def swap_groups(arrays, group):
    count = len(arrays)
    lane = lax.broadcasted_iota(jnp.int32, arrays[0].shape, 1)
    bit = 1
    while bit < count:
        upper = (lane // (group * bit)) % 2 == 1
        out = list(arrays)
        for i in range(count):
            if i & bit == 0:
                low, high = arrays[i], arrays[i | bit]
                out[i] = jnp.where(upper, pltpu.roll(high, group * bit, 1), low)
                out[i | bit] = jnp.where(upper, high, pltpu.roll(low, LANES - group * bit, 1))
        arrays = out
        bit *= 2
    return arrays


def pack_kernel(nz, states_ref, potential_ref, out_ref):
    columns = states_ref.shape[0] // nz
    arrays = [states_ref[pl.ds(z, columns, stride=nz), :] for z in range(nz)]
    for g, value in enumerate(swap_groups(arrays, LANES // nz)):
        out_ref[g, :columns, :] = value
    row = lax.broadcasted_iota(jnp.int32, (nz, LANES), 0)
    lane = lax.broadcasted_iota(jnp.int32, (nz, LANES), 1)
    packed = jnp.zeros((potential_ref.shape[1], LANES), jnp.float32)
    for x in range(potential_ref.shape[0]):
        spread = jnp.where(lane == row + nz * x, 1.0, 0.0)
        packed = packed + dot(potential_ref[x], spread, ((1,), (0,)))
    for g in range(nz):
        out_ref[g, columns:, :] = packed


def filter_kernel(nz, domains_y, size_x, size_y, in_ref, out_ref, field, older, potential):
    domains = in_ref.shape[0]
    total_x = size_x * (domains // domains_y)
    total_y = size_y * domains_y
    columns = size_x * size_y
    group = LANES // nz

    def place(i, x):
        return size_x * (i // domains_y) + x, size_y * (i % domains_y)

    packed = in_ref[:, columns:, :].reshape(domains * size_y, LANES)
    source = lax.broadcasted_iota(jnp.int32, (LANES, LANES), 0)
    target = lax.broadcasted_iota(jnp.int32, (LANES, LANES), 1)
    for x in range(size_x):
        spread = jnp.where(source == nz * x + target // group, 1.0, 0.0)
        values = dot(packed, spread, ((1,), (0,)))
        for i in range(domains):
            at_x, at_y = place(i, x)
            potential[at_x, at_y : at_y + size_y, :] = values[size_y * i : size_y * (i + 1)] - centre_value
            field[WIDTH + at_x, at_y : at_y + size_y, :] = in_ref[i, size_y * x : size_y * (x + 1), :]

    weights = [0.0] * nz
    for k in range(1, WIDTH + 1):
        weights[k % nz] += coeffs[k]
        weights[-k % nz] += coeffs[k]

    for step in range(DEGREE):
        for k in range(WIDTH):
            field[k] = field[total_x + k]
            field[WIDTH + total_x + k] = field[WIDTH + k]
        scale = 1.0 / half_width if step == 0 else 2.0 / half_width

        def body(x, carry, step=step, scale=scale):
            value = field[WIDTH + x]
            lap = (3.0 * coeffs[0] + weights[0]) * value
            for k in range(1, WIDTH + 1):
                near = field[WIDTH + x + k] + field[WIDTH + x - k]
                near = near + pltpu.roll(value, k, 0) + pltpu.roll(value, total_y - k, 0)
                lap = lap + coeffs[k] * near
            for k in range(1, nz):
                lap = lap + weights[k] * pltpu.roll(value, group * k, 1)
            result = (potential[x] * value - 0.5 * lap) * scale
            if step > 0:
                result = result - older[(step - 1) % 2, x]
            older[step % 2, x] = value if step + 1 < DEGREE else result
            spare[x] = result
            return carry

        spare = older.at[2]
        lax.fori_loop(0, total_x, body, 0, unroll=2)
        if step + 1 < DEGREE:
            field[WIDTH : WIDTH + total_x] = spare[...]

    for i in range(domains):
        for x in range(size_x):
            at_x, at_y = place(i, x)
            out_ref[i, size_y * x : size_y * (x + 1), :] = older[2, at_x, at_y : at_y + size_y, :]


def unpack_kernel(nz, in_ref, out_ref):
    columns = in_ref.shape[1]
    arrays = [in_ref[g] for g in range(nz)]
    for z, value in enumerate(swap_groups(arrays, LANES // nz)):
        out_ref[pl.ds(z, columns, stride=nz), :] = value


def gram_kernel(band_ref, own_ref, other_ref, out_ref):
    own = own_ref[...]
    half = own.shape[1] // 2
    rows = ((0,), (0,))
    diagonal = dot(own, own, rows)
    out_ref[0:half] = diagonal[:half, :half]
    out_ref[half : 2 * half] = diagonal[:half, half:]
    out_ref[2 * half : 3 * half] = diagonal[half:, half:]

    @pl.when(band_ref[0] == 0)
    def _():
        out_ref[3 * half :] = dot(own, other_ref[:, :half], rows)

    @pl.when(band_ref[0] == 1)
    def _():
        out_ref[3 * half :] = dot(other_ref[...], own[:, half:], rows)


def sum_kernel(total, in_ref, out_ref):
    value = in_ref[0]
    for i in range(1, in_ref.shape[0]):
        value = value + in_ref[i]
    value = value / total
    for i in range(out_ref.shape[0]):
        out_ref[i] = value


def spread_row(value, row):
    return jnp.broadcast_to(value[row : row + 1, :], value.shape)


def inverse_factor(matrix, inverse):
    size = matrix.shape[0]
    tiles = PANEL // SUBLANES
    strips = size // LANES
    per_strip = LANES // PANEL
    sublane = lax.broadcasted_iota(jnp.int32, (SUBLANES, LANES), 0)
    lane = lax.broadcasted_iota(jnp.int32, (SUBLANES, LANES), 1)

    def step(p, carry):
        start = pl.multiple_of(p * PANEL, PANEL)
        strip = pl.multiple_of((p // per_strip) * LANES, LANES)
        shift = (p % per_strip) * PANEL
        block = pltpu.roll(matrix[pl.ds(start, PANEL), pl.ds(strip, LANES)], lax.rem(LANES - shift, LANES), 1)
        column = [
            [
                jnp.broadcast_to(block[SUBLANES * t : SUBLANES * (t + 1), j : j + 1], (SUBLANES, LANES))
                if t >= j // SUBLANES
                else None
                for t in range(tiles)
            ]
            for j in range(PANEL)
        ]
        rows = []
        for t in range(tiles):
            row = []
            for c in range(strips):
                value = matrix[pl.ds(start + SUBLANES * t, SUBLANES), LANES * c : LANES * (c + 1)]
                at = lane + (LANES * c - start)
                inside = (at >= 0) & (at < PANEL)
                row.append(jnp.where(inside, jnp.where(at == sublane + SUBLANES * t, 1.0, 0.0), value))
            rows.append(row)
        scales = [jnp.zeros((SUBLANES, LANES), jnp.float32) for _ in range(tiles)]
        for k in range(PANEL):
            tile, at = k // SUBLANES, k % SUBLANES
            pivot = spread_row(column[k][tile], at)
            scales[tile] = jnp.where(sublane == at, pivot, scales[tile])
            over = 1.0 / pivot
            factors = [None] * tiles
            for t in range(tile, tiles):
                factors[t] = column[k][t] * over
            factors[tile] = jnp.where(sublane > at, factors[tile], 0.0)
            for j in range(k + 1, PANEL):
                value = spread_row(column[k][j // SUBLANES], j % SUBLANES)
                for t in range(j // SUBLANES, tiles):
                    column[j][t] = column[j][t] - factors[t] * value
            for c in range(strips):
                value = spread_row(rows[tile][c], at)
                for t in range(tile, tiles):
                    rows[t][c] = rows[t][c] - factors[t] * value
        done = []
        for t in range(tiles):
            scale = lax.rsqrt(scales[t])
            done.append(jnp.concatenate([value * scale for value in rows[t]], axis=1))
        done = jnp.concatenate(done, axis=0)
        at = lax.broadcasted_iota(jnp.int32, done.shape, 1)
        inverse[pl.ds(start, PANEL), :] = jnp.where(at < start + PANEL, done, 0.0)
        below = jnp.where(at >= start + PANEL, done, 0.0)
        strip_at = lax.broadcasted_iota(jnp.int32, (LANES, size), 1)
        inside = (strip_at >= start) & (strip_at < start + PANEL)
        for r in range(strips):

            @pl.when(LANES * (r + 1) > start + PANEL)
            def _(r=r):
                update = dot(below[:, LANES * r : LANES * (r + 1)], done, ((0,), (0,)))
                old = matrix[LANES * r : LANES * (r + 1), :]
                matrix[LANES * r : LANES * (r + 1), :] = jnp.where(inside, 0.0, old) - update

        return carry

    lax.fori_loop(0, size // PANEL, step, 0)


def finish_kernel(band_ref, pieces_ref, own_ref, other_ref, out_ref, matrix, inverse):
    size = matrix.shape[0]
    block = own_ref.shape[1]
    half = block // 2
    bands = size // block
    rows = pieces_ref.shape[1]
    matrix[...] = jnp.zeros_like(matrix)
    for band in range(bands):
        spots = [
            (block * band, block * band),
            (block * band, block * band + half),
            (block * band + half, block * band + half),
            (0, block + half * band),
            (half, block + half * band),
        ]
        for r in range(0, 5 * half, SUBLANES):
            top, left = spots[r // half]
            top = top + r % half
            matrix[top : top + SUBLANES, left : left + half] = pieces_ref[
                (r // rows) * bands + band, r % rows : r % rows + SUBLANES, :
            ]
    inverse_factor(matrix, inverse)
    columns = ((1,), (1,))

    @pl.when(band_ref[0] == 0)
    def _():
        out_ref[...] = dot(own_ref[...], inverse[:block, :block], columns)

    @pl.when(band_ref[0] == 1)
    def _():
        out_ref[...] = dot(other_ref[...], inverse[block:, :block], columns) + dot(
            own_ref[...], inverse[block:, block:], columns
        )


def factor_kernel(in_ref, out_ref, matrix):
    matrix[...] = in_ref[...]
    inverse_factor(matrix, out_ref)


def call(kernel, shape, *args, scratch=(), scalars=0):
    specs = [pl.BlockSpec(memory_space=pltpu.SMEM)] * scalars + [VMEM] * (len(args) - scalars)
    return pl.pallas_call(
        kernel,
        out_shape=jax.ShapeDtypeStruct(shape, jnp.float32),
        in_specs=specs,
        out_specs=VMEM,
        scratch_shapes=list(scratch),
    )(*args)


def transposed(states, potential):
    size_x, size_y, nz, block = states.shape
    domains_y = lax.axis_size("dy")
    domains_x = lax.axis_size("dx")
    domains = domains_x * domains_y
    bands = lax.axis_size("band")
    cells = size_x * size_y * nz
    columns = size_x * size_y
    half = block // 2
    area = ("dx", "dy")
    everyone = ("dx", "dy", "band")
    band = lax.axis_index("band").astype(jnp.int32).reshape(1)

    packed = pl.pallas_call(
        functools.partial(pack_kernel, nz),
        out_shape=jax.ShapeDtypeStruct((domains, columns + size_y, LANES), jnp.float32),
        grid=(block // LANES,),
        in_specs=[
            pl.BlockSpec((cells, LANES), lambda i: (0, i)),
            pl.BlockSpec((size_x, size_y, nz), lambda i: (0, 0, 0)),
        ],
        out_specs=pl.BlockSpec((nz, columns + size_y, LANES), lambda i: (i, 0, 0)),
    )(states.reshape(cells, block), potential)
    packed = lax.all_to_all(packed, area, 0, 0, tiled=True)
    grid = (size_x * domains_x, size_y * domains_y, LANES)
    filtered = call(
        functools.partial(filter_kernel, nz, domains_y, size_x, size_y),
        (domains, columns, LANES),
        packed,
        scratch=[
            pltpu.VMEM((grid[0] + 2 * WIDTH,) + grid[1:], jnp.float32),
            pltpu.VMEM((3,) + grid, jnp.float32),
            pltpu.VMEM(grid, jnp.float32),
        ],
    )
    filtered = lax.all_to_all(filtered, area, 0, 0, tiled=True)
    own = pl.pallas_call(
        functools.partial(unpack_kernel, nz),
        out_shape=jax.ShapeDtypeStruct((cells, block), jnp.float32),
        grid=(block // LANES,),
        in_specs=[pl.BlockSpec((nz, columns, LANES), lambda i: (i, 0, 0))],
        out_specs=pl.BlockSpec((cells, LANES), lambda i: (0, i)),
    )(filtered)
    other = lax.ppermute(own, "band", [(0, 1), (1, 0)])
    partial = call(gram_kernel, (5 * half, half), band, own, other, scalars=1)
    partial = lax.all_to_all(partial.reshape(domains, 5 * half // domains, half), area, 0, 0, tiled=True)
    pieces = call(
        functools.partial(sum_kernel, float(cells * domains)),
        (domains * bands,) + partial.shape[1:],
        partial,
    )
    pieces = lax.all_to_all(pieces, everyone, 0, 0, tiled=True)
    size = block * bands
    result = call(
        finish_kernel,
        (cells, block),
        band,
        pieces,
        own,
        other,
        scratch=[pltpu.VMEM((size, size), jnp.float32)] * 2,
        scalars=1,
    )
    return result.reshape(states.shape)


def with_halo(cells, axis, dim, width):
    count = lax.axis_size(axis)
    size = cells.shape[dim]
    head = lax.slice_in_dim(cells, 0, width, axis=dim)
    tail = lax.slice_in_dim(cells, size - width, size, axis=dim)
    before = lax.ppermute(tail, axis, [(i, (i + 1) % count) for i in range(count)])
    after = lax.ppermute(head, axis, [((i + 1) % count, i) for i in range(count)])
    return jnp.concatenate([before, cells, after], axis=dim)


def apply_ham(field, potential):
    padded_x = with_halo(field, "dx", 0, WIDTH)
    padded_y = with_halo(field, "dy", 1, WIDTH)
    size_x = field.shape[0]
    size_y = field.shape[1]
    lap = 3.0 * coeffs[0] * field
    for shift in range(1, WIDTH + 1):
        near = (
            padded_x[WIDTH + shift : WIDTH + shift + size_x]
            + padded_x[WIDTH - shift : WIDTH - shift + size_x]
            + padded_y[:, WIDTH + shift : WIDTH + shift + size_y]
            + padded_y[:, WIDTH - shift : WIDTH - shift + size_y]
        )
        near = near + jnp.roll(field, shift, 2) + jnp.roll(field, -shift, 2)
        lap = lap + coeffs[shift] * near
    return -0.5 * lap + potential[..., None] * field


def haloed(states, potential):
    prev = states
    cur = (apply_ham(states, potential) - centre_value * states) / half_width
    for step in range(1, DEGREE):
        nxt = 2.0 * (apply_ham(cur, potential) - centre_value * cur) / half_width - prev
        prev, cur = (cur, nxt)
    block = cur.shape[3]
    cells = cur.shape[0] * cur.shape[1] * cur.shape[2]
    local = cur.reshape(cells, block)
    gathered = lax.all_gather(local, "band", axis=1, tiled=True)
    total = cells * lax.axis_size("dx") * lax.axis_size("dy")
    partial = jnp.dot(gathered.T, gathered, precision=HIGHEST, preferred_element_type=jnp.float32) / total
    correlation = lax.psum(partial, ("dx", "dy"))
    size = correlation.shape[0]
    if size % LANES == 0:
        inverse = call(factor_kernel, (size, size), correlation, scratch=[pltpu.VMEM((size, size), jnp.float32)])
    else:
        factor = jnp.linalg.cholesky(correlation)
        inverse = jax.scipy.linalg.solve_triangular(factor, jnp.eye(size, dtype=jnp.float32), lower=True)
    my_rows = lax.dynamic_slice_in_dim(inverse, lax.axis_index("band") * block, block, 0)
    result = jnp.dot(gathered, my_rows.T, precision=HIGHEST, preferred_element_type=jnp.float32)
    return result.reshape(cur.shape)


def shards(states, potential):
    size_x, size_y, nz, block = states.shape
    domains = lax.axis_size("dx") * lax.axis_size("dy")
    fits = (
        nz == SUBLANES
        and size_y == SUBLANES
        and nz * size_x <= LANES
        and block * nz == LANES * domains
        and block == 2 * LANES
        and lax.axis_size("band") == 2
        and (5 * LANES) % (domains * SUBLANES) == 0
        and lax.axis_size("dx") * size_x > 2 * WIDTH
        and lax.axis_size("dy") * size_y > 2 * WIDTH
    )
    return transposed(states, potential) if fits else haloed(states, potential)


def solution(mesh):
    return jax.shard_map(
        shards,
        mesh=mesh,
        in_specs=(P("dx", "dy", None, "band"), P("dx", "dy", None)),
        out_specs=P("dx", "dy", None, "band"),
        check_vma=False,
    )
```

```python
import functools

import jax
import jax.numpy as jnp
from jax import lax
from jax.experimental import pallas as pl
from jax.experimental.pallas import tpu as pltpu
from jax.sharding import PartitionSpec as P

DEGREE = 3
LANES = 128
SUBLANES = 8
PANEL = 32
PART = 16

coeffs = (
    -5369.0 / 1800.0,
    12.0 / 7.0,
    -15.0 / 56.0,
    10.0 / 189.0,
    -1.0 / 112.0,
    2.0 / 1925.0,
    -1.0 / 16632.0,
)
WIDTH = len(coeffs) - 1
half_width = 5.0
centre_value = 7.0
VMEM = pl.BlockSpec(memory_space=pltpu.VMEM)
HIGHEST = lax.Precision.HIGHEST


def dot(a, b, dims):
    return lax.dot_general(a, b, (dims, ((), ())), precision=HIGHEST, preferred_element_type=jnp.float32)


def swap_groups(arrays, group):
    count = len(arrays)
    lane = lax.broadcasted_iota(jnp.int32, arrays[0].shape, 1)
    bit = 1
    while bit < count:
        upper = (lane // (group * bit)) % 2 == 1
        out = list(arrays)
        for i in range(count):
            if i & bit == 0:
                low, high = arrays[i], arrays[i | bit]
                out[i] = jnp.where(upper, pltpu.roll(high, group * bit, 1), low)
                out[i | bit] = jnp.where(upper, high, pltpu.roll(low, LANES - group * bit, 1))
        arrays = out
        bit *= 2
    return arrays


def pack_kernel(nz, states_ref, potential_ref, out_ref):
    columns = states_ref.shape[0] // nz
    arrays = [states_ref[pl.ds(z, columns, stride=nz), :] for z in range(nz)]
    for g, value in enumerate(swap_groups(arrays, LANES // nz)):
        out_ref[g, :columns, :] = value
    row = lax.broadcasted_iota(jnp.int32, (nz, LANES), 0)
    lane = lax.broadcasted_iota(jnp.int32, (nz, LANES), 1)
    packed = jnp.zeros((potential_ref.shape[1], LANES), jnp.float32)
    for x in range(potential_ref.shape[0]):
        spread = jnp.where(lane == row + nz * x, 1.0, 0.0)
        packed = packed + dot(potential_ref[x], spread, ((1,), (0,)))
    for g in range(nz):
        out_ref[g, columns:, :] = packed


def filter_kernel(nz, domains_y, size_x, size_y, in_ref, out_ref, field, older, potential):
    domains = in_ref.shape[0]
    total_x = size_x * (domains // domains_y)
    total_y = size_y * domains_y
    columns = size_x * size_y
    group = LANES // nz

    def place(i, x):
        return size_x * (i // domains_y) + x, size_y * (i % domains_y)

    packed = in_ref[:, columns:, :].reshape(domains * size_y, LANES)
    source = lax.broadcasted_iota(jnp.int32, (LANES, LANES), 0)
    target = lax.broadcasted_iota(jnp.int32, (LANES, LANES), 1)
    for x in range(size_x):
        spread = jnp.where(source == nz * x + target // group, 1.0, 0.0)
        values = dot(packed, spread, ((1,), (0,)))
        for i in range(domains):
            at_x, at_y = place(i, x)
            potential[at_x, at_y : at_y + size_y, :] = values[size_y * i : size_y * (i + 1)] - centre_value
            field[WIDTH + at_x, at_y : at_y + size_y, :] = in_ref[i, size_y * x : size_y * (x + 1), :]

    weights = [0.0] * nz
    for k in range(1, WIDTH + 1):
        weights[k % nz] += coeffs[k]
        weights[-k % nz] += coeffs[k]

    for step in range(DEGREE):
        for k in range(WIDTH):
            field[k] = field[total_x + k]
            field[WIDTH + total_x + k] = field[WIDTH + k]
        scale = 1.0 / half_width if step == 0 else 2.0 / half_width

        def body(x, carry, step=step, scale=scale):
            value = field[WIDTH + x]
            lap = (3.0 * coeffs[0] + weights[0]) * value
            for k in range(1, WIDTH + 1):
                near = field[WIDTH + x + k] + field[WIDTH + x - k]
                near = near + pltpu.roll(value, k, 0) + pltpu.roll(value, total_y - k, 0)
                lap = lap + coeffs[k] * near
            for k in range(1, nz):
                lap = lap + weights[k] * pltpu.roll(value, group * k, 1)
            result = (potential[x] * value - 0.5 * lap) * scale
            if step > 0:
                result = result - older[(step - 1) % 2, x]
            older[step % 2, x] = value if step + 1 < DEGREE else result
            spare[x] = result
            return carry

        spare = older.at[2]
        lax.fori_loop(0, total_x, body, 0, unroll=2)
        if step + 1 < DEGREE:
            field[WIDTH : WIDTH + total_x] = spare[...]

    shares = out_ref.shape[0] // domains
    share = size_x // shares
    for i in range(domains):
        for x in range(size_x):
            at_x, at_y = place(i, x)
            row = size_y * (x % share)
            out_ref[i * shares + x // share, row : row + size_y, :] = older[2, at_x, at_y : at_y + size_y, :]


def upper_blocks(strips):
    return [(i, j) for i in range(strips) for j in range(i, strips)]


def gram_kernel(nz, bands, in_ref, cells_ref, out_ref):
    columns = in_ref.shape[1]
    strips = cells_ref.shape[0]
    per_band = strips // bands
    for strip in range(strips):
        first = nz * (strip % per_band)
        arrays = [in_ref[(first + g) * bands + strip // per_band] for g in range(nz)]
        for z, value in enumerate(swap_groups(arrays, LANES // nz)):
            cells_ref[strip, pl.ds(z, columns, stride=nz), :] = value
    values = [cells_ref[strip] for strip in range(strips)]
    at = 0
    for i in range(strips):
        product = dot(values[i], jnp.concatenate(values[i:], axis=1), ((0,), (0,)))
        for j in range(strips - i):
            out_ref[at : at + LANES, :] = product[:, LANES * j : LANES * (j + 1)]
            at += LANES


def sum_kernel(total, in_ref, out_ref):
    value = in_ref[0]
    for i in range(1, in_ref.shape[0]):
        value = value + in_ref[i]
    value = value / total
    for i in range(out_ref.shape[0]):
        out_ref[i] = value


def spread_row(value, row):
    return jnp.broadcast_to(value[row : row + 1, :], value.shape)


def split(value):
    high = value.astype(jnp.bfloat16)
    rest = value - high.astype(jnp.float32)
    middle = rest.astype(jnp.bfloat16)
    return high, middle, (rest - middle.astype(jnp.float32)).astype(jnp.bfloat16)


def outer(left, right):
    a, b, c = left
    d, e, f = right
    left = jnp.concatenate([a, a, b, b, a, c], axis=0)
    right = jnp.concatenate([d, e, d, e, f, d], axis=0)
    return lax.dot_general(left, right, (((0,), (0,)), ((), ())), preferred_element_type=jnp.float32)


def eliminate(work, start):
    tiles = PANEL // SUBLANES
    strips = work.shape[1] // LANES
    sublane = lax.broadcasted_iota(jnp.int32, (SUBLANES, LANES), 0)
    at = lax.broadcasted_iota(jnp.int32, (SUBLANES, LANES), 1) - start
    rows = [
        [work[start + SUBLANES * t : start + SUBLANES * (t + 1), LANES * c : LANES * (c + 1)] for c in range(strips)]
        for t in range(tiles)
    ]
    pivots = [jnp.ones((SUBLANES, LANES), jnp.float32) for _ in range(tiles)]
    for first in range(0, PANEL, PART):
        column = {
            (j, t): jnp.broadcast_to(rows[t][0][:, start + j : start + j + 1], (SUBLANES, LANES))
            for j in range(first, first + PART)
            for t in range(j // SUBLANES, tiles)
        }
        inside = (at >= first) & (at < first + PART)
        for t in range(tiles):
            rows[t][0] = jnp.where(inside, jnp.where(at == sublane + SUBLANES * t, 1.0, 0.0), rows[t][0])
        for k in range(first, first + PART):
            tile, row = k // SUBLANES, k % SUBLANES
            pivot = spread_row(column[k, tile], row)
            pivots[tile] = jnp.where(sublane == row, pivot, pivots[tile])
            over = 1.0 / pivot
            factor = {t: column[k, t] * over for t in range(tile, tiles)}
            factor[tile] = jnp.where(sublane > row, factor[tile], 0.0)
            for j in range(k + 1, first + PART):
                value = spread_row(column[k, j // SUBLANES], j % SUBLANES)
                for t in range(j // SUBLANES, tiles):
                    column[j, t] = column[j, t] - factor[t] * value
            for c in range(strips):
                value = spread_row(rows[tile][c], row)
                for t in range(tile, tiles):
                    rows[t][c] = rows[t][c] - factor[t] * value
    scaled = [jnp.concatenate([v * lax.rsqrt(pivots[t]) for v in rows[t]], axis=1) for t in range(tiles)]
    return jnp.concatenate(scaled, axis=0)


def inverse_factor(matrix, inverse, work, done):
    strips = matrix.shape[0] // LANES

    def step(block, carry):
        base = pl.multiple_of(block * LANES, LANES)
        strip = [pl.multiple_of(lax.rem(block + c, strips) * LANES, LANES) for c in range(strips)]
        for c in range(strips):
            work[:, LANES * c : LANES * (c + 1)] = matrix[pl.ds(base, LANES), pl.ds(strip[c], LANES)]
        for start in range(0, LANES, PANEL):
            end = start + PANEL
            value = eliminate(work, start)
            lane = lax.broadcasted_iota(jnp.int32, (PANEL, LANES), 1)
            done[start:end, :LANES] = jnp.where(lane < end, value[:, :LANES], 0.0)
            done[start:end, LANES:] = value[:, LANES:]
            if end < LANES:
                parts = split(value)
                update = outer([part[:, :LANES] for part in parts], parts)
                lane = lax.broadcasted_iota(jnp.int32, (LANES - end, LANES), 1)
                old = jnp.where((lane >= start) & (lane < end), 0.0, work[end:, :LANES])
                work[end:, :LANES] = old - update[end:, :LANES]
                work[end:, LANES:] = work[end:, LANES:] - update[end:, LANES:]
        inverse[pl.ds(base, LANES), pl.ds(strip[0], LANES)] = done[:, :LANES]
        for c in range(1, strips):
            value = jnp.where(block + c >= strips, done[:, LANES * c : LANES * (c + 1)], 0.0)
            inverse[pl.ds(base, LANES), pl.ds(strip[c], LANES)] = value

        @pl.when(block + 1 < strips)
        def _():
            parts = split(done[...])
            for c in range(1, strips):

                @pl.when(block + c < strips)
                def _(c=c):
                    update = outer([part[:, LANES * c : LANES * (c + 1)] for part in parts], parts)
                    rows = pl.ds(pl.multiple_of((block + c) * LANES, LANES), LANES)
                    matrix[rows, pl.ds(strip[0], LANES)] = -update[:, :LANES]
                    for e in range(1, strips):
                        columns = pl.ds(strip[e], LANES)
                        matrix[rows, columns] = matrix[rows, columns] - update[:, LANES * e : LANES * (e + 1)]

        return carry

    lax.fori_loop(0, strips, step, 0)


def finish_kernel(band_ref, pieces_ref, own_ref, other_ref, out_ref, matrix, inverse, work, done):
    strips = own_ref.shape[0]
    cells = own_ref.shape[1]
    block = out_ref.shape[1]
    rows = pieces_ref.shape[1]
    matrix[...] = jnp.zeros_like(matrix)
    for at, (i, j) in enumerate(upper_blocks(strips)):
        for r in range(0, LANES, SUBLANES):
            from_row = LANES * at + r
            matrix[LANES * i + r : LANES * i + r + SUBLANES, LANES * j : LANES * (j + 1)] = pieces_ref[
                from_row // rows, from_row % rows : from_row % rows + SUBLANES, :
            ]
    inverse_factor(matrix, inverse, work, done)
    band = band_ref[0]
    for b in range(strips * LANES // block):

        @pl.when(band == b)
        def _(b=b):
            used = block * (b + 1)
            mine = inverse[block * b : used, :used]
            for share, ref in ((b, own_ref), (1 - b, other_ref)):
                value = jnp.concatenate([ref[s] for s in range(used // LANES)], axis=1)
                out_ref[cells * share : cells * (share + 1), :] = dot(value, mine, ((1,), (1,)))


def factor_kernel(in_ref, out_ref, matrix, work, done):
    matrix[...] = in_ref[...]
    inverse_factor(matrix, out_ref, work, done)


def factor_scratch(size):
    return [pltpu.VMEM((rows, size), jnp.float32) for rows in (size, LANES, LANES)]


def call(kernel, shape, *args, scratch=(), scalars=0):
    specs = [pl.BlockSpec(memory_space=pltpu.SMEM)] * scalars + [VMEM] * (len(args) - scalars)
    return pl.pallas_call(
        kernel,
        out_shape=jax.ShapeDtypeStruct(shape, jnp.float32),
        in_specs=specs,
        out_specs=VMEM,
        scratch_shapes=list(scratch),
    )(*args)


def transposed(states, potential):
    size_x, size_y, nz, block = states.shape
    domains_y = lax.axis_size("dy")
    domains_x = lax.axis_size("dx")
    domains = domains_x * domains_y
    bands = lax.axis_size("band")
    cells = size_x * size_y * nz
    columns = size_x * size_y
    area = ("dx", "dy")
    everyone = ("dx", "dy", "band")
    band = lax.axis_index("band").astype(jnp.int32).reshape(1)

    packed = pl.pallas_call(
        functools.partial(pack_kernel, nz),
        out_shape=jax.ShapeDtypeStruct((domains, columns + size_y, LANES), jnp.float32),
        grid=(block // LANES,),
        in_specs=[
            pl.BlockSpec((cells, LANES), lambda i: (0, i)),
            pl.BlockSpec((size_x, size_y, nz), lambda i: (0, 0, 0)),
        ],
        out_specs=pl.BlockSpec((nz, columns + size_y, LANES), lambda i: (i, 0, 0)),
    )(states.reshape(cells, block), potential)
    packed = lax.all_to_all(packed, area, 0, 0, tiled=True)
    grid = (size_x * domains_x, size_y * domains_y, LANES)
    filtered = call(
        functools.partial(filter_kernel, nz, domains_y, size_x, size_y),
        (domains * bands, columns // bands, LANES),
        packed,
        scratch=[
            pltpu.VMEM((grid[0] + 2 * WIDTH,) + grid[1:], jnp.float32),
            pltpu.VMEM((3,) + grid, jnp.float32),
            pltpu.VMEM(grid, jnp.float32),
        ],
    )
    filtered = lax.all_to_all(filtered, everyone, 0, 0, tiled=True)
    size = block * bands
    strips = size // LANES
    rows = len(upper_blocks(strips)) * LANES
    own, partial = pl.pallas_call(
        functools.partial(gram_kernel, nz, bands),
        out_shape=(
            jax.ShapeDtypeStruct((strips, cells // bands, LANES), jnp.float32),
            jax.ShapeDtypeStruct((rows, LANES), jnp.float32),
        ),
        in_specs=[VMEM],
        out_specs=(VMEM, VMEM),
    )(filtered)
    other = lax.ppermute(own, "band", [(0, 1), (1, 0)])
    devices = domains * bands
    partial = lax.all_to_all(partial.reshape(devices, rows // devices, LANES), everyone, 0, 0, tiled=True)
    pieces = call(functools.partial(sum_kernel, float(cells * domains)), partial.shape, partial)
    pieces = lax.all_to_all(pieces, everyone, 0, 0, tiled=True)
    result = call(
        finish_kernel,
        (cells, block),
        band,
        pieces,
        own,
        other,
        scratch=[pltpu.VMEM((size, size), jnp.float32)] + factor_scratch(size),
        scalars=1,
    )
    return result.reshape(states.shape)


def with_halo(cells, axis, dim, width):
    count = lax.axis_size(axis)
    size = cells.shape[dim]
    head = lax.slice_in_dim(cells, 0, width, axis=dim)
    tail = lax.slice_in_dim(cells, size - width, size, axis=dim)
    before = lax.ppermute(tail, axis, [(i, (i + 1) % count) for i in range(count)])
    after = lax.ppermute(head, axis, [((i + 1) % count, i) for i in range(count)])
    return jnp.concatenate([before, cells, after], axis=dim)


def apply_ham(field, potential):
    padded_x = with_halo(field, "dx", 0, WIDTH)
    padded_y = with_halo(field, "dy", 1, WIDTH)
    size_x = field.shape[0]
    size_y = field.shape[1]
    lap = 3.0 * coeffs[0] * field
    for shift in range(1, WIDTH + 1):
        near = (
            padded_x[WIDTH + shift : WIDTH + shift + size_x]
            + padded_x[WIDTH - shift : WIDTH - shift + size_x]
            + padded_y[:, WIDTH + shift : WIDTH + shift + size_y]
            + padded_y[:, WIDTH - shift : WIDTH - shift + size_y]
        )
        near = near + jnp.roll(field, shift, 2) + jnp.roll(field, -shift, 2)
        lap = lap + coeffs[shift] * near
    return -0.5 * lap + potential[..., None] * field


def haloed(states, potential):
    prev = states
    cur = (apply_ham(states, potential) - centre_value * states) / half_width
    for step in range(1, DEGREE):
        nxt = 2.0 * (apply_ham(cur, potential) - centre_value * cur) / half_width - prev
        prev, cur = (cur, nxt)
    block = cur.shape[3]
    cells = cur.shape[0] * cur.shape[1] * cur.shape[2]
    local = cur.reshape(cells, block)
    gathered = lax.all_gather(local, "band", axis=1, tiled=True)
    total = cells * lax.axis_size("dx") * lax.axis_size("dy")
    partial = jnp.dot(gathered.T, gathered, precision=HIGHEST, preferred_element_type=jnp.float32) / total
    correlation = lax.psum(partial, ("dx", "dy"))
    size = correlation.shape[0]
    if size % LANES == 0:
        inverse = call(factor_kernel, (size, size), correlation, scratch=factor_scratch(size))
    else:
        factor = jnp.linalg.cholesky(correlation)
        inverse = jax.scipy.linalg.solve_triangular(factor, jnp.eye(size, dtype=jnp.float32), lower=True)
    my_rows = lax.dynamic_slice_in_dim(inverse, lax.axis_index("band") * block, block, 0)
    result = jnp.dot(gathered, my_rows.T, precision=HIGHEST, preferred_element_type=jnp.float32)
    return result.reshape(cur.shape)


def shards(states, potential):
    size_x, size_y, nz, block = states.shape
    domains = lax.axis_size("dx") * lax.axis_size("dy")
    fits = (
        nz == SUBLANES
        and size_y == SUBLANES
        and nz * size_x <= LANES
        and block * nz == LANES * domains
        and block == 2 * LANES
        and lax.axis_size("band") == 2
        and size_x % 2 == 0
        and (10 * LANES) % (2 * domains * SUBLANES) == 0
        and lax.axis_size("dx") * size_x > 2 * WIDTH
        and lax.axis_size("dy") * size_y > 2 * WIDTH
    )
    return transposed(states, potential) if fits else haloed(states, potential)


def solution(mesh):
    return jax.shard_map(
        shards,
        mesh=mesh,
        in_specs=(P("dx", "dy", None, "band"), P("dx", "dy", None)),
        out_specs=P("dx", "dy", None, "band"),
        check_vma=False,
    )
```

```python
import functools

import jax
import jax.numpy as jnp
from jax import lax
from jax.experimental import pallas as pl
from jax.experimental.pallas import tpu as pltpu
from jax.sharding import PartitionSpec as P

DEGREE = 3
LANES = 128
SUBLANES = 8
PANEL = 32
PART = 16
CORES = 2

coeffs = (
    -5369.0 / 1800.0,
    12.0 / 7.0,
    -15.0 / 56.0,
    10.0 / 189.0,
    -1.0 / 112.0,
    2.0 / 1925.0,
    -1.0 / 16632.0,
)
WIDTH = len(coeffs) - 1
half_width = 5.0
centre_value = 7.0
VMEM = pl.BlockSpec(memory_space=pltpu.VMEM)
SMEM = pl.BlockSpec(memory_space=pltpu.SMEM)
HIGHEST = lax.Precision.HIGHEST


def dot(a, b, dims):
    return lax.dot_general(a, b, (dims, ((), ())), precision=HIGHEST, preferred_element_type=jnp.float32)


def swap_groups(arrays, group):
    count = len(arrays)
    lane = lax.broadcasted_iota(jnp.int32, arrays[0].shape, 1)
    bit = 1
    while bit < count:
        upper = (lane // (group * bit)) % 2 == 1
        out = list(arrays)
        for i in range(count):
            if i & bit == 0:
                low, high = arrays[i], arrays[i | bit]
                out[i] = jnp.where(upper, pltpu.roll(high, group * bit, 1), low)
                out[i | bit] = jnp.where(upper, high, pltpu.roll(low, LANES - group * bit, 1))
        arrays = out
        bit *= 2
    return arrays


def pack_kernel(nz, states_ref, potential_ref, out_ref):
    columns = states_ref.shape[0] // nz
    arrays = [states_ref[pl.ds(z, columns, stride=nz), :] for z in range(nz)]
    for g, value in enumerate(swap_groups(arrays, LANES // nz)):
        out_ref[g, :columns, :] = value
    row = lax.broadcasted_iota(jnp.int32, (nz, LANES), 0)
    lane = lax.broadcasted_iota(jnp.int32, (nz, LANES), 1)
    packed = jnp.zeros((potential_ref.shape[1], LANES), jnp.float32)
    for x in range(potential_ref.shape[0]):
        spread = jnp.where(lane == row + nz * x, 1.0, 0.0)
        packed = packed + dot(potential_ref[x], spread, ((1,), (0,)))
    for g in range(nz):
        out_ref[g, columns:, :] = packed


def filter_kernel(nz, domains_y, size_x, size_y, in_ref, out_ref, field, older, potential):
    domains = in_ref.shape[0]
    total_x = size_x * (domains // domains_y)
    total_y = size_y * domains_y
    columns = size_x * size_y
    group = LANES // nz

    def place(i, x):
        return size_x * (i // domains_y) + x, size_y * (i % domains_y)

    packed = in_ref[:, columns:, :].reshape(domains * size_y, LANES)
    source = lax.broadcasted_iota(jnp.int32, (LANES, LANES), 0)
    target = lax.broadcasted_iota(jnp.int32, (LANES, LANES), 1)
    for x in range(size_x):
        spread = jnp.where(source == nz * x + target // group, 1.0, 0.0)
        values = dot(packed, spread, ((1,), (0,)))
        for i in range(domains):
            at_x, at_y = place(i, x)
            potential[at_x, at_y : at_y + size_y, :] = values[size_y * i : size_y * (i + 1)] - centre_value
            field[WIDTH + at_x, at_y : at_y + size_y, :] = in_ref[i, size_y * x : size_y * (x + 1), :]

    weights = [0.0] * nz
    for k in range(1, WIDTH + 1):
        weights[k % nz] += coeffs[k]
        weights[-k % nz] += coeffs[k]

    for step in range(DEGREE):
        for k in range(WIDTH):
            field[k] = field[total_x + k]
            field[WIDTH + total_x + k] = field[WIDTH + k]
        scale = 1.0 / half_width if step == 0 else 2.0 / half_width

        def body(x, carry, step=step, scale=scale):
            value = field[WIDTH + x]
            lap = (3.0 * coeffs[0] + weights[0]) * value
            for k in range(1, WIDTH + 1):
                near = field[WIDTH + x + k] + field[WIDTH + x - k]
                near = near + pltpu.roll(value, k, 0) + pltpu.roll(value, total_y - k, 0)
                lap = lap + coeffs[k] * near
            for k in range(1, nz):
                lap = lap + weights[k] * pltpu.roll(value, group * k, 1)
            result = (potential[x] * value - 0.5 * lap) * scale
            if step > 0:
                result = result - older[(step - 1) % 2, x]
            older[step % 2, x] = value if step + 1 < DEGREE else result
            spare[x] = result
            return carry

        spare = older.at[2]
        lax.fori_loop(0, total_x, body, 0, unroll=2)
        if step + 1 < DEGREE:
            field[WIDTH : WIDTH + total_x] = spare[...]

    shares = out_ref.shape[0] // domains
    share = size_x // shares
    for i in range(domains):
        for x in range(size_x):
            at_x, at_y = place(i, x)
            row = size_y * (x % share)
            out_ref[i * shares + x // share, row : row + size_y, :] = older[2, at_x, at_y : at_y + size_y, :]


def upper_blocks(strips):
    return [(i, j) for i in range(strips) for j in range(i, strips)]


def share_of(strips, core):
    return upper_blocks(strips)[core :: CORES]


def gram_kernel(nz, bands, core_ref, own_ref, other_ref, cells_ref, out_ref, paired):
    columns = own_ref.shape[1]
    strips, rows, _ = cells_ref.shape
    per_band = strips // bands
    for strip in range(strips):
        first = nz * (strip % per_band)
        for half, ref in enumerate((own_ref, other_ref)):
            arrays = [ref[(first + g) * bands + strip // per_band] for g in range(nz)]
            for z, value in enumerate(swap_groups(arrays, LANES // nz)):
                paired[strip, pl.ds(half * rows + z, columns, stride=nz), :] = value
        cells_ref[strip] = paired[strip, :rows, :]
    for core in range(CORES):

        @pl.when(core_ref[0] == core)
        def _(core=core):
            for at, (i, j) in enumerate(share_of(strips, core)):
                out_ref[LANES * at : LANES * (at + 1), :] = dot(paired[i], paired[j], ((0,), (0,)))


def sum_kernel(total, in_ref, out_ref):
    value = in_ref[0]
    for i in range(1, in_ref.shape[0]):
        value = value + in_ref[i]
    value = value / total
    for i in range(out_ref.shape[0]):
        out_ref[i] = value


def spread_row(value, row):
    return jnp.broadcast_to(value[row : row + 1, :], value.shape)


def split(value):
    high = value.astype(jnp.bfloat16)
    rest = value - high.astype(jnp.float32)
    middle = rest.astype(jnp.bfloat16)
    return high, middle, (rest - middle.astype(jnp.float32)).astype(jnp.bfloat16)


def outer(left, right):
    a, b, c = left
    d, e, f = right
    left = jnp.concatenate([a, a, b, b, a, c], axis=0)
    right = jnp.concatenate([d, e, d, e, f, d], axis=0)
    return lax.dot_general(left, right, (((0,), (0,)), ((), ())), preferred_element_type=jnp.float32)


def eliminate(work, start):
    tiles = PANEL // SUBLANES
    strips = work.shape[1] // LANES
    sublane = lax.broadcasted_iota(jnp.int32, (SUBLANES, LANES), 0)
    at = lax.broadcasted_iota(jnp.int32, (SUBLANES, LANES), 1) - start
    rows = [
        [work[start + SUBLANES * t : start + SUBLANES * (t + 1), LANES * c : LANES * (c + 1)] for c in range(strips)]
        for t in range(tiles)
    ]
    pivots = [jnp.ones((SUBLANES, LANES), jnp.float32) for _ in range(tiles)]
    for first in range(0, PANEL, PART):
        column = {
            (j, t): jnp.broadcast_to(rows[t][0][:, start + j : start + j + 1], (SUBLANES, LANES))
            for j in range(first, first + PART)
            for t in range(j // SUBLANES, tiles)
        }
        inside = (at >= first) & (at < first + PART)
        for t in range(tiles):
            rows[t][0] = jnp.where(inside, jnp.where(at == sublane + SUBLANES * t, 1.0, 0.0), rows[t][0])
        for k in range(first, first + PART):
            tile, row = k // SUBLANES, k % SUBLANES
            pivot = spread_row(column[k, tile], row)
            pivots[tile] = jnp.where(sublane == row, pivot, pivots[tile])
            over = 1.0 / pivot
            factor = {t: column[k, t] * over for t in range(tile, tiles)}
            factor[tile] = jnp.where(sublane > row, factor[tile], 0.0)
            for j in range(k + 1, first + PART):
                value = spread_row(column[k, j // SUBLANES], j % SUBLANES)
                for t in range(j // SUBLANES, tiles):
                    column[j, t] = column[j, t] - factor[t] * value
            for c in range(strips):
                value = spread_row(rows[tile][c], row)
                for t in range(tile, tiles):
                    rows[t][c] = rows[t][c] - factor[t] * value
    scaled = [jnp.concatenate([v * lax.rsqrt(pivots[t]) for v in rows[t]], axis=1) for t in range(tiles)]
    return jnp.concatenate(scaled, axis=0)


def inverse_factor(matrix, inverse, work, done):
    strips = matrix.shape[0] // LANES

    def step(block, carry):
        base = pl.multiple_of(block * LANES, LANES)
        strip = [pl.multiple_of(lax.rem(block + c, strips) * LANES, LANES) for c in range(strips)]
        for c in range(strips):
            work[:, LANES * c : LANES * (c + 1)] = matrix[pl.ds(base, LANES), pl.ds(strip[c], LANES)]
        for start in range(0, LANES, PANEL):
            end = start + PANEL
            value = eliminate(work, start)
            lane = lax.broadcasted_iota(jnp.int32, (PANEL, LANES), 1)
            done[start:end, :LANES] = jnp.where(lane < end, value[:, :LANES], 0.0)
            done[start:end, LANES:] = value[:, LANES:]
            if end < LANES:
                parts = split(value)
                update = outer([part[:, :LANES] for part in parts], parts)
                lane = lax.broadcasted_iota(jnp.int32, (LANES - end, LANES), 1)
                old = jnp.where((lane >= start) & (lane < end), 0.0, work[end:, :LANES])
                work[end:, :LANES] = old - update[end:, :LANES]
                work[end:, LANES:] = work[end:, LANES:] - update[end:, LANES:]
        inverse[pl.ds(base, LANES), pl.ds(strip[0], LANES)] = done[:, :LANES]
        for c in range(1, strips):
            value = jnp.where(block + c >= strips, done[:, LANES * c : LANES * (c + 1)], 0.0)
            inverse[pl.ds(base, LANES), pl.ds(strip[c], LANES)] = value

        @pl.when(block + 1 < strips)
        def _():
            parts = split(done[...])
            for c in range(1, strips):

                @pl.when(block + c < strips)
                def _(c=c):
                    update = outer([part[:, LANES * c : LANES * (c + 1)] for part in parts], parts)
                    rows = pl.ds(pl.multiple_of((block + c) * LANES, LANES), LANES)
                    matrix[rows, pl.ds(strip[0], LANES)] = -update[:, :LANES]
                    for e in range(1, strips):
                        columns = pl.ds(strip[e], LANES)
                        matrix[rows, columns] = matrix[rows, columns] - update[:, LANES * e : LANES * (e + 1)]

        return carry

    lax.fori_loop(0, strips, step, 0)


def finish_kernel(place_ref, mine_ref, theirs_ref, own_ref, other_ref, out_ref, matrix, inverse, work, done):
    strips = own_ref.shape[0]
    cells = own_ref.shape[1]
    block = out_ref.shape[1]
    rows = mine_ref.shape[1]
    matrix[...] = jnp.zeros_like(matrix)
    for core in range(CORES):

        @pl.when(place_ref[0] == core)
        def _(core=core):
            for ref, holder in ((mine_ref, core), (theirs_ref, 1 - core)):
                for at, (i, j) in enumerate(share_of(strips, holder)):
                    for r in range(0, LANES, SUBLANES):
                        piece, row = divmod(LANES * at + r, rows)
                        top, left = LANES * i + r, LANES * j
                        matrix[top : top + SUBLANES, left : left + LANES] = ref[piece, row : row + SUBLANES, :]

    inverse_factor(matrix, inverse, work, done)
    band = place_ref[1]
    for b in range(strips * LANES // block):

        @pl.when(band == b)
        def _(b=b):
            used = block * (b + 1)
            mine = inverse[block * b : used, :used]
            for share, ref in ((b, own_ref), (1 - b, other_ref)):
                value = jnp.concatenate([ref[s] for s in range(used // LANES)], axis=1)
                out_ref[cells * share : cells * (share + 1), :] = dot(value, mine, ((1,), (1,)))


def factor_kernel(in_ref, out_ref, matrix, work, done):
    matrix[...] = in_ref[...]
    inverse_factor(matrix, out_ref, work, done)


def factor_scratch(size):
    return [pltpu.VMEM((rows, size), jnp.float32) for rows in (size, LANES, LANES)]


def call(kernel, shape, *args, scratch=(), scalars=0):
    specs = [SMEM] * scalars + [VMEM] * (len(args) - scalars)
    return pl.pallas_call(
        kernel,
        out_shape=jax.ShapeDtypeStruct(shape, jnp.float32),
        in_specs=specs,
        out_specs=VMEM,
        scratch_shapes=list(scratch),
    )(*args)


def transposed(states, potential):
    size_x, size_y, nz, block = states.shape
    domains_y = lax.axis_size("dy")
    domains_x = lax.axis_size("chip") * CORES
    domains = domains_x * domains_y
    bands = lax.axis_size("band")
    cells = size_x * size_y * nz
    columns = size_x * size_y
    area = ("chip", "core", "dy")
    everyone = area + ("band",)
    same_core = ("chip", "dy", "band")
    swap = [(0, 1), (1, 0)]
    place = jnp.stack([lax.axis_index("core"), lax.axis_index("band")]).astype(jnp.int32)

    packed = pl.pallas_call(
        functools.partial(pack_kernel, nz),
        out_shape=jax.ShapeDtypeStruct((domains, columns + size_y, LANES), jnp.float32),
        grid=(block // LANES,),
        in_specs=[
            pl.BlockSpec((cells, LANES), lambda i: (0, i)),
            pl.BlockSpec((size_x, size_y, nz), lambda i: (0, 0, 0)),
        ],
        out_specs=pl.BlockSpec((nz, columns + size_y, LANES), lambda i: (i, 0, 0)),
    )(states.reshape(cells, block), potential)
    packed = lax.all_to_all(packed, area, 0, 0, tiled=True)
    grid = (size_x * domains_x, size_y * domains_y, LANES)
    filtered = call(
        functools.partial(filter_kernel, nz, domains_y, size_x, size_y),
        (domains * bands, columns // bands, LANES),
        packed,
        scratch=[
            pltpu.VMEM((grid[0] + 2 * WIDTH,) + grid[1:], jnp.float32),
            pltpu.VMEM((3,) + grid, jnp.float32),
            pltpu.VMEM(grid, jnp.float32),
        ],
    )
    filtered = lax.all_to_all(filtered, everyone, 0, 0, tiled=True)
    size = block * bands
    strips = size // LANES
    rows = len(share_of(strips, 0)) * LANES
    holders = domains * bands // CORES
    neighbours = lax.ppermute(filtered, "core", swap)
    own, partial = pl.pallas_call(
        functools.partial(gram_kernel, nz, bands),
        out_shape=(
            jax.ShapeDtypeStruct((strips, cells // bands, LANES), jnp.float32),
            jax.ShapeDtypeStruct((rows, LANES), jnp.float32),
        ),
        in_specs=[SMEM, VMEM, VMEM],
        out_specs=(VMEM, VMEM),
        scratch_shapes=[pltpu.VMEM((strips, CORES * cells // bands, LANES), jnp.float32)],
    )(place, filtered, neighbours)
    other = lax.ppermute(own, "band", swap)
    partial = lax.all_to_all(partial.reshape(holders, rows // holders, LANES), same_core, 0, 0, tiled=True)
    pieces = call(functools.partial(sum_kernel, float(cells * domains)), partial.shape, partial)
    mine = lax.all_to_all(pieces, same_core, 0, 0, tiled=True)
    theirs = lax.ppermute(mine, "core", swap)
    result = call(
        finish_kernel,
        (cells, block),
        place,
        mine,
        theirs,
        own,
        other,
        scratch=[pltpu.VMEM((size, size), jnp.float32)] + factor_scratch(size),
        scalars=1,
    )
    return result.reshape(states.shape)


def with_halo(cells, axis, dim, width):
    count = lax.axis_size(axis)
    size = cells.shape[dim]
    head = lax.slice_in_dim(cells, 0, width, axis=dim)
    tail = lax.slice_in_dim(cells, size - width, size, axis=dim)
    before = lax.ppermute(tail, axis, [(i, (i + 1) % count) for i in range(count)])
    after = lax.ppermute(head, axis, [((i + 1) % count, i) for i in range(count)])
    return jnp.concatenate([before, cells, after], axis=dim)


def apply_ham(field, potential):
    padded_x = with_halo(field, "dx", 0, WIDTH)
    padded_y = with_halo(field, "dy", 1, WIDTH)
    size_x = field.shape[0]
    size_y = field.shape[1]
    lap = 3.0 * coeffs[0] * field
    for shift in range(1, WIDTH + 1):
        near = (
            padded_x[WIDTH + shift : WIDTH + shift + size_x]
            + padded_x[WIDTH - shift : WIDTH - shift + size_x]
            + padded_y[:, WIDTH + shift : WIDTH + shift + size_y]
            + padded_y[:, WIDTH - shift : WIDTH - shift + size_y]
        )
        near = near + jnp.roll(field, shift, 2) + jnp.roll(field, -shift, 2)
        lap = lap + coeffs[shift] * near
    return -0.5 * lap + potential[..., None] * field


def haloed(states, potential):
    prev = states
    cur = (apply_ham(states, potential) - centre_value * states) / half_width
    for step in range(1, DEGREE):
        nxt = 2.0 * (apply_ham(cur, potential) - centre_value * cur) / half_width - prev
        prev, cur = (cur, nxt)
    block = cur.shape[3]
    cells = cur.shape[0] * cur.shape[1] * cur.shape[2]
    local = cur.reshape(cells, block)
    gathered = lax.all_gather(local, "band", axis=1, tiled=True)
    total = cells * lax.axis_size("dx") * lax.axis_size("dy")
    partial = jnp.dot(gathered.T, gathered, precision=HIGHEST, preferred_element_type=jnp.float32) / total
    correlation = lax.psum(partial, ("dx", "dy"))
    size = correlation.shape[0]
    if size % LANES == 0:
        inverse = call(factor_kernel, (size, size), correlation, scratch=factor_scratch(size))
    else:
        factor = jnp.linalg.cholesky(correlation)
        inverse = jax.scipy.linalg.solve_triangular(factor, jnp.eye(size, dtype=jnp.float32), lower=True)
    my_rows = lax.dynamic_slice_in_dim(inverse, lax.axis_index("band") * block, block, 0)
    result = jnp.dot(gathered, my_rows.T, precision=HIGHEST, preferred_element_type=jnp.float32)
    return result.reshape(cur.shape)


def solution(mesh):
    domains_x, domains_y, bands = (mesh.shape[name] for name in ("dx", "dy", "band"))
    domains = domains_x * domains_y

    def run(states, potential):
        total_x, total_y, nz, size = states.shape
        size_x, size_y, block = total_x // domains_x, total_y // domains_y, size // bands
        if (
            nz == SUBLANES
            and size_y == SUBLANES
            and nz * size_x <= LANES
            and block * nz == LANES * domains
            and block % LANES == 0
            and bands == 2
            and size_x % bands == 0
            and domains_x % CORES == 0
            and (size // LANES) * (size // LANES + 1) * LANES % (2 * domains * bands * SUBLANES) == 0
            and total_x > 2 * WIDTH
            and total_y > 2 * WIDTH
        ):
            devices = mesh.devices.reshape(domains_x // CORES, CORES, domains_y, bands)
            body, over = transposed, jax.sharding.Mesh(devices, ("chip", "core", "dy", "band"))
            x_axis = ("chip", "core")
        else:
            body, over, x_axis = haloed, mesh, "dx"
        spec = P(x_axis, "dy", None, "band")
        return jax.shard_map(
            body, mesh=over, in_specs=(spec, P(x_axis, "dy", None)), out_specs=spec, check_vma=False
        )(states, potential)

    return run
```

```python
import functools

import jax
import jax.numpy as jnp
from jax import lax
from jax.experimental import pallas as pl
from jax.experimental.pallas import tpu as pltpu
from jax.sharding import PartitionSpec as P


DEGREE = 3
LANES = 128
SUBLANES = 8
PANEL = 32
PART = 16
CORES = 2

coeffs = (
    -5369.0 / 1800.0,
    12.0 / 7.0,
    -15.0 / 56.0,
    10.0 / 189.0,
    -1.0 / 112.0,
    2.0 / 1925.0,
    -1.0 / 16632.0,
)
WIDTH = len(coeffs) - 1
half_width = 5.0
centre_value = 7.0
VMEM = pl.BlockSpec(memory_space=pltpu.VMEM)
SMEM = pl.BlockSpec(memory_space=pltpu.SMEM)
ANY = pl.BlockSpec(memory_space=pl.ANY)
ROOM = pltpu.CompilerParams(vmem_limit_bytes=24 << 20)
HIGHEST = lax.Precision.HIGHEST


def dot(a, b, dims):
    return lax.dot_general(a, b, (dims, ((), ())), precision=HIGHEST, preferred_element_type=jnp.float32)


def swap_groups(arrays, group):
    count = len(arrays)
    lane = lax.broadcasted_iota(jnp.int32, arrays[0].shape, 1)
    bit = 1
    while bit < count:
        upper = (lane // (group * bit)) % 2 == 1
        out = list(arrays)
        for i in range(count):
            if i & bit == 0:
                low, high = arrays[i], arrays[i | bit]
                out[i] = jnp.where(upper, pltpu.roll(high, group * bit, 1), low)
                out[i | bit] = jnp.where(upper, high, pltpu.roll(low, LANES - group * bit, 1))
        arrays = out
        bit *= 2
    return arrays


def pack_kernel(nz, states_ref, potential_ref, out_ref):
    columns = states_ref.shape[0] // nz
    arrays = [states_ref[pl.ds(z, columns, stride=nz), :] for z in range(nz)]
    for g, value in enumerate(swap_groups(arrays, LANES // nz)):
        out_ref[g, :columns, :] = value
    row = lax.broadcasted_iota(jnp.int32, (nz, LANES), 0)
    lane = lax.broadcasted_iota(jnp.int32, (nz, LANES), 1)
    packed = jnp.zeros((potential_ref.shape[1], LANES), jnp.float32)
    for x in range(potential_ref.shape[0]):
        spread = jnp.where(lane == row + nz * x, 1.0, 0.0)
        packed = packed + dot(potential_ref[x], spread, ((1,), (0,)))
    for g in range(nz):
        out_ref[g, columns:, :] = packed


def filter_kernel(nz, domains_y, size_x, size_y, in_ref, out_ref, field, older, potential):
    domains = in_ref.shape[0]
    total_x = size_x * (domains // domains_y)
    total_y = size_y * domains_y
    columns = size_x * size_y
    group = LANES // nz

    def place(i, x):
        return size_x * (i // domains_y) + x, size_y * (i % domains_y)

    packed = in_ref[:, columns:, :].reshape(domains * size_y, LANES)
    source = lax.broadcasted_iota(jnp.int32, (LANES, LANES), 0)
    target = lax.broadcasted_iota(jnp.int32, (LANES, LANES), 1)
    for x in range(size_x):
        spread = jnp.where(source == nz * x + target // group, 1.0, 0.0)
        values = dot(packed, spread, ((1,), (0,)))
        for i in range(domains):
            at_x, at_y = place(i, x)
            potential[at_x, at_y : at_y + size_y, :] = values[size_y * i : size_y * (i + 1)] - centre_value
            field[WIDTH + at_x, at_y : at_y + size_y, :] = in_ref[i, size_y * x : size_y * (x + 1), :]

    weights = [0.0] * nz
    for k in range(1, WIDTH + 1):
        weights[k % nz] += coeffs[k]
        weights[-k % nz] += coeffs[k]

    for step in range(DEGREE):
        for k in range(WIDTH):
            field[k] = field[total_x + k]
            field[WIDTH + total_x + k] = field[WIDTH + k]
        scale = 1.0 / half_width if step == 0 else 2.0 / half_width

        def body(x, carry, step=step, scale=scale):
            value = field[WIDTH + x]
            lap = (3.0 * coeffs[0] + weights[0]) * value
            for k in range(1, WIDTH + 1):
                near = field[WIDTH + x + k] + field[WIDTH + x - k]
                near = near + pltpu.roll(value, k, 0) + pltpu.roll(value, total_y - k, 0)
                lap = lap + coeffs[k] * near
            for k in range(1, nz):
                lap = lap + weights[k] * pltpu.roll(value, group * k, 1)
            result = (potential[x] * value - 0.5 * lap) * scale
            if step > 0:
                result = result - older[(step - 1) % 2, x]
            older[step % 2, x] = value if step + 1 < DEGREE else result
            spare[x] = result
            return carry

        spare = older.at[2]
        lax.fori_loop(0, total_x, body, 0, unroll=2)
        if step + 1 < DEGREE:
            field[WIDTH : WIDTH + total_x] = spare[...]

    shares = out_ref.shape[0] // domains
    share = size_x // shares
    for i in range(domains):
        for x in range(size_x):
            at_x, at_y = place(i, x)
            row = size_y * (x % share)
            out_ref[i * shares + x // share, row : row + size_y, :] = older[2, at_x, at_y : at_y + size_y, :]


def upper_blocks(strips):
    return [(i, j) for i in range(strips) for j in range(i, strips)]


def share_of(strips, core):
    return upper_blocks(strips)[core :: CORES]


def gram_kernel(nz, bands, core_ref, own_in, other_in, cells_ref, out_ref, paired, own_ref, other_ref, arrived):
    fetches = [
        pltpu.make_async_copy(*copy, arrived.at[i])
        for i, copy in enumerate(((own_in, own_ref), (other_in, other_ref)))
    ]
    for fetch in fetches:
        fetch.start()
    columns = own_ref.shape[1]
    strips, rows, _ = cells_ref.shape
    per_band = strips // bands
    for half, ref in enumerate((own_ref, other_ref)):
        fetches[half].wait()
        for strip in range(strips):
            first = nz * (strip % per_band)
            arrays = [ref[(first + g) * bands + strip // per_band] for g in range(nz)]
            for z, value in enumerate(swap_groups(arrays, LANES // nz)):
                paired[strip, pl.ds(half * rows + z, columns, stride=nz), :] = value
    for strip in range(strips):
        cells_ref[strip] = paired[strip, :rows, :]
    for core in range(CORES):

        @pl.when(core_ref[0] == core)
        def _(core=core):
            for at, (i, j) in enumerate(share_of(strips, core)):
                out_ref[LANES * at : LANES * (at + 1), :] = dot(paired[i], paired[j], ((0,), (0,)))


def sum_kernel(total, in_ref, out_ref):
    value = in_ref[0]
    for i in range(1, in_ref.shape[0]):
        value = value + in_ref[i]
    value = value / total
    for i in range(out_ref.shape[0]):
        out_ref[i] = value


def spread_row(value, row):
    return jnp.broadcast_to(value[row : row + 1, :], value.shape)


def split(value):
    high = value.astype(jnp.bfloat16)
    rest = value - high.astype(jnp.float32)
    middle = rest.astype(jnp.bfloat16)
    return high, middle, (rest - middle.astype(jnp.float32)).astype(jnp.bfloat16)


def outer(left, right):
    a, b, c = left
    d, e, f = right
    left = jnp.concatenate([a, a, b, b, a, c], axis=0)
    right = jnp.concatenate([d, e, d, e, f, d], axis=0)
    return lax.dot_general(left, right, (((0,), (0,)), ((), ())), preferred_element_type=jnp.float32)


def eliminate(work, start):
    tiles = PANEL // SUBLANES
    strips = work.shape[1] // LANES
    sublane = lax.broadcasted_iota(jnp.int32, (SUBLANES, LANES), 0)
    at = lax.broadcasted_iota(jnp.int32, (SUBLANES, LANES), 1) - start
    rows = [
        [work[start + SUBLANES * t : start + SUBLANES * (t + 1), LANES * c : LANES * (c + 1)] for c in range(strips)]
        for t in range(tiles)
    ]
    pivots = [jnp.ones((SUBLANES, LANES), jnp.float32) for _ in range(tiles)]
    for first in range(0, PANEL, PART):
        column = {
            (j, t): jnp.broadcast_to(rows[t][0][:, start + j : start + j + 1], (SUBLANES, LANES))
            for j in range(first, first + PART)
            for t in range(j // SUBLANES, tiles)
        }
        inside = (at >= first) & (at < first + PART)
        for t in range(tiles):
            rows[t][0] = jnp.where(inside, jnp.where(at == sublane + SUBLANES * t, 1.0, 0.0), rows[t][0])
        for k in range(first, first + PART):
            tile, row = k // SUBLANES, k % SUBLANES
            pivot = spread_row(column[k, tile], row)
            pivots[tile] = jnp.where(sublane == row, pivot, pivots[tile])
            over = 1.0 / pivot
            factor = {t: column[k, t] * over for t in range(tile, tiles)}
            for j in range(k + 1, first + PART):
                value = spread_row(column[k, j // SUBLANES], j % SUBLANES)
                for t in range(j // SUBLANES, tiles):
                    column[j, t] = column[j, t] - factor[t] * value
            factor[tile] = jnp.where(sublane > row, factor[tile], 0.0)
            for c in range(strips):
                value = spread_row(rows[tile][c], row)
                for t in range(tile, tiles):
                    rows[t][c] = rows[t][c] - factor[t] * value
    scaled = [jnp.concatenate([v * lax.rsqrt(pivots[t]) for v in rows[t]], axis=1) for t in range(tiles)]
    return jnp.concatenate(scaled, axis=0)


def inverse_factor(matrix, inverse, work, done):
    strips = matrix.shape[0] // LANES

    def step(block, carry):
        base = pl.multiple_of(block * LANES, LANES)
        strip = [pl.multiple_of(lax.rem(block + c, strips) * LANES, LANES) for c in range(strips)]
        for c in range(strips):
            work[:, LANES * c : LANES * (c + 1)] = matrix[pl.ds(base, LANES), pl.ds(strip[c], LANES)]
        for start in range(0, LANES, PANEL):
            end = start + PANEL
            value = eliminate(work, start)
            lane = lax.broadcasted_iota(jnp.int32, (PANEL, LANES), 1)
            done[start:end, :LANES] = jnp.where(lane < end, value[:, :LANES], 0.0)
            done[start:end, LANES:] = value[:, LANES:]
            if end < LANES:
                parts = split(value)
                update = outer([part[:, :LANES] for part in parts], parts)
                lane = lax.broadcasted_iota(jnp.int32, (LANES - end, LANES), 1)
                old = jnp.where((lane >= start) & (lane < end), 0.0, work[end:, :LANES])
                work[end:, :LANES] = old - update[end:, :LANES]
                work[end:, LANES:] = work[end:, LANES:] - update[end:, LANES:]
        inverse[pl.ds(base, LANES), pl.ds(strip[0], LANES)] = done[:, :LANES]
        for c in range(1, strips):
            value = jnp.where(block + c >= strips, done[:, LANES * c : LANES * (c + 1)], 0.0)
            inverse[pl.ds(base, LANES), pl.ds(strip[c], LANES)] = value

        @pl.when(block + 1 < strips)
        def _():
            parts = split(done[...])
            for c in range(1, strips):

                @pl.when(block + c < strips)
                def _(c=c):
                    update = outer([part[:, LANES * c : LANES * (c + 1)] for part in parts], parts)
                    rows = pl.ds(pl.multiple_of((block + c) * LANES, LANES), LANES)
                    matrix[rows, pl.ds(strip[0], LANES)] = -update[:, :LANES]
                    for e in range(1, strips):
                        columns = pl.ds(strip[e], LANES)
                        matrix[rows, columns] = matrix[rows, columns] - update[:, LANES * e : LANES * (e + 1)]

        return carry

    lax.fori_loop(0, strips, step, 0)


def finish_kernel(place_ref, *refs):
    inputs, out_ref, buffers, arrived = refs[:4], refs[4], refs[5:9], refs[9]
    matrix, inverse, work, done = refs[10:]
    fetches = [pltpu.make_async_copy(*copy, arrived.at[i]) for i, copy in enumerate(zip(inputs, buffers))]
    for fetch in fetches:
        fetch.start()
    mine_ref, theirs_ref, own_ref, other_ref = buffers
    strips = own_ref.shape[0]
    cells = own_ref.shape[1]
    block = out_ref.shape[1]
    rows = mine_ref.shape[1]
    matrix[...] = jnp.zeros_like(matrix)
    fetches[0].wait()
    fetches[1].wait()
    for core in range(CORES):

        @pl.when(place_ref[0] == core)
        def _(core=core):
            for ref, holder in ((mine_ref, core), (theirs_ref, 1 - core)):
                for at, (i, j) in enumerate(share_of(strips, holder)):
                    for r in range(0, LANES, SUBLANES):
                        piece, row = divmod(LANES * at + r, rows)
                        top, left = LANES * i + r, LANES * j
                        matrix[top : top + SUBLANES, left : left + LANES] = ref[piece, row : row + SUBLANES, :]

    inverse_factor(matrix, inverse, work, done)
    fetches[2].wait()
    fetches[3].wait()
    band = place_ref[1]
    for b in range(strips * LANES // block):

        @pl.when(band == b)
        def _(b=b):
            used = block * (b + 1)
            mine = inverse[block * b : used, :used]
            for share, ref in ((b, own_ref), (1 - b, other_ref)):
                value = jnp.concatenate([ref[s] for s in range(used // LANES)], axis=1)
                out_ref[cells * share : cells * (share + 1), :] = dot(value, mine, ((1,), (1,)))


def factor_kernel(in_ref, out_ref, matrix, work, done):
    matrix[...] = in_ref[...]
    inverse_factor(matrix, out_ref, work, done)


def factor_scratch(size):
    return [pltpu.VMEM((rows, size), jnp.float32) for rows in (size, LANES, LANES)]


def call(kernel, shape, *args, scratch=(), scalars=0):
    specs = [SMEM] * scalars + [VMEM] * (len(args) - scalars)
    return pl.pallas_call(
        kernel,
        out_shape=jax.ShapeDtypeStruct(shape, jnp.float32),
        in_specs=specs,
        out_specs=VMEM,
        scratch_shapes=list(scratch),
        compiler_params=ROOM,
    )(*args)


def transposed(states, potential):
    size_x, size_y, nz, block = states.shape
    domains_y = lax.axis_size("dy")
    domains_x = lax.axis_size("chip") * CORES
    domains = domains_x * domains_y
    bands = lax.axis_size("band")
    cells = size_x * size_y * nz
    columns = size_x * size_y
    area = ("chip", "core", "dy")
    everyone = area + ("band",)
    same_core = ("chip", "dy", "band")
    swap = [(0, 1), (1, 0)]
    place = jnp.stack([lax.axis_index("core"), lax.axis_index("band")]).astype(jnp.int32)

    packed = pl.pallas_call(
        functools.partial(pack_kernel, nz),
        out_shape=jax.ShapeDtypeStruct((domains, columns + size_y, LANES), jnp.float32),
        grid=(block // LANES,),
        in_specs=[
            pl.BlockSpec((cells, LANES), lambda i: (0, i)),
            pl.BlockSpec((size_x, size_y, nz), lambda i: (0, 0, 0)),
        ],
        out_specs=pl.BlockSpec((nz, columns + size_y, LANES), lambda i: (i, 0, 0)),
        compiler_params=ROOM,
    )(states.reshape(cells, block), potential)
    packed = lax.all_to_all(packed, area, 0, 0, tiled=True)
    grid = (size_x * domains_x, size_y * domains_y, LANES)
    filtered = call(
        functools.partial(filter_kernel, nz, domains_y, size_x, size_y),
        (domains * bands, columns // bands, LANES),
        packed,
        scratch=[
            pltpu.VMEM((grid[0] + 2 * WIDTH,) + grid[1:], jnp.float32),
            pltpu.VMEM((3,) + grid, jnp.float32),
            pltpu.VMEM(grid, jnp.float32),
        ],
    )
    filtered = lax.all_to_all(filtered, everyone, 0, 0, tiled=True)
    size = block * bands
    strips = size // LANES
    rows = len(share_of(strips, 0)) * LANES
    holders = domains * bands // CORES
    neighbours = lax.ppermute(filtered, "core", swap)
    own, partial = pl.pallas_call(
        functools.partial(gram_kernel, nz, bands),
        out_shape=(
            jax.ShapeDtypeStruct((strips, cells // bands, LANES), jnp.float32),
            jax.ShapeDtypeStruct((rows, LANES), jnp.float32),
        ),
        in_specs=[SMEM, ANY, ANY],
        out_specs=(VMEM, VMEM),
        scratch_shapes=[
            pltpu.VMEM((strips, CORES * cells // bands, LANES), jnp.float32),
            pltpu.VMEM(filtered.shape, jnp.float32),
            pltpu.VMEM(filtered.shape, jnp.float32),
            pltpu.SemaphoreType.DMA((2,)),
        ],
        compiler_params=ROOM,
    )(place, filtered, neighbours)
    other = lax.ppermute(own, "band", swap)
    partial = lax.all_to_all(partial.reshape(holders, rows // holders, LANES), same_core, 0, 0, tiled=True)
    pieces = call(functools.partial(sum_kernel, float(cells * domains)), partial.shape, partial)
    mine = lax.all_to_all(pieces, same_core, 0, 0, tiled=True)
    theirs = lax.ppermute(mine, "core", swap)
    inputs = (mine, theirs, own, other)
    result = pl.pallas_call(
        finish_kernel,
        out_shape=jax.ShapeDtypeStruct((cells, block), jnp.float32),
        in_specs=[SMEM] + [ANY] * len(inputs),
        out_specs=VMEM,
        scratch_shapes=[pltpu.VMEM(value.shape, jnp.float32) for value in inputs]
        + [pltpu.SemaphoreType.DMA((len(inputs),)), pltpu.VMEM((size, size), jnp.float32)]
        + factor_scratch(size),
        compiler_params=ROOM,
    )(place, *inputs)
    return result.reshape(states.shape)


def with_halo(cells, axis, dim, width):
    count = lax.axis_size(axis)
    size = cells.shape[dim]
    head = lax.slice_in_dim(cells, 0, width, axis=dim)
    tail = lax.slice_in_dim(cells, size - width, size, axis=dim)
    before = lax.ppermute(tail, axis, [(i, (i + 1) % count) for i in range(count)])
    after = lax.ppermute(head, axis, [((i + 1) % count, i) for i in range(count)])
    return jnp.concatenate([before, cells, after], axis=dim)


def apply_ham(field, potential):
    padded_x = with_halo(field, "dx", 0, WIDTH)
    padded_y = with_halo(field, "dy", 1, WIDTH)
    size_x = field.shape[0]
    size_y = field.shape[1]
    lap = 3.0 * coeffs[0] * field
    for shift in range(1, WIDTH + 1):
        near = (
            padded_x[WIDTH + shift : WIDTH + shift + size_x]
            + padded_x[WIDTH - shift : WIDTH - shift + size_x]
            + padded_y[:, WIDTH + shift : WIDTH + shift + size_y]
            + padded_y[:, WIDTH - shift : WIDTH - shift + size_y]
        )
        near = near + jnp.roll(field, shift, 2) + jnp.roll(field, -shift, 2)
        lap = lap + coeffs[shift] * near
    return -0.5 * lap + potential[..., None] * field


def haloed(states, potential):
    prev = states
    cur = (apply_ham(states, potential) - centre_value * states) / half_width
    for _ in range(1, DEGREE):
        nxt = 2.0 * (apply_ham(cur, potential) - centre_value * cur) / half_width - prev
        prev, cur = (cur, nxt)
    block = cur.shape[3]
    cells = cur.shape[0] * cur.shape[1] * cur.shape[2]
    local = cur.reshape(cells, block)
    gathered = lax.all_gather(local, "band", axis=1, tiled=True)
    total = cells * lax.axis_size("dx") * lax.axis_size("dy")
    partial = jnp.dot(gathered.T, gathered, precision=HIGHEST, preferred_element_type=jnp.float32) / total
    correlation = lax.psum(partial, ("dx", "dy"))
    size = correlation.shape[0]
    if size % LANES == 0:
        inverse = call(factor_kernel, (size, size), correlation, scratch=factor_scratch(size))
    else:
        factor = jnp.linalg.cholesky(correlation)
        inverse = jax.scipy.linalg.solve_triangular(factor, jnp.eye(size, dtype=jnp.float32), lower=True)
    my_rows = lax.dynamic_slice_in_dim(inverse, lax.axis_index("band") * block, block, 0)
    result = jnp.dot(gathered, my_rows.T, precision=HIGHEST, preferred_element_type=jnp.float32)
    return result.reshape(cur.shape)


def solution(mesh):
    domains_x, domains_y, bands = (mesh.shape[name] for name in ("dx", "dy", "band"))
    domains = domains_x * domains_y

    def run(states, potential):
        total_x, total_y, nz, size = states.shape
        size_x, size_y, block = total_x // domains_x, total_y // domains_y, size // bands
        if (
            nz == SUBLANES
            and size_y == SUBLANES
            and nz * size_x <= LANES
            and block * nz == LANES * domains
            and block % LANES == 0
            and bands == 2
            and size_x % bands == 0
            and domains_x % CORES == 0
            and (size // LANES) * (size // LANES + 1) * LANES % (2 * domains * bands * SUBLANES) == 0
            and total_x > 2 * WIDTH
            and total_y > 2 * WIDTH
        ):
            devices = mesh.devices.reshape(domains_x // CORES, CORES, domains_y, bands)
            body, over = transposed, jax.sharding.Mesh(devices, ("chip", "core", "dy", "band"))
            x_axis = ("chip", "core")
        else:
            body, over, x_axis = haloed, mesh, "dx"
        spec = P(x_axis, "dy", None, "band")
        step = jax.shard_map(
            body, mesh=over, in_specs=(spec, P(x_axis, "dy", None)), out_specs=spec, check_vma=False
        )
        return step(states, potential)

    return run
```

```python
import functools

import jax
import jax.numpy as jnp
from jax import lax
from jax.experimental import pallas as pl
from jax.experimental.pallas import tpu as pltpu
from jax.sharding import PartitionSpec as P


DEGREE = 3
LANES = 128
SUBLANES = 8
PANEL = 32
PART = 16
CORES = 2
PRODUCTS = 6

coeffs = (
    -5369.0 / 1800.0,
    12.0 / 7.0,
    -15.0 / 56.0,
    10.0 / 189.0,
    -1.0 / 112.0,
    2.0 / 1925.0,
    -1.0 / 16632.0,
)
WIDTH = len(coeffs) - 1
half_width = 5.0
centre_value = 7.0
VMEM = pl.BlockSpec(memory_space=pltpu.VMEM)
SMEM = pl.BlockSpec(memory_space=pltpu.SMEM)
HBM = pl.BlockSpec(memory_space=pltpu.HBM)
ROOM = pltpu.CompilerParams(vmem_limit_bytes=24 << 20)
HIGHEST = lax.Precision.HIGHEST


def dot(a, b, dims):
    return lax.dot_general(a, b, (dims, ((), ())), precision=HIGHEST, preferred_element_type=jnp.float32)


def split(value):
    high = value.astype(jnp.bfloat16)
    rest = value - high.astype(jnp.float32)
    middle = rest.astype(jnp.bfloat16)
    return high, middle, (rest - middle.astype(jnp.float32)).astype(jnp.bfloat16)


def left_parts(parts):
    high, middle, low = parts
    return [high, high, middle, middle, high, low]


def right_parts(parts):
    high, middle, low = parts
    return [high, middle, high, middle, low, high]


def outer(left, right):
    left = jnp.concatenate(left_parts(left), axis=0)
    right = jnp.concatenate(right_parts(right), axis=0)
    return lax.dot_general(left, right, (((0,), (0,)), ((), ())), preferred_element_type=jnp.float32)


def product(left, right):
    left = jnp.concatenate(left_parts(left), axis=1)
    right = jnp.concatenate(right_parts(right), axis=0)
    return lax.dot_general(left, right, (((1,), (0,)), ((), ())), preferred_element_type=jnp.float32)


def swap_groups(arrays, group):
    count = len(arrays)
    lane = lax.broadcasted_iota(jnp.int32, arrays[0].shape, 1)
    bit = 1
    while bit < count:
        upper = (lane // (group * bit)) % 2 == 1
        out = list(arrays)
        for i in range(count):
            if i & bit == 0:
                low, high = arrays[i], arrays[i | bit]
                out[i] = jnp.where(upper, pltpu.roll(high, group * bit, 1), low)
                out[i | bit] = jnp.where(upper, high, pltpu.roll(low, LANES - group * bit, 1))
        arrays = out
        bit *= 2
    return arrays


def pack_kernel(nz, states_in, potential_in, out_ref, states, potential, arrived):
    halves = range(states.shape[0])
    fetches = [
        pltpu.make_async_copy(states_in.at[:, pl.ds(LANES * half, LANES)], states.at[half], arrived.at[half])
        for half in halves
    ]
    last = pltpu.make_async_copy(potential_in, potential, arrived.at[len(fetches)])
    for fetch in [last] + fetches:
        fetch.start()
    columns = states.shape[1] // nz
    row = lax.broadcasted_iota(jnp.int32, (nz, LANES), 0)
    lane = lax.broadcasted_iota(jnp.int32, (nz, LANES), 1)
    last.wait()
    packed = jnp.zeros((potential.shape[1], LANES), jnp.float32)
    for x in range(potential.shape[0]):
        spread = jnp.where(lane == row + nz * x, 1.0, 0.0)
        packed = packed + dot(potential[x], spread, ((1,), (0,)))
    for i in range(out_ref.shape[0]):
        out_ref[i, columns:, :] = packed
    for half in halves:
        fetches[half].wait()
        arrays = [states[half, pl.ds(z, columns, stride=nz), :] for z in range(nz)]
        for g, value in enumerate(swap_groups(arrays, LANES // nz)):
            out_ref[half * nz + g, :columns, :] = value


def filter_kernel(nz, domains_y, size_x, size_y, in_ref, out_ref, field, potential):
    domains = in_ref.shape[0]
    total_x = size_x * (domains // domains_y)
    total_y = size_y * domains_y
    columns = size_x * size_y
    group = LANES // nz
    shares = out_ref.shape[0] // domains
    share = size_x // shares

    def place(i, x):
        return size_x * (i // domains_y) + x, size_y * (i % domains_y)

    def keep(which, x, rows, value):
        field[which, WIDTH + x, rows, :] = value
        if x < WIDTH:
            field[which, WIDTH + total_x + x, rows, :] = value
        if x >= total_x - WIDTH:
            field[which, WIDTH + x - total_x, rows, :] = value

    packed = in_ref[:, columns:, :].reshape(domains * size_y, LANES)
    source = lax.broadcasted_iota(jnp.int32, (LANES, LANES), 0)
    target = lax.broadcasted_iota(jnp.int32, (LANES, LANES), 1)
    for x in range(size_x):
        spread = jnp.where(source == nz * x + target // group, 1.0, 0.0)
        values = dot(packed, spread, ((1,), (0,)))
        for i in range(domains):
            at_x, at_y = place(i, x)
            rows = slice(at_y, at_y + size_y)
            potential[at_x, rows, :] = values[size_y * i : size_y * (i + 1)] - centre_value
            keep(0, at_x, rows, in_ref[i, size_y * x : size_y * (x + 1), :])

    def ring(distance, size):
        value = jnp.zeros(distance.shape, jnp.float32)
        for k in range(1, WIDTH + 1):
            for shift in (k, -k):
                value = value + jnp.where(distance == shift % size, coeffs[k], 0.0)
        return value

    along_z = ring((source // group - target // group + nz) % nz, nz)
    along_z = jnp.where((source - target) % group == 0, along_z, 0.0)
    along_z = along_z + jnp.where(source == target, 3.0 * coeffs[0], 0.0)
    along_z = jnp.concatenate(right_parts(split(along_z)), axis=0)
    shape = (total_y, PRODUCTS * total_y)
    row = lax.broadcasted_iota(jnp.int32, shape, 0)
    lane = lax.broadcasted_iota(jnp.int32, shape, 1)
    ring_y = ring((row - lane % total_y + total_y) % total_y, total_y)
    along_y = jnp.zeros(shape, jnp.float32)
    for part, value in enumerate(left_parts(split(ring_y))):
        along_y = jnp.where(lane // total_y == part, value.astype(jnp.float32), along_y)
    along_y = along_y.astype(jnp.bfloat16)

    for step in range(DEGREE):
        now, other = step % 2, (step + 1) % 2
        scale = 1.0 / half_width if step == 0 else 2.0 / half_width
        for x in range(total_x):
            value = field[now, WIDTH + x]
            parts = split(value)
            lap = lax.dot_general(
                jnp.concatenate(left_parts(parts), axis=1),
                along_z,
                (((1,), (0,)), ((), ())),
                preferred_element_type=jnp.float32,
            )
            lap = lap + lax.dot_general(
                along_y,
                jnp.concatenate(right_parts(parts), axis=0),
                (((1,), (0,)), ((), ())),
                preferred_element_type=jnp.float32,
            )
            for k in range(1, WIDTH + 1):
                lap = lap + coeffs[k] * (field[now, WIDTH + x + k] + field[now, WIDTH + x - k])
            result = (potential[x] * value - 0.5 * lap) * scale
            if step > 0:
                result = result - field[other, WIDTH + x]
            if step + 1 < DEGREE:
                keep(other, x, slice(None), result)
                continue
            for j in range(domains_y):
                i = x // size_x * domains_y + j
                row = size_y * (x % share)
                out_ref[i * shares + x % size_x // share, row : row + size_y, :] = result[size_y * j : size_y * (j + 1)]


def unpack(nz, in_ref, bands, strip, out_ref, offset):
    per_band = nz_strips(in_ref, nz, bands)
    first = nz * (strip % per_band)
    arrays = [in_ref[(first + g) * bands + strip // per_band] for g in range(nz)]
    for z, value in enumerate(swap_groups(arrays, LANES // nz)):
        out_ref[strip, pl.ds(offset + z, in_ref.shape[1], stride=nz), :] = value


def nz_strips(in_ref, nz, bands):
    return in_ref.shape[0] // (nz * bands)


def upper_blocks(strips):
    return [(i, j) for i in range(strips) for j in range(i, strips)]


def share_of(strips, core):
    return upper_blocks(strips)[core :: CORES]


def gram_kernel(nz, bands, core_ref, own_ref, other_ref, cells_ref, out_ref, paired):
    strips, rows, _ = cells_ref.shape
    for strip in range(strips):
        unpack(nz, own_ref, bands, strip, paired, 0)
        unpack(nz, other_ref, bands, strip, paired, rows)
        cells_ref[strip] = paired[strip, :rows, :]
    parts = [split(paired[strip]) for strip in range(strips)]
    for core in range(CORES):

        @pl.when(core_ref[0] == core)
        def _(core=core):
            for at, (i, j) in enumerate(share_of(strips, core)):
                out_ref[LANES * at : LANES * (at + 1), :] = outer(parts[i], parts[j])


def sum_kernel(total, in_ref, out_ref):
    value = in_ref[0]
    for i in range(1, in_ref.shape[0]):
        value = value + in_ref[i]
    value = value / total
    for i in range(out_ref.shape[0]):
        out_ref[i] = value


def spread_row(value, row):
    return jnp.broadcast_to(value[row : row + 1, :], value.shape)


def eliminate(rows, start):
    rows = list(rows)
    tiles = len(rows)
    sublane = lax.broadcasted_iota(jnp.int32, (SUBLANES, LANES), 0)
    at = lax.broadcasted_iota(jnp.int32, (SUBLANES, LANES), 1) - start
    pivots = [jnp.ones((SUBLANES, LANES), jnp.float32) for _ in range(tiles)]
    for first in range(0, PANEL, PART):
        column = {
            (j, t): jnp.broadcast_to(rows[t][:, start + j : start + j + 1], (SUBLANES, LANES))
            for j in range(first, first + PART)
            for t in range(j // SUBLANES, tiles)
        }
        inside = (at >= first) & (at < first + PART)
        for t in range(tiles):
            rows[t] = jnp.where(inside, jnp.where(at == sublane + SUBLANES * t, 1.0, 0.0), rows[t])
        for k in range(first, first + PART):
            tile, row = k // SUBLANES, k % SUBLANES
            pivot = spread_row(column[k, tile], row)
            pivots[tile] = jnp.where(sublane == row, pivot, pivots[tile])
            over = 1.0 / pivot
            factor = {t: column[k, t] * over for t in range(tile, tiles)}
            for j in range(k + 1, first + PART):
                value = spread_row(column[k, j // SUBLANES], j % SUBLANES)
                for t in range(j // SUBLANES, tiles):
                    column[j, t] = column[j, t] - factor[t] * value
            factor[tile] = jnp.where(sublane > row, factor[tile], 0.0)
            value = spread_row(rows[tile], row)
            for t in range(tile, tiles):
                rows[t] = rows[t] - factor[t] * value
    return [rows[t] * lax.rsqrt(pivots[t]) for t in range(tiles)]


def inverse_of_block(value):
    rest = [value[t : t + SUBLANES] for t in range(0, LANES, SUBLANES)]
    lane = lax.broadcasted_iota(jnp.int32, (SUBLANES, LANES), 1)
    out = []
    for start in range(0, LANES, PANEL):
        end = start + PANEL
        rows = eliminate(rest[start // SUBLANES : end // SUBLANES], start)
        out += [jnp.where(lane < end, row, 0.0) for row in rows]
        if end < LANES:
            parts = split(jnp.concatenate(rows, axis=0))
            update = outer(parts, parts)
            for t in range(end // SUBLANES, LANES // SUBLANES):
                old = jnp.where((lane >= start) & (lane < end), 0.0, rest[t])
                rest[t] = old - update[SUBLANES * t : SUBLANES * (t + 1)]
    return jnp.concatenate(out, axis=0)


def beside(left, right):
    return tuple(jnp.concatenate(pair, axis=1) for pair in zip(left, right))


def inverse_factor(matrix, inverse):
    size = matrix.shape[0]
    for low in range(0, size, LANES):
        high = low + LANES
        rows = slice(low, high)
        block = inverse_of_block(matrix[rows, rows])
        left = split(block)
        inverse[rows, rows] = block
        if high < size:
            inverse[rows, high:] = jnp.zeros((LANES, size - high), jnp.float32)
            following = slice(high, high + LANES)
            above = split(product(left, split(matrix[rows, following])))
            matrix[following, following] = matrix[following, following] - outer(above, above)
            if high + LANES < size:
                above = beside(above, split(product(left, split(matrix[rows, high + LANES :]))))
        below = left
        if low:
            value = product(left, split(matrix[rows, :low]))
            inverse[rows, :low] = value
            below = beside(split(value), left)
        for at in range(high, size, LANES):
            mine = tuple(part[:, at - high : at - high + LANES] for part in above)
            target = slice(at, at + LANES)
            update = outer(mine, below)
            if low:
                matrix[target, :low] = matrix[target, :low] - update[:, :low]
            matrix[target, rows] = -update[:, low:]
            first = max(at, high + LANES)
            if first < size:
                update = outer(mine, tuple(part[:, first - high :] for part in above))
                matrix[target, first:] = matrix[target, first:] - update


def finish_kernel(place_ref, mine_ref, theirs_ref, own_ref, other_ref, out_ref, matrix, inverse):
    strips = own_ref.shape[0]
    cells = own_ref.shape[1]
    block = out_ref.shape[1]
    rows = mine_ref.shape[1]
    for core in range(CORES):

        @pl.when(place_ref[0] == core)
        def _(core=core):
            for ref, holder in ((mine_ref, core), (theirs_ref, 1 - core)):
                for at, (i, j) in enumerate(share_of(strips, holder)):
                    for r in range(0, LANES, SUBLANES):
                        piece, row = divmod(LANES * at + r, rows)
                        top, left = LANES * i + r, LANES * j
                        matrix[top : top + SUBLANES, left : left + LANES] = ref[piece, row : row + SUBLANES, :]

    inverse_factor(matrix, inverse)
    band = place_ref[1]
    for b in range(strips * LANES // block):

        @pl.when(band == b)
        def _(b=b):
            used = block * (b + 1)
            mine = inverse[block * b : used, :used]
            for share, ref in ((b, own_ref), (1 - b, other_ref)):
                value = jnp.concatenate([ref[s] for s in range(used // LANES)], axis=1)
                out_ref[cells * share : cells * (share + 1), :] = dot(value, mine, ((1,), (1,)))


def factor_kernel(in_ref, out_ref, matrix):
    matrix[...] = in_ref[...]
    inverse_factor(matrix, out_ref)


def call(kernel, shape, *args, scratch=(), scalars=0):
    specs = [SMEM] * scalars + [VMEM] * (len(args) - scalars)
    return pl.pallas_call(
        kernel,
        out_shape=jax.ShapeDtypeStruct(shape, jnp.float32),
        in_specs=specs,
        out_specs=VMEM,
        scratch_shapes=list(scratch),
        compiler_params=ROOM,
    )(*args)


def transposed(states, potential):
    size_x, size_y, nz, block = states.shape
    domains_y = lax.axis_size("dy")
    domains_x = lax.axis_size("chip") * CORES
    domains = domains_x * domains_y
    bands = lax.axis_size("band")
    cells = size_x * size_y * nz
    columns = size_x * size_y
    area = ("chip", "core", "dy")
    everyone = area + ("band",)
    same_core = ("chip", "dy", "band")
    swap = [(0, 1), (1, 0)]
    place = jnp.stack([lax.axis_index("core"), lax.axis_index("band")]).astype(jnp.int32)

    packed = pl.pallas_call(
        functools.partial(pack_kernel, nz),
        out_shape=jax.ShapeDtypeStruct((domains, columns + size_y, LANES), jnp.float32),
        in_specs=[HBM, HBM],
        out_specs=VMEM,
        scratch_shapes=[
            pltpu.VMEM((block // LANES, cells, LANES), jnp.float32),
            pltpu.VMEM(potential.shape, jnp.float32),
            pltpu.SemaphoreType.DMA((block // LANES + 1,)),
        ],
        compiler_params=ROOM,
    )(*(pltpu.with_memory_space_constraint(v, pltpu.HBM) for v in (states.reshape(cells, block), potential)))
    packed = lax.all_to_all(packed, area, 0, 0, tiled=True)
    grid = (size_x * domains_x, size_y * domains_y, LANES)
    filtered = call(
        functools.partial(filter_kernel, nz, domains_y, size_x, size_y),
        (domains * bands, columns // bands, LANES),
        packed,
        scratch=[
            pltpu.VMEM((2, grid[0] + 2 * WIDTH) + grid[1:], jnp.float32),
            pltpu.VMEM(grid, jnp.float32),
        ],
    )
    filtered = lax.all_to_all(filtered, everyone, 0, 0, tiled=True)
    size = block * bands
    strips = size // LANES
    rows = len(share_of(strips, 0)) * LANES
    holders = domains * bands // CORES
    neighbours = lax.ppermute(filtered, "core", swap)
    own, partial = pl.pallas_call(
        functools.partial(gram_kernel, nz, bands),
        out_shape=(
            jax.ShapeDtypeStruct((strips, cells // bands, LANES), jnp.float32),
            jax.ShapeDtypeStruct((rows, LANES), jnp.float32),
        ),
        in_specs=[SMEM, VMEM, VMEM],
        out_specs=(VMEM, VMEM),
        scratch_shapes=[pltpu.VMEM((strips, CORES * cells // bands, LANES), jnp.float32)],
        compiler_params=ROOM,
    )(place, filtered, neighbours)
    other = lax.ppermute(own, "band", swap)
    partial = lax.all_to_all(partial.reshape(holders, rows // holders, LANES), same_core, 0, 0, tiled=True)
    pieces = call(functools.partial(sum_kernel, float(cells * domains)), partial.shape, partial)
    mine = lax.all_to_all(pieces, same_core, 0, 0, tiled=True)
    theirs = lax.ppermute(mine, "core", swap)
    result = call(
        finish_kernel,
        (cells, block),
        place,
        mine,
        theirs,
        own,
        other,
        scratch=[pltpu.VMEM((size, size), jnp.float32)] * 2,
        scalars=1,
    )
    return result.reshape(states.shape)


def with_halo(cells, axis, dim, width):
    count = lax.axis_size(axis)
    size = cells.shape[dim]
    head = lax.slice_in_dim(cells, 0, width, axis=dim)
    tail = lax.slice_in_dim(cells, size - width, size, axis=dim)
    before = lax.ppermute(tail, axis, [(i, (i + 1) % count) for i in range(count)])
    after = lax.ppermute(head, axis, [((i + 1) % count, i) for i in range(count)])
    return jnp.concatenate([before, cells, after], axis=dim)


def apply_ham(field, potential):
    padded_x = with_halo(field, "dx", 0, WIDTH)
    padded_y = with_halo(field, "dy", 1, WIDTH)
    size_x = field.shape[0]
    size_y = field.shape[1]
    lap = 3.0 * coeffs[0] * field
    for shift in range(1, WIDTH + 1):
        near = (
            padded_x[WIDTH + shift : WIDTH + shift + size_x]
            + padded_x[WIDTH - shift : WIDTH - shift + size_x]
            + padded_y[:, WIDTH + shift : WIDTH + shift + size_y]
            + padded_y[:, WIDTH - shift : WIDTH - shift + size_y]
        )
        near = near + jnp.roll(field, shift, 2) + jnp.roll(field, -shift, 2)
        lap = lap + coeffs[shift] * near
    return -0.5 * lap + potential[..., None] * field


def haloed(states, potential):
    prev = states
    cur = (apply_ham(states, potential) - centre_value * states) / half_width
    for _ in range(1, DEGREE):
        nxt = 2.0 * (apply_ham(cur, potential) - centre_value * cur) / half_width - prev
        prev, cur = (cur, nxt)
    block = cur.shape[3]
    cells = cur.shape[0] * cur.shape[1] * cur.shape[2]
    local = cur.reshape(cells, block)
    gathered = lax.all_gather(local, "band", axis=1, tiled=True)
    total = cells * lax.axis_size("dx") * lax.axis_size("dy")
    partial = jnp.dot(gathered.T, gathered, precision=HIGHEST, preferred_element_type=jnp.float32) / total
    correlation = lax.psum(partial, ("dx", "dy"))
    size = correlation.shape[0]
    if size % LANES == 0:
        inverse = call(factor_kernel, (size, size), correlation, scratch=[pltpu.VMEM((size, size), jnp.float32)])
    else:
        factor = jnp.linalg.cholesky(correlation)
        inverse = jax.scipy.linalg.solve_triangular(factor, jnp.eye(size, dtype=jnp.float32), lower=True)
    my_rows = lax.dynamic_slice_in_dim(inverse, lax.axis_index("band") * block, block, 0)
    result = jnp.dot(gathered, my_rows.T, precision=HIGHEST, preferred_element_type=jnp.float32)
    return result.reshape(cur.shape)


def solution(mesh):
    domains_x, domains_y, bands = (mesh.shape[name] for name in ("dx", "dy", "band"))
    domains = domains_x * domains_y

    def run(states, potential):
        total_x, total_y, nz, size = states.shape
        size_x, size_y, block = total_x // domains_x, total_y // domains_y, size // bands
        if (
            nz == SUBLANES
            and size_y == SUBLANES
            and nz * size_x <= LANES
            and block * nz == LANES * domains
            and block % LANES == 0
            and bands == 2
            and size_x % bands == 0
            and domains_x % CORES == 0
            and (size // LANES) * (size // LANES + 1) * LANES % (2 * domains * bands * SUBLANES) == 0
            and total_x > 2 * WIDTH
            and total_y > 2 * WIDTH
        ):
            devices = mesh.devices.reshape(domains_x // CORES, CORES, domains_y, bands)
            body, over = transposed, jax.sharding.Mesh(devices, ("chip", "core", "dy", "band"))
            x_axis = ("chip", "core")
        else:
            body, over, x_axis = haloed, mesh, "dx"
        spec = P(x_axis, "dy", None, "band")
        step = jax.shard_map(
            body, mesh=over, in_specs=(spec, P(x_axis, "dy", None)), out_specs=spec, check_vma=False
        )
        return step(states, potential)

    return run
```

```python
import functools

import jax
import jax.numpy as jnp
from jax import lax
from jax.experimental import pallas as pl
from jax.experimental.pallas import tpu as pltpu
from jax.sharding import PartitionSpec as P


DEGREE = 3
LANES = 128
SUBLANES = 8
PANEL = 32
PART = 16
CORES = 2
PRODUCTS = 6

coeffs = (
    -5369.0 / 1800.0,
    12.0 / 7.0,
    -15.0 / 56.0,
    10.0 / 189.0,
    -1.0 / 112.0,
    2.0 / 1925.0,
    -1.0 / 16632.0,
)
WIDTH = len(coeffs) - 1
half_width = 5.0
centre_value = 7.0
VMEM = pl.BlockSpec(memory_space=pltpu.VMEM)
SMEM = pl.BlockSpec(memory_space=pltpu.SMEM)
HBM = pl.BlockSpec(memory_space=pltpu.HBM)
ROOM = pltpu.CompilerParams(vmem_limit_bytes=24 << 20)
HIGHEST = lax.Precision.HIGHEST


def dot(a, b, dims):
    return lax.dot_general(a, b, (dims, ((), ())), precision=HIGHEST, preferred_element_type=jnp.float32)


def split(value):
    high = value.astype(jnp.bfloat16)
    rest = value - high.astype(jnp.float32)
    middle = rest.astype(jnp.bfloat16)
    return high, middle, (rest - middle.astype(jnp.float32)).astype(jnp.bfloat16)


def left_parts(parts):
    high, middle, low = parts
    return [high, high, middle, middle, high, low]


def right_parts(parts):
    high, middle, low = parts
    return [high, middle, high, middle, low, high]


def outer(left, right):
    left = jnp.concatenate(left_parts(left), axis=0)
    right = jnp.concatenate(right_parts(right), axis=0)
    return lax.dot_general(left, right, (((0,), (0,)), ((), ())), preferred_element_type=jnp.float32)


def product(left, right):
    left = jnp.concatenate(left_parts(left), axis=1)
    right = jnp.concatenate(right_parts(right), axis=0)
    return lax.dot_general(left, right, (((1,), (0,)), ((), ())), preferred_element_type=jnp.float32)


def swap_groups(arrays, group):
    count = len(arrays)
    lane = lax.broadcasted_iota(jnp.int32, arrays[0].shape, 1)
    bit = 1
    while bit < count:
        upper = (lane // (group * bit)) % 2 == 1
        out = list(arrays)
        for i in range(count):
            if i & bit == 0:
                low, high = arrays[i], arrays[i | bit]
                out[i] = jnp.where(upper, pltpu.roll(high, group * bit, 1), low)
                out[i | bit] = jnp.where(upper, high, pltpu.roll(low, LANES - group * bit, 1))
        arrays = out
        bit *= 2
    return arrays


def pack_kernel(nz, states_in, potential_in, out_ref, states, potential, arrived):
    halves = range(states.shape[0])
    fetches = [
        pltpu.make_async_copy(states_in.at[:, pl.ds(LANES * half, LANES)], states.at[half], arrived.at[half])
        for half in halves
    ]
    last = pltpu.make_async_copy(potential_in, potential, arrived.at[len(fetches)])
    for fetch in [last] + fetches:
        fetch.start()
    columns = states.shape[1] // nz
    row = lax.broadcasted_iota(jnp.int32, (nz, LANES), 0)
    lane = lax.broadcasted_iota(jnp.int32, (nz, LANES), 1)
    last.wait()
    packed = jnp.zeros((potential.shape[1], LANES), jnp.float32)
    for x in range(potential.shape[0]):
        spread = jnp.where(lane == row + nz * x, 1.0, 0.0)
        packed = packed + dot(potential[x], spread, ((1,), (0,)))
    for i in range(out_ref.shape[0]):
        out_ref[i, columns:, :] = packed
    for half in halves:
        fetches[half].wait()
        arrays = [states[half, pl.ds(z, columns, stride=nz), :] for z in range(nz)]
        for g, value in enumerate(swap_groups(arrays, LANES // nz)):
            out_ref[half * nz + g, :columns, :] = value


def filter_kernel(nz, domains_y, size_x, size_y, in_ref, out_ref, field, potential):
    domains = in_ref.shape[0]
    total_x = size_x * (domains // domains_y)
    total_y = size_y * domains_y
    columns = size_x * size_y
    group = LANES // nz
    shares = out_ref.shape[0] // domains
    share = size_x // shares

    def place(i, x):
        return size_x * (i // domains_y) + x, size_y * (i % domains_y)

    def keep(which, x, rows, value):
        field[which, WIDTH + x, rows, :] = value
        if x < WIDTH:
            field[which, WIDTH + total_x + x, rows, :] = value
        if x >= total_x - WIDTH:
            field[which, WIDTH + x - total_x, rows, :] = value

    packed = in_ref[:, columns:, :].reshape(domains * size_y, LANES)
    source = lax.broadcasted_iota(jnp.int32, (LANES, LANES), 0)
    target = lax.broadcasted_iota(jnp.int32, (LANES, LANES), 1)
    for x in range(size_x):
        spread = jnp.where(source == nz * x + target // group, 1.0, 0.0)
        values = dot(packed, spread, ((1,), (0,)))
        for i in range(domains):
            at_x, at_y = place(i, x)
            rows = slice(at_y, at_y + size_y)
            potential[at_x, rows, :] = values[size_y * i : size_y * (i + 1)] - centre_value
            keep(0, at_x, rows, in_ref[i, size_y * x : size_y * (x + 1), :])

    def ring(distance, size):
        value = jnp.zeros(distance.shape, jnp.float32)
        for k in range(1, WIDTH + 1):
            for shift in (k, -k):
                value = value + jnp.where(distance == shift % size, coeffs[k], 0.0)
        return value

    along_z = ring((source // group - target // group + nz) % nz, nz)
    along_z = jnp.where((source - target) % group == 0, along_z, 0.0)
    along_z = along_z + jnp.where(source == target, 3.0 * coeffs[0], 0.0)
    along_z = jnp.concatenate(right_parts(split(along_z)), axis=0)
    shape = (total_y, PRODUCTS * total_y)
    row = lax.broadcasted_iota(jnp.int32, shape, 0)
    lane = lax.broadcasted_iota(jnp.int32, shape, 1)
    ring_y = ring((row - lane % total_y + total_y) % total_y, total_y)
    along_y = jnp.zeros(shape, jnp.float32)
    for part, value in enumerate(left_parts(split(ring_y))):
        along_y = jnp.where(lane // total_y == part, value.astype(jnp.float32), along_y)
    along_y = along_y.astype(jnp.bfloat16)

    for step in range(DEGREE):
        now, other = step % 2, (step + 1) % 2
        scale = 1.0 / half_width if step == 0 else 2.0 / half_width
        for x in range(total_x):
            value = field[now, WIDTH + x]
            parts = split(value)
            lap = lax.dot_general(
                jnp.concatenate(left_parts(parts), axis=1),
                along_z,
                (((1,), (0,)), ((), ())),
                preferred_element_type=jnp.float32,
            )
            lap = lap + lax.dot_general(
                along_y,
                jnp.concatenate(right_parts(parts), axis=0),
                (((1,), (0,)), ((), ())),
                preferred_element_type=jnp.float32,
            )
            for k in range(1, WIDTH + 1):
                lap = lap + coeffs[k] * (field[now, WIDTH + x + k] + field[now, WIDTH + x - k])
            result = (potential[x] * value - 0.5 * lap) * scale
            if step > 0:
                result = result - field[other, WIDTH + x]
            if step + 1 < DEGREE:
                keep(other, x, slice(None), result)
                continue
            for j in range(domains_y):
                i = x // size_x * domains_y + j
                row = size_y * (x % share)
                out_ref[i * shares + x % size_x // share, row : row + size_y, :] = result[size_y * j : size_y * (j + 1)]


def unpack(nz, bands, in_ref, strip):
    per_band = in_ref.shape[0] // (nz * bands)
    first = nz * (strip % per_band)
    arrays = [in_ref[(first + g) * bands + strip // per_band] for g in range(nz)]
    return swap_groups(arrays, LANES // nz)


def unpack_kernel(nz, bands, in_ref, out_ref):
    for strip in range(out_ref.shape[0]):
        for z, value in enumerate(unpack(nz, bands, in_ref, strip)):
            out_ref[strip, pl.ds(z, in_ref.shape[1], stride=nz), :] = value


def upper_blocks(strips):
    return [(i, j) for i in range(strips) for j in range(i, strips)]


def share_of(strips, core):
    return upper_blocks(strips)[core :: CORES]


def gram_kernel(nz, bands, core_ref, own_ref, other_in, out_ref, other_ref):
    strips = own_ref.shape[0]
    unpack_kernel(nz, bands, other_in, other_ref)
    parts = [split(jnp.concatenate([own_ref[strip], other_ref[strip]], axis=0)) for strip in range(strips)]
    for core in range(CORES):

        @pl.when(core_ref[0] == core)
        def _(core=core):
            for at, (i, j) in enumerate(share_of(strips, core)):
                out_ref[LANES * at : LANES * (at + 1), :] = outer(parts[i], parts[j])


def sum_kernel(total, in_ref, out_ref):
    value = in_ref[0]
    for i in range(1, in_ref.shape[0]):
        value = value + in_ref[i]
    value = value / total
    for i in range(out_ref.shape[0]):
        out_ref[i] = value


def spread_row(value, row):
    return jnp.broadcast_to(value[row : row + 1, :], value.shape)


def eliminate(rows, start):
    rows = list(rows)
    tiles = len(rows)
    sublane = lax.broadcasted_iota(jnp.int32, (SUBLANES, LANES), 0)
    at = lax.broadcasted_iota(jnp.int32, (SUBLANES, LANES), 1) - start
    pivots = [jnp.ones((SUBLANES, LANES), jnp.float32) for _ in range(tiles)]
    for first in range(0, PANEL, PART):
        column = {
            (j, t): jnp.broadcast_to(rows[t][:, start + j : start + j + 1], (SUBLANES, LANES))
            for j in range(first, first + PART)
            for t in range(j // SUBLANES, tiles)
        }
        inside = (at >= first) & (at < first + PART)
        for t in range(tiles):
            rows[t] = jnp.where(inside, jnp.where(at == sublane + SUBLANES * t, 1.0, 0.0), rows[t])
        for k in range(first, first + PART):
            tile, row = k // SUBLANES, k % SUBLANES
            pivot = spread_row(column[k, tile], row)
            pivots[tile] = jnp.where(sublane == row, pivot, pivots[tile])
            over = 1.0 / pivot
            factor = {t: column[k, t] * over for t in range(tile, tiles)}
            for j in range(k + 1, first + PART):
                value = spread_row(column[k, j // SUBLANES], j % SUBLANES)
                for t in range(j // SUBLANES, tiles):
                    column[j, t] = column[j, t] - factor[t] * value
            factor[tile] = jnp.where(sublane > row, factor[tile], 0.0)
            value = spread_row(rows[tile], row)
            for t in range(tile, tiles):
                rows[t] = rows[t] - factor[t] * value
    return [rows[t] * lax.rsqrt(pivots[t]) for t in range(tiles)]


def inverse_of_block(value):
    rest = [value[t : t + SUBLANES] for t in range(0, LANES, SUBLANES)]
    lane = lax.broadcasted_iota(jnp.int32, (SUBLANES, LANES), 1)
    out = []
    for start in range(0, LANES, PANEL):
        end = start + PANEL
        rows = eliminate(rest[start // SUBLANES : end // SUBLANES], start)
        out += [jnp.where(lane < end, row, 0.0) for row in rows]
        if end < LANES:
            parts = split(jnp.concatenate(rows, axis=0))
            update = outer(parts, parts)
            for t in range(end // SUBLANES, LANES // SUBLANES):
                old = jnp.where((lane >= start) & (lane < end), 0.0, rest[t])
                rest[t] = old - update[SUBLANES * t : SUBLANES * (t + 1)]
    return jnp.concatenate(out, axis=0)


def beside(left, right):
    return tuple(jnp.concatenate(pair, axis=1) for pair in zip(left, right))


def inverse_factor(matrix, inverse):
    size = matrix.shape[0]
    for low in range(0, size, LANES):
        high = low + LANES
        rows = slice(low, high)
        block = inverse_of_block(matrix[rows, rows])
        left = split(block)
        inverse[rows, rows] = block
        if high < size:
            inverse[rows, high:] = jnp.zeros((LANES, size - high), jnp.float32)
            following = slice(high, high + LANES)
            above = split(product(left, split(matrix[rows, following])))
            matrix[following, following] = matrix[following, following] - outer(above, above)
            if high + LANES < size:
                above = beside(above, split(product(left, split(matrix[rows, high + LANES :]))))
        below = left
        if low:
            value = product(left, split(matrix[rows, :low]))
            inverse[rows, :low] = value
            below = beside(split(value), left)
        for at in range(high, size, LANES):
            mine = tuple(part[:, at - high : at - high + LANES] for part in above)
            target = slice(at, at + LANES)
            update = outer(mine, below)
            if low:
                matrix[target, :low] = matrix[target, :low] - update[:, :low]
            matrix[target, rows] = -update[:, low:]
            first = max(at, high + LANES)
            if first < size:
                update = outer(mine, tuple(part[:, first - high :] for part in above))
                matrix[target, first:] = matrix[target, first:] - update


def prepare_kernel(place_ref, own_ref, first_ref, second_ref, *out_refs):
    strips, cells, _ = own_ref.shape
    band = place_ref[1]
    for strip in range(strips):
        received = first_ref if strip < strips // 2 else second_ref
        for share, value in ((band, own_ref[strip]), (1 - band, received[strip % (strips // 2)])):
            rows = pl.ds(pl.multiple_of(share * cells, cells), cells)
            for ref, part in zip(out_refs, split(value)):
                ref[strip, rows, :] = part


def finish_kernel(place_ref, mine_ref, theirs_ref, high_ref, middle_ref, low_ref, out_ref, matrix, inverse):
    strips = high_ref.shape[0]
    block = out_ref.shape[1]
    rows = mine_ref.shape[1]
    for core in range(CORES):

        @pl.when(place_ref[0] == core)
        def _(core=core):
            for ref, holder in ((mine_ref, core), (theirs_ref, 1 - core)):
                for at, (i, j) in enumerate(share_of(strips, holder)):
                    for r in range(0, LANES, SUBLANES):
                        piece, row = divmod(LANES * at + r, rows)
                        top, left = LANES * i + r, LANES * j
                        matrix[top : top + SUBLANES, left : left + LANES] = ref[piece, row : row + SUBLANES, :]

    inverse_factor(matrix, inverse)
    band = place_ref[1]
    for b in range(strips * LANES // block):

        @pl.when(band == b)
        def _(b=b):
            used = block * (b + 1)
            left = left_parts(
                [
                    jnp.concatenate([ref[s] for s in range(used // LANES)], axis=1)
                    for ref in (high_ref, middle_ref, low_ref)
                ]
            )
            right = right_parts(split(inverse[block * b : used, :used]))
            out_ref[...] = lax.dot_general(
                jnp.concatenate(left, axis=1),
                jnp.concatenate(right, axis=1),
                (((1,), (1,)), ((), ())),
                preferred_element_type=jnp.float32,
            )


def factor_kernel(in_ref, out_ref, matrix):
    matrix[...] = in_ref[...]
    inverse_factor(matrix, out_ref)


def call(kernel, shape, *args, scratch=(), scalars=0):
    specs = [SMEM] * scalars + [VMEM] * (len(args) - scalars)
    return pl.pallas_call(
        kernel,
        out_shape=jax.ShapeDtypeStruct(shape, jnp.float32),
        in_specs=specs,
        out_specs=VMEM,
        scratch_shapes=list(scratch),
        compiler_params=ROOM,
    )(*args)


def transposed(states, potential):
    size_x, size_y, nz, block = states.shape
    domains_y = lax.axis_size("dy")
    domains_x = lax.axis_size("chip") * CORES
    domains = domains_x * domains_y
    bands = lax.axis_size("band")
    cells = size_x * size_y * nz
    columns = size_x * size_y
    area = ("chip", "core", "dy")
    everyone = area + ("band",)
    same_core = ("chip", "dy", "band")
    swap = [(0, 1), (1, 0)]
    place = jnp.stack([lax.axis_index("core"), lax.axis_index("band")]).astype(jnp.int32)

    packed = pl.pallas_call(
        functools.partial(pack_kernel, nz),
        out_shape=jax.ShapeDtypeStruct((domains, columns + size_y, LANES), jnp.float32),
        in_specs=[HBM, HBM],
        out_specs=VMEM,
        scratch_shapes=[
            pltpu.VMEM((block // LANES, cells, LANES), jnp.float32),
            pltpu.VMEM(potential.shape, jnp.float32),
            pltpu.SemaphoreType.DMA((block // LANES + 1,)),
        ],
        compiler_params=ROOM,
    )(*(pltpu.with_memory_space_constraint(v, pltpu.HBM) for v in (states.reshape(cells, block), potential)))
    packed = lax.all_to_all(packed, area, 0, 0, tiled=True)
    grid = (size_x * domains_x, size_y * domains_y, LANES)
    filtered = call(
        functools.partial(filter_kernel, nz, domains_y, size_x, size_y),
        (domains * bands, columns // bands, LANES),
        packed,
        scratch=[
            pltpu.VMEM((2, grid[0] + 2 * WIDTH) + grid[1:], jnp.float32),
            pltpu.VMEM(grid, jnp.float32),
        ],
    )
    filtered = lax.all_to_all(filtered, everyone, 0, 0, tiled=True)
    size = block * bands
    strips = size // LANES
    rows = len(share_of(strips, 0)) * LANES
    holders = domains * bands // CORES
    neighbours = lax.ppermute(filtered, "core", swap)
    split_cells = (strips, cells // bands, LANES)
    own = call(functools.partial(unpack_kernel, nz, bands), split_cells, filtered)
    partial = call(
        functools.partial(gram_kernel, nz, bands),
        (rows, LANES),
        place,
        own,
        neighbours,
        scratch=[pltpu.VMEM(split_cells, jnp.float32)],
        scalars=1,
    )
    first, second = jnp.split(own, 2)
    first = lax.ppermute(first, "band", swap)
    second = lax.ppermute(second, "band", swap)
    partial = lax.all_to_all(partial.reshape(holders, rows // holders, LANES), same_core, 0, 0, tiled=True)
    pieces = call(functools.partial(sum_kernel, float(cells * domains)), partial.shape, partial)
    mine = lax.all_to_all(pieces, same_core, 0, 0, tiled=True)
    theirs = lax.ppermute(mine, "core", swap)
    whole_cells = (strips, cells, LANES)
    parts = pl.pallas_call(
        prepare_kernel,
        out_shape=[jax.ShapeDtypeStruct(whole_cells, jnp.bfloat16)] * 3,
        in_specs=[SMEM] + [VMEM] * 3,
        out_specs=[VMEM] * 3,
        compiler_params=ROOM,
    )(place, own, first, second)
    result = call(
        finish_kernel,
        (cells, block),
        place,
        mine,
        theirs,
        *parts,
        scratch=[pltpu.VMEM((size, size), jnp.float32)] * 2,
        scalars=1,
    )
    return result.reshape(states.shape)


def with_halo(cells, axis, dim, width):
    count = lax.axis_size(axis)
    size = cells.shape[dim]
    head = lax.slice_in_dim(cells, 0, width, axis=dim)
    tail = lax.slice_in_dim(cells, size - width, size, axis=dim)
    before = lax.ppermute(tail, axis, [(i, (i + 1) % count) for i in range(count)])
    after = lax.ppermute(head, axis, [((i + 1) % count, i) for i in range(count)])
    return jnp.concatenate([before, cells, after], axis=dim)


def apply_ham(field, potential):
    padded_x = with_halo(field, "dx", 0, WIDTH)
    padded_y = with_halo(field, "dy", 1, WIDTH)
    size_x = field.shape[0]
    size_y = field.shape[1]
    lap = 3.0 * coeffs[0] * field
    for shift in range(1, WIDTH + 1):
        near = (
            padded_x[WIDTH + shift : WIDTH + shift + size_x]
            + padded_x[WIDTH - shift : WIDTH - shift + size_x]
            + padded_y[:, WIDTH + shift : WIDTH + shift + size_y]
            + padded_y[:, WIDTH - shift : WIDTH - shift + size_y]
        )
        near = near + jnp.roll(field, shift, 2) + jnp.roll(field, -shift, 2)
        lap = lap + coeffs[shift] * near
    return -0.5 * lap + potential[..., None] * field


def haloed(states, potential):
    prev = states
    cur = (apply_ham(states, potential) - centre_value * states) / half_width
    for _ in range(1, DEGREE):
        nxt = 2.0 * (apply_ham(cur, potential) - centre_value * cur) / half_width - prev
        prev, cur = (cur, nxt)
    block = cur.shape[3]
    cells = cur.shape[0] * cur.shape[1] * cur.shape[2]
    local = cur.reshape(cells, block)
    gathered = lax.all_gather(local, "band", axis=1, tiled=True)
    total = cells * lax.axis_size("dx") * lax.axis_size("dy")
    partial = jnp.dot(gathered.T, gathered, precision=HIGHEST, preferred_element_type=jnp.float32) / total
    correlation = lax.psum(partial, ("dx", "dy"))
    size = correlation.shape[0]
    if size % LANES == 0:
        inverse = call(factor_kernel, (size, size), correlation, scratch=[pltpu.VMEM((size, size), jnp.float32)])
    else:
        factor = jnp.linalg.cholesky(correlation)
        inverse = jax.scipy.linalg.solve_triangular(factor, jnp.eye(size, dtype=jnp.float32), lower=True)
    my_rows = lax.dynamic_slice_in_dim(inverse, lax.axis_index("band") * block, block, 0)
    result = jnp.dot(gathered, my_rows.T, precision=HIGHEST, preferred_element_type=jnp.float32)
    return result.reshape(cur.shape)


def solution(mesh):
    domains_x, domains_y, bands = (mesh.shape[name] for name in ("dx", "dy", "band"))
    domains = domains_x * domains_y

    def run(states, potential):
        total_x, total_y, nz, size = states.shape
        size_x, size_y, block = total_x // domains_x, total_y // domains_y, size // bands
        if (
            nz == SUBLANES
            and size_y == SUBLANES
            and nz * size_x <= LANES
            and block * nz == LANES * domains
            and block % LANES == 0
            and bands == 2
            and size_x % bands == 0
            and size // LANES % 2 == 0
            and domains_x % CORES == 0
            and (size // LANES) * (size // LANES + 1) * LANES % (2 * domains * bands * SUBLANES) == 0
            and total_x > 2 * WIDTH
            and total_y > 2 * WIDTH
        ):
            devices = mesh.devices.reshape(domains_x // CORES, CORES, domains_y, bands)
            body, over = transposed, jax.sharding.Mesh(devices, ("chip", "core", "dy", "band"))
            x_axis = ("chip", "core")
        else:
            body, over, x_axis = haloed, mesh, "dx"
        spec = P(x_axis, "dy", None, "band")
        step = jax.shard_map(
            body, mesh=over, in_specs=(spec, P(x_axis, "dy", None)), out_specs=spec, check_vma=False
        )
        return step(states, potential)

    return run
```

```python
import functools

import jax
import jax.numpy as jnp
from jax import lax
from jax.experimental import pallas as pl
from jax.experimental.pallas import tpu as pltpu
from jax.sharding import PartitionSpec as P


DEGREE = 3
LANES = 128
SUBLANES = 8
PANEL = 32
PART = 16
CORES = 2
PRODUCTS = 6

coeffs = (
    -5369.0 / 1800.0,
    12.0 / 7.0,
    -15.0 / 56.0,
    10.0 / 189.0,
    -1.0 / 112.0,
    2.0 / 1925.0,
    -1.0 / 16632.0,
)
WIDTH = len(coeffs) - 1
half_width = 5.0
centre_value = 7.0
VMEM = pl.BlockSpec(memory_space=pltpu.VMEM)
SMEM = pl.BlockSpec(memory_space=pltpu.SMEM)
HBM = pl.BlockSpec(memory_space=pltpu.HBM)
ROOM = pltpu.CompilerParams(vmem_limit_bytes=24 << 20)
HIGHEST = lax.Precision.HIGHEST


def dot(a, b, dims):
    return lax.dot_general(a, b, (dims, ((), ())), precision=HIGHEST, preferred_element_type=jnp.float32)


def split(value):
    high = value.astype(jnp.bfloat16)
    rest = value - high.astype(jnp.float32)
    middle = rest.astype(jnp.bfloat16)
    return high, middle, (rest - middle.astype(jnp.float32)).astype(jnp.bfloat16)


def left_parts(parts):
    high, middle, low = parts
    return [high, high, middle, middle, high, low]


def right_parts(parts):
    high, middle, low = parts
    return [high, middle, high, middle, low, high]


def outer(left, right):
    left = jnp.concatenate(left_parts(left), axis=0)
    right = jnp.concatenate(right_parts(right), axis=0)
    return lax.dot_general(left, right, (((0,), (0,)), ((), ())), preferred_element_type=jnp.float32)


def product(left, right):
    left = jnp.concatenate(left_parts(left), axis=1)
    right = jnp.concatenate(right_parts(right), axis=0)
    return lax.dot_general(left, right, (((1,), (0,)), ((), ())), preferred_element_type=jnp.float32)


def swap_groups(arrays, group):
    count = len(arrays)
    lane = lax.broadcasted_iota(jnp.int32, arrays[0].shape, 1)
    bit = 1
    while bit < count:
        upper = (lane // (group * bit)) % 2 == 1
        out = list(arrays)
        for i in range(count):
            if i & bit == 0:
                low, high = arrays[i], arrays[i | bit]
                out[i] = jnp.where(upper, pltpu.roll(high, group * bit, 1), low)
                out[i | bit] = jnp.where(upper, high, pltpu.roll(low, LANES - group * bit, 1))
        arrays = out
        bit *= 2
    return arrays


def pack_kernel(nz, states_in, potential_in, out_ref, states, potential, arrived):
    halves = range(states.shape[0])
    fetches = [
        pltpu.make_async_copy(states_in.at[:, pl.ds(LANES * half, LANES)], states.at[half], arrived.at[half])
        for half in halves
    ]
    last = pltpu.make_async_copy(potential_in, potential, arrived.at[len(fetches)])
    for fetch in [last] + fetches:
        fetch.start()
    columns = states.shape[1] // nz
    row = lax.broadcasted_iota(jnp.int32, (nz, LANES), 0)
    lane = lax.broadcasted_iota(jnp.int32, (nz, LANES), 1)
    last.wait()
    packed = jnp.zeros((potential.shape[1], LANES), jnp.float32)
    for x in range(potential.shape[0]):
        spread = jnp.where(lane == row + nz * x, 1.0, 0.0)
        packed = packed + dot(potential[x], spread, ((1,), (0,)))
    for i in range(out_ref.shape[0]):
        out_ref[i, columns:, :] = packed
    for half in halves:
        fetches[half].wait()
        arrays = [states[half, pl.ds(z, columns, stride=nz), :] for z in range(nz)]
        for g, value in enumerate(swap_groups(arrays, LANES // nz)):
            out_ref[half * nz + g, :columns, :] = value


def filter_kernel(nz, domains_y, size_x, size_y, in_ref, out_ref, field, potential):
    domains = in_ref.shape[0]
    total_x = size_x * (domains // domains_y)
    total_y = size_y * domains_y
    columns = size_x * size_y
    group = LANES // nz
    shares = out_ref.shape[0] // domains
    share = size_x // shares

    def place(i, x):
        return size_x * (i // domains_y) + x, size_y * (i % domains_y)

    def keep(which, x, rows, value):
        field[which, WIDTH + x, rows, :] = value
        if x < WIDTH:
            field[which, WIDTH + total_x + x, rows, :] = value
        if x >= total_x - WIDTH:
            field[which, WIDTH + x - total_x, rows, :] = value

    packed = in_ref[:, columns:, :].reshape(domains * size_y, LANES)
    source = lax.broadcasted_iota(jnp.int32, (LANES, LANES), 0)
    target = lax.broadcasted_iota(jnp.int32, (LANES, LANES), 1)
    shape = (LANES, LANES * size_x)
    row = lax.broadcasted_iota(jnp.int32, shape, 0)
    lane = lax.broadcasted_iota(jnp.int32, shape, 1)
    spread = jnp.where(row == nz * (lane // LANES) + lane % LANES // group, 1.0, 0.0).astype(jnp.bfloat16)
    spread_all = lax.dot_general(
        jnp.concatenate(split(packed), axis=1),
        jnp.concatenate([spread] * 3, axis=0),
        (((1,), (0,)), ((), ())),
        preferred_element_type=jnp.float32,
    )
    for x in range(size_x):
        values = spread_all[:, LANES * x : LANES * (x + 1)]
        for i in range(domains):
            at_x, at_y = place(i, x)
            rows = slice(at_y, at_y + size_y)
            potential[at_x, rows, :] = values[size_y * i : size_y * (i + 1)] - centre_value
            keep(0, at_x, rows, in_ref[i, size_y * x : size_y * (x + 1), :])

    def ring(distance, size):
        value = jnp.zeros(distance.shape, jnp.float32)
        for k in range(1, WIDTH + 1):
            for shift in (k, -k):
                value = value + jnp.where(distance == shift % size, coeffs[k], 0.0)
        return value

    along_z = ring((source // group - target // group + nz) % nz, nz)
    along_z = jnp.where((source - target) % group == 0, along_z, 0.0)
    along_z = along_z + jnp.where(source == target, 3.0 * coeffs[0], 0.0)
    along_z = jnp.concatenate(right_parts(split(along_z)), axis=0)
    shape = (total_y, PRODUCTS * total_y)
    row = lax.broadcasted_iota(jnp.int32, shape, 0)
    lane = lax.broadcasted_iota(jnp.int32, shape, 1)
    ring_y = ring((row - lane % total_y + total_y) % total_y, total_y)
    along_y = jnp.zeros(shape, jnp.float32)
    for part, value in enumerate(left_parts(split(ring_y))):
        along_y = jnp.where(lane // total_y == part, value.astype(jnp.float32), along_y)
    along_y = along_y.astype(jnp.bfloat16)

    for step in range(DEGREE):
        now, other = step % 2, (step + 1) % 2
        scale = 1.0 / half_width if step == 0 else 2.0 / half_width
        for x in range(total_x):
            value = field[now, WIDTH + x]
            parts = split(value)
            lap = lax.dot_general(
                jnp.concatenate(left_parts(parts), axis=1),
                along_z,
                (((1,), (0,)), ((), ())),
                preferred_element_type=jnp.float32,
            )
            lap = lap + lax.dot_general(
                along_y,
                jnp.concatenate(right_parts(parts), axis=0),
                (((1,), (0,)), ((), ())),
                preferred_element_type=jnp.float32,
            )
            for k in range(1, WIDTH + 1):
                lap = lap + coeffs[k] * (field[now, WIDTH + x + k] + field[now, WIDTH + x - k])
            result = (potential[x] * value - 0.5 * lap) * scale
            if step > 0:
                result = result - field[other, WIDTH + x]
            if step + 1 < DEGREE:
                keep(other, x, slice(None), result)
                continue
            for j in range(domains_y):
                i = x // size_x * domains_y + j
                row = size_y * (x % share)
                out_ref[i * shares + x % size_x // share, row : row + size_y, :] = result[size_y * j : size_y * (j + 1)]


def unpack(nz, bands, in_ref, strip):
    per_band = in_ref.shape[0] // (nz * bands)
    first = nz * (strip % per_band)
    arrays = [in_ref[(first + g) * bands + strip // per_band] for g in range(nz)]
    return swap_groups(arrays, LANES // nz)


def unpack_kernel(nz, bands, in_ref, out_ref):
    for strip in range(out_ref.shape[0]):
        for z, value in enumerate(unpack(nz, bands, in_ref, strip)):
            out_ref[strip, pl.ds(z, in_ref.shape[1], stride=nz), :] = value


def upper_blocks(strips):
    return [(i, j) for i in range(strips) for j in range(i, strips)]


def share_of(strips, core):
    return upper_blocks(strips)[core :: CORES]


def gram_kernel(nz, bands, core_ref, own_ref, other_in, out_ref, other_ref):
    strips = own_ref.shape[0]
    unpack_kernel(nz, bands, other_in, other_ref)
    parts = [split(jnp.concatenate([own_ref[strip], other_ref[strip]], axis=0)) for strip in range(strips)]
    for core in range(CORES):

        @pl.when(core_ref[0] == core)
        def _(core=core):
            pairs = share_of(strips, core)
            for left in sorted({i for i, _ in pairs}):
                spots = [at for at, (i, _) in enumerate(pairs) if i == left]
                right = [jnp.concatenate([parts[pairs[at][1]][p] for at in spots], axis=1) for p in range(3)]
                value = product([part.T for part in parts[left]], right)
                for n, at in enumerate(spots):
                    out_ref[LANES * at : LANES * (at + 1), :] = value[:, LANES * n : LANES * (n + 1)]


def sum_kernel(total, in_ref, out_ref):
    value = in_ref[0]
    for i in range(1, in_ref.shape[0]):
        value = value + in_ref[i]
    value = value / total
    for i in range(out_ref.shape[0]):
        out_ref[i] = value


def spread_row(value, row):
    return jnp.broadcast_to(value[row : row + 1, :], value.shape)


def eliminate(rows, start):
    rows = list(rows)
    tiles = len(rows)
    sublane = lax.broadcasted_iota(jnp.int32, (SUBLANES, LANES), 0)
    at = lax.broadcasted_iota(jnp.int32, (SUBLANES, LANES), 1) - start
    pivots = [jnp.ones((SUBLANES, LANES), jnp.float32) for _ in range(tiles)]
    for first in range(0, PANEL, PART):
        column = {
            (j, t): jnp.broadcast_to(rows[t][:, start + j : start + j + 1], (SUBLANES, LANES))
            for j in range(first, first + PART)
            for t in range(j // SUBLANES, tiles)
        }
        inside = (at >= first) & (at < first + PART)
        for t in range(tiles):
            rows[t] = jnp.where(inside, jnp.where(at == sublane + SUBLANES * t, 1.0, 0.0), rows[t])
        for k in range(first, first + PART):
            tile, row = k // SUBLANES, k % SUBLANES
            pivot = spread_row(column[k, tile], row)
            pivots[tile] = jnp.where(sublane == row, pivot, pivots[tile])
            over = 1.0 / pivot
            factor = {t: column[k, t] * over for t in range(tile, tiles)}
            for j in range(k + 1, first + PART):
                value = spread_row(column[k, j // SUBLANES], j % SUBLANES)
                for t in range(j // SUBLANES, tiles):
                    column[j, t] = column[j, t] - factor[t] * value
            factor[tile] = jnp.where(sublane > row, factor[tile], 0.0)
            value = spread_row(rows[tile], row)
            for t in range(tile, tiles):
                rows[t] = rows[t] - factor[t] * value
    return [rows[t] * lax.rsqrt(pivots[t]) for t in range(tiles)]


def inverse_of_block(value):
    rest = [value[t : t + SUBLANES] for t in range(0, LANES, SUBLANES)]
    lane = lax.broadcasted_iota(jnp.int32, (SUBLANES, LANES), 1)
    out = []
    for start in range(0, LANES, PANEL):
        end = start + PANEL
        rows = eliminate(rest[start // SUBLANES : end // SUBLANES], start)
        out += [jnp.where(lane < end, row, 0.0) for row in rows]
        if end < LANES:
            parts = split(jnp.concatenate(rows, axis=0))
            update = outer(parts, parts)
            for t in range(end // SUBLANES, LANES // SUBLANES):
                old = jnp.where((lane >= start) & (lane < end), 0.0, rest[t])
                rest[t] = old - update[SUBLANES * t : SUBLANES * (t + 1)]
    return jnp.concatenate(out, axis=0)


def beside(left, right):
    return tuple(jnp.concatenate(pair, axis=1) for pair in zip(left, right))


def inverse_factor(matrix, inverse):
    size = matrix.shape[0]
    for low in range(0, size, LANES):
        high = low + LANES
        rows = slice(low, high)
        block = inverse_of_block(matrix[rows, rows])
        left = split(block)
        inverse[rows, rows] = block
        if high < size:
            inverse[rows, high:] = jnp.zeros((LANES, size - high), jnp.float32)
            following = slice(high, high + LANES)
            above = split(product(left, split(matrix[rows, following])))
            matrix[following, following] = matrix[following, following] - outer(above, above)
            if high + LANES < size:
                above = beside(above, split(product(left, split(matrix[rows, high + LANES :]))))
        below = left
        if low:
            value = product(left, split(matrix[rows, :low]))
            inverse[rows, :low] = value
            below = beside(split(value), left)
        for at in range(high, size, LANES):
            mine = tuple(part[:, at - high : at - high + LANES] for part in above)
            target = slice(at, at + LANES)
            update = outer(mine, below)
            if low:
                matrix[target, :low] = matrix[target, :low] - update[:, :low]
            matrix[target, rows] = -update[:, low:]
            first = max(at, high + LANES)
            if first < size:
                update = outer(mine, tuple(part[:, first - high :] for part in above))
                matrix[target, first:] = matrix[target, first:] - update


def prepare_kernel(place_ref, own_ref, other_ref, *out_refs):
    strips, cells, _ = own_ref.shape
    band = place_ref[1]
    for strip in range(strips):
        for share, value in ((band, own_ref[strip]), (1 - band, other_ref[strip])):
            rows = pl.ds(pl.multiple_of(share * cells, cells), cells)
            for ref, part in zip(out_refs, split(value)):
                ref[strip, rows, :] = part


def finish_kernel(place_ref, mine_ref, theirs_ref, high_ref, middle_ref, low_ref, out_ref, matrix, inverse):
    strips = high_ref.shape[0]
    block = out_ref.shape[1]
    rows = mine_ref.shape[1]
    for core in range(CORES):

        @pl.when(place_ref[0] == core)
        def _(core=core):
            for ref, holder in ((mine_ref, core), (theirs_ref, 1 - core)):
                for at, (i, j) in enumerate(share_of(strips, holder)):
                    for r in range(0, LANES, SUBLANES):
                        piece, row = divmod(LANES * at + r, rows)
                        top, left = LANES * i + r, LANES * j
                        matrix[top : top + SUBLANES, left : left + LANES] = ref[piece, row : row + SUBLANES, :]

    inverse_factor(matrix, inverse)
    band = place_ref[1]
    for b in range(strips * LANES // block):

        @pl.when(band == b)
        def _(b=b):
            used = block * (b + 1)
            left = left_parts(
                [
                    jnp.concatenate([ref[s] for s in range(used // LANES)], axis=1)
                    for ref in (high_ref, middle_ref, low_ref)
                ]
            )
            right = right_parts(split(inverse[block * b : used, :used]))
            out_ref[...] = lax.dot_general(
                jnp.concatenate(left, axis=1),
                jnp.concatenate(right, axis=1),
                (((1,), (1,)), ((), ())),
                preferred_element_type=jnp.float32,
            )


def factor_kernel(in_ref, out_ref, matrix):
    matrix[...] = in_ref[...]
    inverse_factor(matrix, out_ref)


def call(kernel, shape, *args, scratch=(), scalars=0):
    specs = [SMEM] * scalars + [VMEM] * (len(args) - scalars)
    return pl.pallas_call(
        kernel,
        out_shape=jax.ShapeDtypeStruct(shape, jnp.float32),
        in_specs=specs,
        out_specs=VMEM,
        scratch_shapes=list(scratch),
        compiler_params=ROOM,
    )(*args)


def transposed(states, potential):
    size_x, size_y, nz, block = states.shape
    domains_y = lax.axis_size("dy")
    domains_x = lax.axis_size("chip") * CORES
    domains = domains_x * domains_y
    bands = lax.axis_size("band")
    cells = size_x * size_y * nz
    columns = size_x * size_y
    area = ("chip", "core", "dy")
    everyone = area + ("band",)
    same_core = ("chip", "dy", "band")
    swap = [(0, 1), (1, 0)]
    place = jnp.stack([lax.axis_index("core"), lax.axis_index("band")]).astype(jnp.int32)

    packed = pl.pallas_call(
        functools.partial(pack_kernel, nz),
        out_shape=jax.ShapeDtypeStruct((domains, columns + size_y, LANES), jnp.float32),
        in_specs=[HBM, HBM],
        out_specs=VMEM,
        scratch_shapes=[
            pltpu.VMEM((block // LANES, cells, LANES), jnp.float32),
            pltpu.VMEM(potential.shape, jnp.float32),
            pltpu.SemaphoreType.DMA((block // LANES + 1,)),
        ],
        compiler_params=ROOM,
    )(*(pltpu.with_memory_space_constraint(v, pltpu.HBM) for v in (states.reshape(cells, block), potential)))
    packed = lax.all_to_all(packed, area, 0, 0, tiled=True)
    grid = (size_x * domains_x, size_y * domains_y, LANES)
    filtered = call(
        functools.partial(filter_kernel, nz, domains_y, size_x, size_y),
        (domains * bands, columns // bands, LANES),
        packed,
        scratch=[
            pltpu.VMEM((2, grid[0] + 2 * WIDTH) + grid[1:], jnp.float32),
            pltpu.VMEM(grid, jnp.float32),
        ],
    )
    filtered = lax.all_to_all(filtered, everyone, 0, 0, tiled=True)
    size = block * bands
    strips = size // LANES
    rows = len(share_of(strips, 0)) * LANES
    holders = domains * bands // CORES
    neighbours = lax.ppermute(filtered, "core", swap)
    split_cells = (strips, cells // bands, LANES)
    own = call(functools.partial(unpack_kernel, nz, bands), split_cells, filtered)
    partial = call(
        functools.partial(gram_kernel, nz, bands),
        (rows, LANES),
        place,
        own,
        neighbours,
        scratch=[pltpu.VMEM(split_cells, jnp.float32)],
        scalars=1,
    )
    other = lax.ppermute(own, "band", swap)
    partial = lax.all_to_all(partial.reshape(holders, rows // holders, LANES), same_core, 0, 0, tiled=True)
    pieces = call(functools.partial(sum_kernel, float(cells * domains)), partial.shape, partial)
    mine = lax.all_to_all(pieces, same_core, 0, 0, tiled=True)
    theirs = lax.ppermute(mine, "core", swap)
    whole_cells = (strips, cells, LANES)
    parts = pl.pallas_call(
        prepare_kernel,
        out_shape=[jax.ShapeDtypeStruct(whole_cells, jnp.bfloat16)] * 3,
        in_specs=[SMEM] + [VMEM] * 2,
        out_specs=[VMEM] * 3,
        compiler_params=ROOM,
    )(place, own, other)
    result = call(
        finish_kernel,
        (cells, block),
        place,
        mine,
        theirs,
        *parts,
        scratch=[pltpu.VMEM((size, size), jnp.float32)] * 2,
        scalars=1,
    )
    return result.reshape(states.shape)


def with_halo(cells, axis, dim, width):
    count = lax.axis_size(axis)
    size = cells.shape[dim]
    head = lax.slice_in_dim(cells, 0, width, axis=dim)
    tail = lax.slice_in_dim(cells, size - width, size, axis=dim)
    before = lax.ppermute(tail, axis, [(i, (i + 1) % count) for i in range(count)])
    after = lax.ppermute(head, axis, [((i + 1) % count, i) for i in range(count)])
    return jnp.concatenate([before, cells, after], axis=dim)


def apply_ham(field, potential):
    padded_x = with_halo(field, "dx", 0, WIDTH)
    padded_y = with_halo(field, "dy", 1, WIDTH)
    size_x = field.shape[0]
    size_y = field.shape[1]
    lap = 3.0 * coeffs[0] * field
    for shift in range(1, WIDTH + 1):
        near = (
            padded_x[WIDTH + shift : WIDTH + shift + size_x]
            + padded_x[WIDTH - shift : WIDTH - shift + size_x]
            + padded_y[:, WIDTH + shift : WIDTH + shift + size_y]
            + padded_y[:, WIDTH - shift : WIDTH - shift + size_y]
        )
        near = near + jnp.roll(field, shift, 2) + jnp.roll(field, -shift, 2)
        lap = lap + coeffs[shift] * near
    return -0.5 * lap + potential[..., None] * field


def haloed(states, potential):
    prev = states
    cur = (apply_ham(states, potential) - centre_value * states) / half_width
    for _ in range(1, DEGREE):
        nxt = 2.0 * (apply_ham(cur, potential) - centre_value * cur) / half_width - prev
        prev, cur = (cur, nxt)
    block = cur.shape[3]
    cells = cur.shape[0] * cur.shape[1] * cur.shape[2]
    local = cur.reshape(cells, block)
    gathered = lax.all_gather(local, "band", axis=1, tiled=True)
    total = cells * lax.axis_size("dx") * lax.axis_size("dy")
    partial = jnp.dot(gathered.T, gathered, precision=HIGHEST, preferred_element_type=jnp.float32) / total
    correlation = lax.psum(partial, ("dx", "dy"))
    size = correlation.shape[0]
    if size % LANES == 0:
        inverse = call(factor_kernel, (size, size), correlation, scratch=[pltpu.VMEM((size, size), jnp.float32)])
    else:
        factor = jnp.linalg.cholesky(correlation)
        inverse = jax.scipy.linalg.solve_triangular(factor, jnp.eye(size, dtype=jnp.float32), lower=True)
    my_rows = lax.dynamic_slice_in_dim(inverse, lax.axis_index("band") * block, block, 0)
    result = jnp.dot(gathered, my_rows.T, precision=HIGHEST, preferred_element_type=jnp.float32)
    return result.reshape(cur.shape)


def solution(mesh):
    domains_x, domains_y, bands = (mesh.shape[name] for name in ("dx", "dy", "band"))
    domains = domains_x * domains_y

    def run(states, potential):
        total_x, total_y, nz, size = states.shape
        size_x, size_y, block = total_x // domains_x, total_y // domains_y, size // bands
        if (
            nz == SUBLANES
            and size_y == SUBLANES
            and nz * size_x <= LANES
            and block * nz == LANES * domains
            and block % LANES == 0
            and bands == 2
            and size_x % bands == 0
            and domains_x % CORES == 0
            and (size // LANES) * (size // LANES + 1) * LANES % (2 * domains * bands * SUBLANES) == 0
            and total_x > 2 * WIDTH
            and total_y > 2 * WIDTH
        ):
            devices = mesh.devices.reshape(domains_x // CORES, CORES, domains_y, bands)
            body, over = transposed, jax.sharding.Mesh(devices, ("chip", "core", "dy", "band"))
            x_axis = ("chip", "core")
        else:
            body, over, x_axis = haloed, mesh, "dx"
        spec = P(x_axis, "dy", None, "band")
        step = jax.shard_map(
            body, mesh=over, in_specs=(spec, P(x_axis, "dy", None)), out_specs=spec, check_vma=False
        )
        return step(states, potential)

    return run
```

```python
import functools

import jax
import jax.numpy as jnp
from jax import lax
from jax.experimental import pallas as pl
from jax.experimental.pallas import tpu as pltpu
from jax.sharding import PartitionSpec as P


DEGREE = 3
LANES = 128
SUBLANES = 8
PANEL = 32
PART = 16
CORES = 2
PRODUCTS = 6
TILE = SUBLANES // 2
WHOLE, HALF, QUADRANTS = range(3)

coeffs = (
    -5369.0 / 1800.0,
    12.0 / 7.0,
    -15.0 / 56.0,
    10.0 / 189.0,
    -1.0 / 112.0,
    2.0 / 1925.0,
    -1.0 / 16632.0,
)
WIDTH = len(coeffs) - 1
half_width = 5.0
centre_value = 7.0
VMEM = pl.BlockSpec(memory_space=pltpu.VMEM)
SMEM = pl.BlockSpec(memory_space=pltpu.SMEM)
HBM = pl.BlockSpec(memory_space=pltpu.HBM)
ROOM = pltpu.CompilerParams(vmem_limit_bytes=24 << 20)
HIGHEST = lax.Precision.HIGHEST


def dot(a, b, dims):
    return lax.dot_general(a, b, (dims, ((), ())), precision=HIGHEST, preferred_element_type=jnp.float32)


def split(value):
    high = value.astype(jnp.bfloat16)
    rest = value - high.astype(jnp.float32)
    middle = rest.astype(jnp.bfloat16)
    return high, middle, (rest - middle.astype(jnp.float32)).astype(jnp.bfloat16)


def left_parts(parts):
    high, middle, low = parts
    return [high, high, middle, middle, high, low]


def right_parts(parts):
    high, middle, low = parts
    return [high, middle, high, middle, low, high]


def outer(left, right):
    left = jnp.concatenate(left_parts(left), axis=0)
    right = jnp.concatenate(right_parts(right), axis=0)
    return lax.dot_general(left, right, (((0,), (0,)), ((), ())), preferred_element_type=jnp.float32)


def product(left, right):
    left = jnp.concatenate(left_parts(left), axis=1)
    right = jnp.concatenate(right_parts(right), axis=0)
    return lax.dot_general(left, right, (((1,), (0,)), ((), ())), preferred_element_type=jnp.float32)


def swap_groups(arrays, group):
    count = len(arrays)
    lane = lax.broadcasted_iota(jnp.int32, arrays[0].shape, 1)
    bit = 1
    while bit < count:
        upper = (lane // (group * bit)) % 2 == 1
        out = list(arrays)
        for i in range(count):
            if i & bit == 0:
                low, high = arrays[i], arrays[i | bit]
                out[i] = jnp.where(upper, pltpu.roll(high, group * bit, 1), low)
                out[i | bit] = jnp.where(upper, high, pltpu.roll(low, LANES - group * bit, 1))
        arrays = out
        bit *= 2
    return arrays


def pack_kernel(nz, states_in, potential_in, out_ref, states, potential, arrived):
    halves = range(states.shape[0])
    fetches = [
        pltpu.make_async_copy(states_in.at[:, pl.ds(LANES * half, LANES)], states.at[half], arrived.at[half])
        for half in halves
    ]
    last = pltpu.make_async_copy(potential_in, potential, arrived.at[len(fetches)])
    for fetch in [last] + fetches:
        fetch.start()
    columns = states.shape[1] // nz
    row = lax.broadcasted_iota(jnp.int32, (nz, LANES), 0)
    lane = lax.broadcasted_iota(jnp.int32, (nz, LANES), 1)
    tiles = columns // TILE
    last.wait()
    packed = jnp.zeros((TILE, LANES), jnp.float32)
    for part in range(2):
        wide = jnp.zeros((potential.shape[1], LANES), jnp.float32)
        for x in range(potential.shape[0]):
            spread = jnp.where(lane == row + nz * x + LANES // 2 * part, 1.0, 0.0)
            wide = wide + dot(potential[x], spread, ((1,), (0,)))
        packed = packed + wide[TILE * part : TILE * (part + 1)]
    for i in range(out_ref.shape[0]):
        out_ref[i, tiles] = packed
    for half in halves:
        fetches[half].wait()
        arrays = [states[half, pl.ds(z, columns, stride=nz), :] for z in range(nz)]
        for g, value in enumerate(swap_groups(arrays, LANES // nz)):
            out_ref[half * nz + g, :tiles] = value.reshape(tiles, TILE, LANES)


def filter_kernel(nz, domains_y, size_x, size_y, in_ref, out_ref, field, potential):
    domains = in_ref.shape[0]
    total_x = size_x * (domains // domains_y)
    total_y = size_y * domains_y
    columns = size_x * size_y
    group = LANES // nz
    shares = out_ref.shape[0] // domains
    share = size_x // shares

    def place(i, x):
        return size_x * (i // domains_y) + x, size_y * (i % domains_y)

    def keep(which, x, rows, value):
        field[which, WIDTH + x, rows, :] = value
        if x < WIDTH:
            field[which, WIDTH + total_x + x, rows, :] = value
        if x >= total_x - WIDTH:
            field[which, WIDTH + x - total_x, rows, :] = value

    packed = in_ref[:, columns // TILE].reshape(domains * TILE, LANES)
    source = lax.broadcasted_iota(jnp.int32, (LANES, LANES), 0)
    target = lax.broadcasted_iota(jnp.int32, (LANES, LANES), 1)
    shape = (LANES, 2 * LANES * size_x)
    row = lax.broadcasted_iota(jnp.int32, shape, 0)
    lane = lax.broadcasted_iota(jnp.int32, shape, 1)
    held_at = nz * (lane // LANES // 2) + LANES // 2 * (lane // LANES % 2) + lane % LANES // group
    spread = jnp.where(row == held_at, 1.0, 0.0).astype(jnp.bfloat16)
    spread_all = lax.dot_general(
        jnp.concatenate(split(packed), axis=1),
        jnp.concatenate([spread] * 3, axis=0),
        (((1,), (0,)), ((), ())),
        preferred_element_type=jnp.float32,
    )
    for x in range(size_x):
        values = [spread_all[:, LANES * at : LANES * (at + 1)] for at in (2 * x, 2 * x + 1)]
        for i in range(domains):
            at_x, at_y = place(i, x)
            rows = slice(at_y, at_y + size_y)
            value = jnp.concatenate([part[TILE * i : TILE * (i + 1)] for part in values], axis=0)
            potential[at_x, rows, :] = value - centre_value
            keep(0, at_x, rows, in_ref[i, 2 * x : 2 * x + 2].reshape(size_y, LANES))

    def ring(distance, size):
        value = jnp.zeros(distance.shape, jnp.float32)
        for k in range(1, WIDTH + 1):
            for shift in (k, -k):
                value = value + jnp.where(distance == shift % size, coeffs[k], 0.0)
        return value

    along_z = ring((source // group - target // group + nz) % nz, nz)
    along_z = jnp.where((source - target) % group == 0, along_z, 0.0)
    along_z = along_z + jnp.where(source == target, 3.0 * coeffs[0], 0.0)
    along_z = jnp.concatenate(right_parts(split(along_z)), axis=0)
    shape = (total_y, PRODUCTS * total_y)
    row = lax.broadcasted_iota(jnp.int32, shape, 0)
    lane = lax.broadcasted_iota(jnp.int32, shape, 1)
    ring_y = ring((row - lane % total_y + total_y) % total_y, total_y)
    along_y = jnp.zeros(shape, jnp.float32)
    for part, value in enumerate(left_parts(split(ring_y))):
        along_y = jnp.where(lane // total_y == part, value.astype(jnp.float32), along_y)
    along_y = along_y.astype(jnp.bfloat16)

    for step in range(DEGREE):
        now, other = step % 2, (step + 1) % 2
        scale = 1.0 / half_width if step == 0 else 2.0 / half_width
        for x in range(total_x):
            value = field[now, WIDTH + x]
            parts = split(value)
            lap = lax.dot_general(
                jnp.concatenate(left_parts(parts), axis=1),
                along_z,
                (((1,), (0,)), ((), ())),
                preferred_element_type=jnp.float32,
            )
            lap = lap + lax.dot_general(
                along_y,
                jnp.concatenate(right_parts(parts), axis=0),
                (((1,), (0,)), ((), ())),
                preferred_element_type=jnp.float32,
            )
            for k in range(1, WIDTH + 1):
                lap = lap + coeffs[k] * (field[now, WIDTH + x + k] + field[now, WIDTH + x - k])
            result = (potential[x] * value - 0.5 * lap) * scale
            if step > 0:
                result = result - field[other, WIDTH + x]
            if step + 1 < DEGREE:
                keep(other, x, slice(None), result)
                continue
            for j in range(domains_y):
                i = x // size_x * domains_y + j
                row = size_y * (x % share)
                out_ref[i * shares + x % size_x // share, row : row + size_y, :] = result[size_y * j : size_y * (j + 1)]


def unpack(nz, bands, in_ref, strip):
    per_band = in_ref.shape[0] // (nz * bands)
    first = nz * (strip % per_band)
    arrays = [in_ref[(first + g) * bands + strip // per_band] for g in range(nz)]
    return swap_groups(arrays, LANES // nz)


def unpack_kernel(nz, bands, in_ref, out_ref):
    for strip in range(out_ref.shape[0]):
        for z, value in enumerate(unpack(nz, bands, in_ref, strip)):
            out_ref[strip, pl.ds(z, in_ref.shape[1], stride=nz), :] = value


def upper_blocks(strips):
    return [(i, j) for i in range(strips) for j in range(i, strips)]


def share_of(strips, core):
    return upper_blocks(strips)[core :: CORES]


def layout(strips, core):
    pairs = share_of(strips, core)
    diagonal = [i for i, j in pairs if i == j]
    return (
        [(WHOLE, LANES, (i, j)) for i, j in pairs if i != j]
        + [(HALF, LANES // 2, (i, i)) for i in diagonal]
        + [(QUADRANTS, LANES // 2, (i, j)) for i, j in zip(diagonal[::2], diagonal[1::2])]
    )


def rows_of(strips, core):
    return sum(rows for _, rows, _ in layout(strips, core))


def gram_kernel(nz, bands, core_ref, own_ref, other_in, out_ref, other_ref):
    strips = own_ref.shape[0]
    unpack_kernel(nz, bands, other_in, other_ref)
    parts = [split(jnp.concatenate([own_ref[strip], other_ref[strip]], axis=0)) for strip in range(strips)]
    for core in range(CORES):

        @pl.when(core_ref[0] == core)
        def _(core=core):
            pairs = share_of(strips, core)
            blocks = {}
            for left in sorted({i for i, _ in pairs}):
                spots = [at for at, (i, _) in enumerate(pairs) if i == left]
                right = [jnp.concatenate([parts[pairs[at][1]][p] for at in spots], axis=1) for p in range(3)]
                value = product([part.T for part in parts[left]], right)
                for n, at in enumerate(spots):
                    blocks[pairs[at]] = value[:, LANES * n : LANES * (n + 1)]
            lane = lax.broadcasted_iota(jnp.int32, (LANES // 2, LANES), 1)
            at = 0
            for kind, rows, (i, j) in layout(strips, core):
                if kind == QUADRANTS:
                    first, second = blocks[i, i][LANES // 2 :], blocks[j, j][LANES // 2 :]
                    value = jnp.where(lane < LANES // 2, pltpu.roll(first, LANES // 2, 1), second)
                else:
                    value = blocks[i, j][:rows]
                out_ref[at : at + rows // TILE] = value.reshape(rows // TILE, TILE, LANES)
                at += rows // TILE


def sum_kernel(total, in_ref, out_ref):
    value = in_ref[0]
    for i in range(1, in_ref.shape[0]):
        value = value + in_ref[i]
    value = value / total
    for i in range(out_ref.shape[0]):
        out_ref[i] = value


def spread_row(value, row):
    return jnp.broadcast_to(value[row : row + 1, :], value.shape)


def eliminate(rows, start):
    rows = list(rows)
    tiles = len(rows)
    sublane = lax.broadcasted_iota(jnp.int32, (SUBLANES, LANES), 0)
    at = lax.broadcasted_iota(jnp.int32, (SUBLANES, LANES), 1) - start
    pivots = [jnp.ones((SUBLANES, LANES), jnp.float32) for _ in range(tiles)]
    for first in range(0, PANEL, PART):
        column = {
            (j, t): jnp.broadcast_to(rows[t][:, start + j : start + j + 1], (SUBLANES, LANES))
            for j in range(first, first + PART)
            for t in range(j // SUBLANES, tiles)
        }
        inside = (at >= first) & (at < first + PART)
        for t in range(tiles):
            rows[t] = jnp.where(inside, jnp.where(at == sublane + SUBLANES * t, 1.0, 0.0), rows[t])
        for k in range(first, first + PART):
            tile, row = k // SUBLANES, k % SUBLANES
            pivot = spread_row(column[k, tile], row)
            pivots[tile] = jnp.where(sublane == row, pivot, pivots[tile])
            over = 1.0 / pivot
            factor = {t: column[k, t] * over for t in range(tile, tiles)}
            for j in range(k + 1, first + PART):
                value = spread_row(column[k, j // SUBLANES], j % SUBLANES)
                for t in range(j // SUBLANES, tiles):
                    column[j, t] = column[j, t] - factor[t] * value
            factor[tile] = jnp.where(sublane > row, factor[tile], 0.0)
            value = spread_row(rows[tile], row)
            for t in range(tile, tiles):
                rows[t] = rows[t] - factor[t] * value
    return [rows[t] * lax.rsqrt(pivots[t]) for t in range(tiles)]


def inverse_of_block(value):
    rest = [value[t : t + SUBLANES] for t in range(0, LANES, SUBLANES)]
    lane = lax.broadcasted_iota(jnp.int32, (SUBLANES, LANES), 1)
    out = []
    for start in range(0, LANES, PANEL):
        end = start + PANEL
        rows = eliminate(rest[start // SUBLANES : end // SUBLANES], start)
        out += [jnp.where(lane < end, row, 0.0) for row in rows]
        if end < LANES:
            parts = split(jnp.concatenate(rows, axis=0))
            update = outer(parts, parts)
            for t in range(end // SUBLANES, LANES // SUBLANES):
                old = jnp.where((lane >= start) & (lane < end), 0.0, rest[t])
                rest[t] = old - update[SUBLANES * t : SUBLANES * (t + 1)]
    return jnp.concatenate(out, axis=0)


def beside(left, right):
    return tuple(jnp.concatenate(pair, axis=1) for pair in zip(left, right))


def inverse_factor(matrix, inverse):
    size = matrix.shape[0]
    for low in range(0, size, LANES):
        high = low + LANES
        rows = slice(low, high)
        block = inverse_of_block(matrix[rows, rows])
        left = split(block)
        inverse[rows, rows] = block
        if high < size:
            inverse[rows, high:] = jnp.zeros((LANES, size - high), jnp.float32)
            following = slice(high, high + LANES)
            above = split(product(left, split(matrix[rows, following])))
            matrix[following, following] = matrix[following, following] - outer(above, above)
            if high + LANES < size:
                above = beside(above, split(product(left, split(matrix[rows, high + LANES :]))))
        below = left
        if low:
            value = product(left, split(matrix[rows, :low]))
            inverse[rows, :low] = value
            below = beside(split(value), left)
        for at in range(high, size, LANES):
            mine = tuple(part[:, at - high : at - high + LANES] for part in above)
            target = slice(at, at + LANES)
            update = outer(mine, below)
            if low:
                matrix[target, :low] = matrix[target, :low] - update[:, :low]
            matrix[target, rows] = -update[:, low:]
            first = max(at, high + LANES)
            if first < size:
                update = outer(mine, tuple(part[:, first - high :] for part in above))
                matrix[target, first:] = matrix[target, first:] - update


def prepare_kernel(place_ref, own_ref, other_ref, *out_refs):
    strips, cells, _ = own_ref.shape
    band = place_ref[1]
    for strip in range(strips):
        for share, value in ((band, own_ref[strip]), (1 - band, other_ref[strip])):
            rows = pl.ds(pl.multiple_of(share * cells, cells), cells)
            for ref, part in zip(out_refs, split(value)):
                ref[strip, rows, :] = part


def finish_kernel(place_ref, mine_ref, theirs_ref, high_ref, middle_ref, low_ref, out_ref, matrix, inverse):
    strips = high_ref.shape[0]
    block = out_ref.shape[1]
    held = mine_ref.shape[1]
    for core in range(CORES):

        @pl.when(place_ref[0] == core)
        def _(core=core):
            for ref, holder in ((mine_ref, core), (theirs_ref, 1 - core)):
                tile = 0
                for kind, rows, (i, j) in layout(strips, holder):
                    for row in range(0, rows, SUBLANES):
                        value = jnp.concatenate([ref[t // held, t % held] for t in (tile, tile + 1)], axis=0)
                        tile += 2
                        targets = [(LANES * i + row, LANES * j, value)]
                        if kind == QUADRANTS:
                            row += LANES // 2
                            targets = [
                                (LANES * i + row, LANES * i, pltpu.roll(value, LANES // 2, 1)),
                                (LANES * j + row, LANES * j, value),
                            ]
                        for top, left, part in targets:
                            matrix[top : top + SUBLANES, left : left + LANES] = part

    inverse_factor(matrix, inverse)
    band = place_ref[1]
    for b in range(strips * LANES // block):

        @pl.when(band == b)
        def _(b=b):
            used = block * (b + 1)
            left = left_parts(
                [
                    jnp.concatenate([ref[s] for s in range(used // LANES)], axis=1)
                    for ref in (high_ref, middle_ref, low_ref)
                ]
            )
            right = right_parts(split(inverse[block * b : used, :used]))
            out_ref[...] = lax.dot_general(
                jnp.concatenate(left, axis=1),
                jnp.concatenate(right, axis=1),
                (((1,), (1,)), ((), ())),
                preferred_element_type=jnp.float32,
            )


def factor_kernel(in_ref, out_ref, matrix):
    matrix[...] = in_ref[...]
    inverse_factor(matrix, out_ref)


def call(kernel, shape, *args, scratch=(), scalars=0):
    specs = [SMEM] * scalars + [VMEM] * (len(args) - scalars)
    return pl.pallas_call(
        kernel,
        out_shape=jax.ShapeDtypeStruct(shape, jnp.float32),
        in_specs=specs,
        out_specs=VMEM,
        scratch_shapes=list(scratch),
        compiler_params=ROOM,
    )(*args)


def transposed(states, potential):
    size_x, size_y, nz, block = states.shape
    domains_y = lax.axis_size("dy")
    domains_x = lax.axis_size("chip") * CORES
    domains = domains_x * domains_y
    bands = lax.axis_size("band")
    cells = size_x * size_y * nz
    columns = size_x * size_y
    area = ("chip", "core", "dy")
    everyone = area + ("band",)
    same_core = ("chip", "dy", "band")
    swap = [(0, 1), (1, 0)]
    place = jnp.stack([lax.axis_index("core"), lax.axis_index("band")]).astype(jnp.int32)

    packed = pl.pallas_call(
        functools.partial(pack_kernel, nz),
        out_shape=jax.ShapeDtypeStruct((domains, columns // TILE + 1, TILE, LANES), jnp.float32),
        in_specs=[HBM, HBM],
        out_specs=VMEM,
        scratch_shapes=[
            pltpu.VMEM((block // LANES, cells, LANES), jnp.float32),
            pltpu.VMEM(potential.shape, jnp.float32),
            pltpu.SemaphoreType.DMA((block // LANES + 1,)),
        ],
        compiler_params=ROOM,
    )(*(pltpu.with_memory_space_constraint(v, pltpu.HBM) for v in (states.reshape(cells, block), potential)))
    packed = lax.all_to_all(packed, area, 0, 0, tiled=True)
    grid = (size_x * domains_x, size_y * domains_y, LANES)
    filtered = call(
        functools.partial(filter_kernel, nz, domains_y, size_x, size_y),
        (domains * bands, columns // bands, LANES),
        packed,
        scratch=[
            pltpu.VMEM((2, grid[0] + 2 * WIDTH) + grid[1:], jnp.float32),
            pltpu.VMEM(grid, jnp.float32),
        ],
    )
    filtered = lax.all_to_all(filtered, everyone, 0, 0, tiled=True)
    size = block * bands
    strips = size // LANES
    rows = rows_of(strips, 0)
    holders = domains * bands // CORES
    neighbours = lax.ppermute(filtered, "core", swap)
    split_cells = (strips, cells // bands, LANES)
    own = call(functools.partial(unpack_kernel, nz, bands), split_cells, filtered)
    partial = call(
        functools.partial(gram_kernel, nz, bands),
        (rows // TILE, TILE, LANES),
        place,
        own,
        neighbours,
        scratch=[pltpu.VMEM(split_cells, jnp.float32)],
        scalars=1,
    )
    other = lax.ppermute(own, "band", swap)
    partial = lax.all_to_all(partial.reshape(holders, rows // holders // TILE, TILE, LANES), same_core, 0, 0, tiled=True)
    pieces = call(functools.partial(sum_kernel, float(cells * domains)), partial.shape, partial)
    mine = lax.all_to_all(pieces, same_core, 0, 0, tiled=True)
    theirs = lax.ppermute(mine, "core", swap)
    whole_cells = (strips, cells, LANES)
    parts = pl.pallas_call(
        prepare_kernel,
        out_shape=[jax.ShapeDtypeStruct(whole_cells, jnp.bfloat16)] * 3,
        in_specs=[SMEM] + [VMEM] * 2,
        out_specs=[VMEM] * 3,
        compiler_params=ROOM,
    )(place, own, other)
    result = call(
        finish_kernel,
        (cells, block),
        place,
        mine,
        theirs,
        *parts,
        scratch=[pltpu.VMEM((size, size), jnp.float32)] * 2,
        scalars=1,
    )
    return result.reshape(states.shape)


def with_halo(cells, axis, dim, width):
    count = lax.axis_size(axis)
    size = cells.shape[dim]
    head = lax.slice_in_dim(cells, 0, width, axis=dim)
    tail = lax.slice_in_dim(cells, size - width, size, axis=dim)
    before = lax.ppermute(tail, axis, [(i, (i + 1) % count) for i in range(count)])
    after = lax.ppermute(head, axis, [((i + 1) % count, i) for i in range(count)])
    return jnp.concatenate([before, cells, after], axis=dim)


def apply_ham(field, potential):
    padded_x = with_halo(field, "dx", 0, WIDTH)
    padded_y = with_halo(field, "dy", 1, WIDTH)
    size_x = field.shape[0]
    size_y = field.shape[1]
    lap = 3.0 * coeffs[0] * field
    for shift in range(1, WIDTH + 1):
        near = (
            padded_x[WIDTH + shift : WIDTH + shift + size_x]
            + padded_x[WIDTH - shift : WIDTH - shift + size_x]
            + padded_y[:, WIDTH + shift : WIDTH + shift + size_y]
            + padded_y[:, WIDTH - shift : WIDTH - shift + size_y]
        )
        near = near + jnp.roll(field, shift, 2) + jnp.roll(field, -shift, 2)
        lap = lap + coeffs[shift] * near
    return -0.5 * lap + potential[..., None] * field


def haloed(states, potential):
    prev = states
    cur = (apply_ham(states, potential) - centre_value * states) / half_width
    for _ in range(1, DEGREE):
        nxt = 2.0 * (apply_ham(cur, potential) - centre_value * cur) / half_width - prev
        prev, cur = (cur, nxt)
    block = cur.shape[3]
    cells = cur.shape[0] * cur.shape[1] * cur.shape[2]
    local = cur.reshape(cells, block)
    gathered = lax.all_gather(local, "band", axis=1, tiled=True)
    total = cells * lax.axis_size("dx") * lax.axis_size("dy")
    partial = jnp.dot(gathered.T, gathered, precision=HIGHEST, preferred_element_type=jnp.float32) / total
    correlation = lax.psum(partial, ("dx", "dy"))
    size = correlation.shape[0]
    if size % LANES == 0:
        inverse = call(factor_kernel, (size, size), correlation, scratch=[pltpu.VMEM((size, size), jnp.float32)])
    else:
        factor = jnp.linalg.cholesky(correlation)
        inverse = jax.scipy.linalg.solve_triangular(factor, jnp.eye(size, dtype=jnp.float32), lower=True)
    my_rows = lax.dynamic_slice_in_dim(inverse, lax.axis_index("band") * block, block, 0)
    result = jnp.dot(gathered, my_rows.T, precision=HIGHEST, preferred_element_type=jnp.float32)
    return result.reshape(cur.shape)


def fits_cores(strips, devices):
    rows = {rows_of(strips, core) for core in range(CORES)}
    even = all(sum(i == j for i, j in share_of(strips, core)) % 2 == 0 for core in range(CORES))
    return even and len(rows) == 1 and rows.pop() % (devices // CORES * TILE) == 0


def solution(mesh):
    domains_x, domains_y, bands = (mesh.shape[name] for name in ("dx", "dy", "band"))
    domains = domains_x * domains_y

    def run(states, potential):
        total_x, total_y, nz, size = states.shape
        size_x, size_y, block = total_x // domains_x, total_y // domains_y, size // bands
        if (
            nz == SUBLANES
            and size_y == SUBLANES
            and 2 * nz * size_x <= LANES
            and block * nz == LANES * domains
            and block % LANES == 0
            and bands == 2
            and size_x % bands == 0
            and domains_x % CORES == 0
            and fits_cores(size // LANES, domains * bands)
            and total_x > 2 * WIDTH
            and total_y > 2 * WIDTH
        ):
            devices = mesh.devices.reshape(domains_x // CORES, CORES, domains_y, bands)
            body, over = transposed, jax.sharding.Mesh(devices, ("chip", "core", "dy", "band"))
            x_axis = ("chip", "core")
        else:
            body, over, x_axis = haloed, mesh, "dx"
        spec = P(x_axis, "dy", None, "band")
        step = jax.shard_map(
            body, mesh=over, in_specs=(spec, P(x_axis, "dy", None)), out_specs=spec, check_vma=False
        )
        return step(states, potential)

    return run
```

```python
import functools

import jax
import jax.numpy as jnp
from jax import lax
from jax.experimental import pallas as pl
from jax.experimental.pallas import tpu as pltpu
from jax.sharding import PartitionSpec as P


DEGREE = 3
LANES = 128
SUBLANES = 8
PANEL = 32
PART = 16
CORES = 2
PRODUCTS = 6
TILE = SUBLANES // 2
WHOLE, HALF, QUADRANTS = range(3)

coeffs = (
    -5369.0 / 1800.0,
    12.0 / 7.0,
    -15.0 / 56.0,
    10.0 / 189.0,
    -1.0 / 112.0,
    2.0 / 1925.0,
    -1.0 / 16632.0,
)
WIDTH = len(coeffs) - 1
half_width = 5.0
centre_value = 7.0
VMEM = pl.BlockSpec(memory_space=pltpu.VMEM)
SMEM = pl.BlockSpec(memory_space=pltpu.SMEM)
HBM = pl.BlockSpec(memory_space=pltpu.HBM)
ROOM = pltpu.CompilerParams(vmem_limit_bytes=24 << 20)
HIGHEST = lax.Precision.HIGHEST


def dot(a, b, dims):
    return lax.dot_general(a, b, (dims, ((), ())), precision=HIGHEST, preferred_element_type=jnp.float32)


def split(value):
    high = value.astype(jnp.bfloat16)
    rest = value - high.astype(jnp.float32)
    middle = rest.astype(jnp.bfloat16)
    return high, middle, (rest - middle.astype(jnp.float32)).astype(jnp.bfloat16)


def left_parts(parts):
    high, middle, low = parts
    return [high, high, middle, middle, high, low]


def right_parts(parts):
    high, middle, low = parts
    return [high, middle, high, middle, low, high]


def outer(left, right):
    left = jnp.concatenate(left_parts(left), axis=0)
    right = jnp.concatenate(right_parts(right), axis=0)
    return lax.dot_general(left, right, (((0,), (0,)), ((), ())), preferred_element_type=jnp.float32)


def product(left, right):
    left = jnp.concatenate(left_parts(left), axis=1)
    right = jnp.concatenate(right_parts(right), axis=0)
    return lax.dot_general(left, right, (((1,), (0,)), ((), ())), preferred_element_type=jnp.float32)


def swap_groups(arrays, group):
    count = len(arrays)
    lane = lax.broadcasted_iota(jnp.int32, arrays[0].shape, 1)
    bit = 1
    while bit < count:
        upper = (lane // (group * bit)) % 2 == 1
        out = list(arrays)
        for i in range(count):
            if i & bit == 0:
                low, high = arrays[i], arrays[i | bit]
                out[i] = jnp.where(upper, pltpu.roll(high, group * bit, 1), low)
                out[i | bit] = jnp.where(upper, high, pltpu.roll(low, LANES - group * bit, 1))
        arrays = out
        bit *= 2
    return arrays


def pack_kernel(nz, states_in, potential_in, out_ref, states, potential, arrived):
    halves = range(states.shape[0])
    fetches = [
        pltpu.make_async_copy(states_in.at[:, pl.ds(LANES * half, LANES)], states.at[half], arrived.at[half])
        for half in halves
    ]
    last = pltpu.make_async_copy(potential_in, potential, arrived.at[len(fetches)])
    for fetch in [last] + fetches:
        fetch.start()
    columns = states.shape[1] // nz
    row = lax.broadcasted_iota(jnp.int32, (nz, LANES), 0)
    lane = lax.broadcasted_iota(jnp.int32, (nz, LANES), 1)
    tiles = columns // TILE
    last.wait()
    packed = jnp.zeros((TILE, LANES), jnp.float32)
    for part in range(2):
        wide = jnp.zeros((potential.shape[1], LANES), jnp.float32)
        for x in range(potential.shape[0]):
            spread = jnp.where(lane == row + nz * x + LANES // 2 * part, 1.0, 0.0)
            wide = wide + dot(potential[x], spread, ((1,), (0,)))
        packed = packed + wide[TILE * part : TILE * (part + 1)]
    for i in range(out_ref.shape[0]):
        out_ref[i, tiles] = packed
    for half in halves:
        fetches[half].wait()
        arrays = [states[half, pl.ds(z, columns, stride=nz), :] for z in range(nz)]
        for g, value in enumerate(swap_groups(arrays, LANES // nz)):
            out_ref[half * nz + g, :tiles] = value.reshape(tiles, TILE, LANES)


def filter_kernel(nz, domains_y, size_x, size_y, in_ref, out_ref, field, potential):
    domains = in_ref.shape[0]
    total_x = size_x * (domains // domains_y)
    total_y = size_y * domains_y
    columns = size_x * size_y
    group = LANES // nz
    shares = out_ref.shape[0] // domains
    share = size_x // shares

    def place(i, x):
        return size_x * (i // domains_y) + x, size_y * (i % domains_y)

    def keep(which, x, rows, value):
        field[which, WIDTH + x, rows, :] = value
        if x < WIDTH:
            field[which, WIDTH + total_x + x, rows, :] = value
        if x >= total_x - WIDTH:
            field[which, WIDTH + x - total_x, rows, :] = value

    packed = in_ref[:, columns // TILE].reshape(domains * TILE, LANES)
    source = lax.broadcasted_iota(jnp.int32, (LANES, LANES), 0)
    target = lax.broadcasted_iota(jnp.int32, (LANES, LANES), 1)
    shape = (LANES, 2 * LANES * size_x)
    row = lax.broadcasted_iota(jnp.int32, shape, 0)
    lane = lax.broadcasted_iota(jnp.int32, shape, 1)
    held_at = nz * (lane // LANES // 2) + LANES // 2 * (lane // LANES % 2) + lane % LANES // group
    spread = jnp.where(row == held_at, 1.0, 0.0).astype(jnp.bfloat16)
    spread_all = lax.dot_general(
        jnp.concatenate(split(packed), axis=1),
        jnp.concatenate([spread] * 3, axis=0),
        (((1,), (0,)), ((), ())),
        preferred_element_type=jnp.float32,
    )
    for x in range(size_x):
        values = [spread_all[:, LANES * at : LANES * (at + 1)] for at in (2 * x, 2 * x + 1)]
        for i in range(domains):
            at_x, at_y = place(i, x)
            rows = slice(at_y, at_y + size_y)
            value = jnp.concatenate([part[TILE * i : TILE * (i + 1)] for part in values], axis=0)
            potential[at_x, rows, :] = value - centre_value
            keep(0, at_x, rows, in_ref[i, 2 * x : 2 * x + 2].reshape(size_y, LANES))

    def ring(distance, size):
        value = jnp.zeros(distance.shape, jnp.float32)
        for k in range(1, WIDTH + 1):
            for shift in (k, -k):
                value = value + jnp.where(distance == shift % size, coeffs[k], 0.0)
        return value

    along_z = ring((source // group - target // group + nz) % nz, nz)
    along_z = jnp.where((source - target) % group == 0, along_z, 0.0)
    along_z = along_z + jnp.where(source == target, 3.0 * coeffs[0], 0.0)
    along_z = jnp.concatenate(right_parts(split(along_z)), axis=0)
    shape = (total_y, PRODUCTS * total_y)
    row = lax.broadcasted_iota(jnp.int32, shape, 0)
    lane = lax.broadcasted_iota(jnp.int32, shape, 1)
    ring_y = ring((row - lane % total_y + total_y) % total_y, total_y)
    along_y = jnp.zeros(shape, jnp.float32)
    for part, value in enumerate(left_parts(split(ring_y))):
        along_y = jnp.where(lane // total_y == part, value.astype(jnp.float32), along_y)
    along_y = along_y.astype(jnp.bfloat16)

    for step in range(DEGREE):
        now, other = step % 2, (step + 1) % 2
        scale = 1.0 / half_width if step == 0 else 2.0 / half_width
        for x in range(total_x):
            value = field[now, WIDTH + x]
            parts = split(value)
            lap = lax.dot_general(
                jnp.concatenate(left_parts(parts), axis=1),
                along_z,
                (((1,), (0,)), ((), ())),
                preferred_element_type=jnp.float32,
            )
            lap = lap + lax.dot_general(
                along_y,
                jnp.concatenate(right_parts(parts), axis=0),
                (((1,), (0,)), ((), ())),
                preferred_element_type=jnp.float32,
            )
            for k in range(1, WIDTH + 1):
                lap = lap + coeffs[k] * (field[now, WIDTH + x + k] + field[now, WIDTH + x - k])
            result = (potential[x] * value - 0.5 * lap) * scale
            if step > 0:
                result = result - field[other, WIDTH + x]
            if step + 1 < DEGREE:
                keep(other, x, slice(None), result)
                continue
            for j in range(domains_y):
                i = x // size_x * domains_y + j
                row = size_y * (x % share)
                out_ref[i * shares + x % size_x // share, row : row + size_y, :] = result[size_y * j : size_y * (j + 1)]


def unpack(nz, bands, in_ref, strip):
    per_band = in_ref.shape[0] // (nz * bands)
    first = nz * (strip % per_band)
    arrays = [in_ref[(first + g) * bands + strip // per_band] for g in range(nz)]
    return swap_groups(arrays, LANES // nz)


def unpack_kernel(nz, bands, in_ref, out_ref):
    for strip in range(out_ref.shape[0]):
        for z, value in enumerate(unpack(nz, bands, in_ref, strip)):
            out_ref[strip, pl.ds(z, in_ref.shape[1], stride=nz), :] = value


def upper_blocks(strips):
    return [(i, j) for i in range(strips) for j in range(i, strips)]


def share_of(strips, core):
    return upper_blocks(strips)[core :: CORES]


def layout(strips, core):
    pairs = share_of(strips, core)
    diagonal = [i for i, j in pairs if i == j]
    return (
        [(WHOLE, LANES, (i, j)) for i, j in pairs if i != j]
        + [(HALF, LANES // 2, (i, i)) for i in diagonal]
        + [(QUADRANTS, LANES // 2, (i, j)) for i, j in zip(diagonal[::2], diagonal[1::2])]
    )


def rows_of(strips, core):
    return sum(rows for _, rows, _ in layout(strips, core))


def products(cells_ref, core):
    strips = cells_ref.shape[0]
    pairs = share_of(strips, core)
    used = sorted({strip for pair in pairs for strip in pair})
    parts = {strip: split(cells_ref[strip]) for strip in used}
    blocks = {}
    for left in sorted({i for i, _ in pairs}):
        rights = [j for i, j in pairs if i == left]
        value = product([part.T for part in parts[left]], [jnp.concatenate([parts[j][p] for j in rights], axis=1) for p in range(3)])
        for n, j in enumerate(rights):
            blocks[left, j] = value[:, LANES * n : LANES * (n + 1)]
    return blocks


def own_kernel(nz, bands, core_ref, in_ref, cells_ref, blocks_ref):
    unpack_kernel(nz, bands, in_ref, cells_ref)
    for core in range(CORES):

        @pl.when(core_ref[0] == core)
        def _(core=core):
            for at, value in enumerate(products(cells_ref, core).values()):
                blocks_ref[at] = value


def gram_kernel(nz, bands, core_ref, blocks_ref, in_ref, out_ref, cells_ref):
    strips = cells_ref.shape[0]
    unpack_kernel(nz, bands, in_ref, cells_ref)
    for core in range(CORES):

        @pl.when(core_ref[0] == core)
        def _(core=core):
            added = products(cells_ref, core)
            blocks = {pair: value + blocks_ref[at] for at, (pair, value) in enumerate(added.items())}
            lane = lax.broadcasted_iota(jnp.int32, (LANES // 2, LANES), 1)
            at = 0
            for kind, rows, (i, j) in layout(strips, core):
                if kind == QUADRANTS:
                    first, second = blocks[i, i][LANES // 2 :], blocks[j, j][LANES // 2 :]
                    value = jnp.where(lane < LANES // 2, pltpu.roll(first, LANES // 2, 1), second)
                else:
                    value = blocks[i, j][:rows]
                out_ref[at : at + rows // TILE] = value.reshape(rows // TILE, TILE, LANES)
                at += rows // TILE


def sum_kernel(total, in_ref, out_ref):
    value = in_ref[0]
    for i in range(1, in_ref.shape[0]):
        value = value + in_ref[i]
    value = value / total
    for i in range(out_ref.shape[0]):
        out_ref[i] = value


def spread_row(value, row):
    return jnp.broadcast_to(value[row : row + 1, :], value.shape)


def eliminate(rows, start):
    rows = list(rows)
    tiles = len(rows)
    sublane = lax.broadcasted_iota(jnp.int32, (SUBLANES, LANES), 0)
    at = lax.broadcasted_iota(jnp.int32, (SUBLANES, LANES), 1) - start
    pivots = [jnp.ones((SUBLANES, LANES), jnp.float32) for _ in range(tiles)]
    for first in range(0, PANEL, PART):
        column = {
            (j, t): jnp.broadcast_to(rows[t][:, start + j : start + j + 1], (SUBLANES, LANES))
            for j in range(first, first + PART)
            for t in range(j // SUBLANES, tiles)
        }
        inside = (at >= first) & (at < first + PART)
        for t in range(tiles):
            rows[t] = jnp.where(inside, jnp.where(at == sublane + SUBLANES * t, 1.0, 0.0), rows[t])
        for k in range(first, first + PART):
            tile, row = k // SUBLANES, k % SUBLANES
            pivot = spread_row(column[k, tile], row)
            pivots[tile] = jnp.where(sublane == row, pivot, pivots[tile])
            over = 1.0 / pivot
            factor = {t: column[k, t] * over for t in range(tile, tiles)}
            for j in range(k + 1, first + PART):
                value = spread_row(column[k, j // SUBLANES], j % SUBLANES)
                for t in range(j // SUBLANES, tiles):
                    column[j, t] = column[j, t] - factor[t] * value
            factor[tile] = jnp.where(sublane > row, factor[tile], 0.0)
            value = spread_row(rows[tile], row)
            for t in range(tile, tiles):
                rows[t] = rows[t] - factor[t] * value
    return [rows[t] * lax.rsqrt(pivots[t]) for t in range(tiles)]


def inverse_of_block(value):
    rest = [value[t : t + SUBLANES] for t in range(0, LANES, SUBLANES)]
    lane = lax.broadcasted_iota(jnp.int32, (SUBLANES, LANES), 1)
    out = []
    for start in range(0, LANES, PANEL):
        end = start + PANEL
        rows = eliminate(rest[start // SUBLANES : end // SUBLANES], start)
        out += [jnp.where(lane < end, row, 0.0) for row in rows]
        if end < LANES:
            parts = split(jnp.concatenate(rows, axis=0))
            update = outer(parts, parts)
            for t in range(end // SUBLANES, LANES // SUBLANES):
                old = jnp.where((lane >= start) & (lane < end), 0.0, rest[t])
                rest[t] = old - update[SUBLANES * t : SUBLANES * (t + 1)]
    return jnp.concatenate(out, axis=0)


def beside(left, right):
    return tuple(jnp.concatenate(pair, axis=1) for pair in zip(left, right))


def inverse_factor(matrix, inverse):
    size = matrix.shape[0]
    for low in range(0, size, LANES):
        high = low + LANES
        rows = slice(low, high)
        block = inverse_of_block(matrix[rows, rows])
        left = split(block)
        inverse[rows, rows] = block
        if high < size:
            inverse[rows, high:] = jnp.zeros((LANES, size - high), jnp.float32)
            following = slice(high, high + LANES)
            above = split(product(left, split(matrix[rows, following])))
            matrix[following, following] = matrix[following, following] - outer(above, above)
            if high + LANES < size:
                above = beside(above, split(product(left, split(matrix[rows, high + LANES :]))))
        below = left
        if low:
            value = product(left, split(matrix[rows, :low]))
            inverse[rows, :low] = value
            below = beside(split(value), left)
        for at in range(high, size, LANES):
            mine = tuple(part[:, at - high : at - high + LANES] for part in above)
            target = slice(at, at + LANES)
            update = outer(mine, below)
            if low:
                matrix[target, :low] = matrix[target, :low] - update[:, :low]
            matrix[target, rows] = -update[:, low:]
            first = max(at, high + LANES)
            if first < size:
                update = outer(mine, tuple(part[:, first - high :] for part in above))
                matrix[target, first:] = matrix[target, first:] - update


def prepare_kernel(place_ref, own_ref, other_ref, *out_refs):
    strips, cells, _ = own_ref.shape
    band = place_ref[1]
    for strip in range(strips):
        for share, value in ((band, own_ref[strip]), (1 - band, other_ref[strip])):
            rows = pl.ds(pl.multiple_of(share * cells, cells), cells)
            for ref, part in zip(out_refs, split(value)):
                ref[strip, rows, :] = part


def finish_kernel(place_ref, mine_ref, theirs_ref, high_ref, middle_ref, low_ref, out_ref, matrix, inverse):
    strips = high_ref.shape[0]
    block = out_ref.shape[1]
    held = mine_ref.shape[1]
    for core in range(CORES):

        @pl.when(place_ref[0] == core)
        def _(core=core):
            for ref, holder in ((mine_ref, core), (theirs_ref, 1 - core)):
                tile = 0
                for kind, rows, (i, j) in layout(strips, holder):
                    for row in range(0, rows, SUBLANES):
                        value = jnp.concatenate([ref[t // held, t % held] for t in (tile, tile + 1)], axis=0)
                        tile += 2
                        targets = [(LANES * i + row, LANES * j, value)]
                        if kind == QUADRANTS:
                            row += LANES // 2
                            targets = [
                                (LANES * i + row, LANES * i, pltpu.roll(value, LANES // 2, 1)),
                                (LANES * j + row, LANES * j, value),
                            ]
                        for top, left, part in targets:
                            matrix[top : top + SUBLANES, left : left + LANES] = part

    inverse_factor(matrix, inverse)
    band = place_ref[1]
    for b in range(strips * LANES // block):

        @pl.when(band == b)
        def _(b=b):
            used = block * (b + 1)
            left = left_parts(
                [
                    jnp.concatenate([ref[s] for s in range(used // LANES)], axis=1)
                    for ref in (high_ref, middle_ref, low_ref)
                ]
            )
            right = right_parts(split(inverse[block * b : used, :used]))
            out_ref[...] = lax.dot_general(
                jnp.concatenate(left, axis=1),
                jnp.concatenate(right, axis=1),
                (((1,), (1,)), ((), ())),
                preferred_element_type=jnp.float32,
            )


def factor_kernel(in_ref, out_ref, matrix):
    matrix[...] = in_ref[...]
    inverse_factor(matrix, out_ref)


def call(kernel, shape, *args, scratch=(), scalars=0):
    specs = [SMEM] * scalars + [VMEM] * (len(args) - scalars)
    return pl.pallas_call(
        kernel,
        out_shape=jax.ShapeDtypeStruct(shape, jnp.float32),
        in_specs=specs,
        out_specs=VMEM,
        scratch_shapes=list(scratch),
        compiler_params=ROOM,
    )(*args)


def transposed(states, potential):
    size_x, size_y, nz, block = states.shape
    domains_y = lax.axis_size("dy")
    domains_x = lax.axis_size("chip") * CORES
    domains = domains_x * domains_y
    bands = lax.axis_size("band")
    cells = size_x * size_y * nz
    columns = size_x * size_y
    area = ("chip", "core", "dy")
    everyone = area + ("band",)
    same_core = ("chip", "dy", "band")
    swap = [(0, 1), (1, 0)]
    place = jnp.stack([lax.axis_index("core"), lax.axis_index("band")]).astype(jnp.int32)

    packed = pl.pallas_call(
        functools.partial(pack_kernel, nz),
        out_shape=jax.ShapeDtypeStruct((domains, columns // TILE + 1, TILE, LANES), jnp.float32),
        in_specs=[HBM, HBM],
        out_specs=VMEM,
        scratch_shapes=[
            pltpu.VMEM((block // LANES, cells, LANES), jnp.float32),
            pltpu.VMEM(potential.shape, jnp.float32),
            pltpu.SemaphoreType.DMA((block // LANES + 1,)),
        ],
        compiler_params=ROOM,
    )(*(pltpu.with_memory_space_constraint(v, pltpu.HBM) for v in (states.reshape(cells, block), potential)))
    packed = lax.all_to_all(packed, area, 0, 0, tiled=True)
    grid = (size_x * domains_x, size_y * domains_y, LANES)
    filtered = call(
        functools.partial(filter_kernel, nz, domains_y, size_x, size_y),
        (domains * bands, columns // bands, LANES),
        packed,
        scratch=[
            pltpu.VMEM((2, grid[0] + 2 * WIDTH) + grid[1:], jnp.float32),
            pltpu.VMEM(grid, jnp.float32),
        ],
    )
    filtered = lax.all_to_all(filtered, everyone, 0, 0, tiled=True)
    size = block * bands
    strips = size // LANES
    rows = rows_of(strips, 0)
    holders = domains * bands // CORES
    neighbours = lax.ppermute(filtered, "core", swap)
    split_cells = (strips, cells // bands, LANES)
    own, blocks = pl.pallas_call(
        functools.partial(own_kernel, nz, bands),
        out_shape=[
            jax.ShapeDtypeStruct(split_cells, jnp.float32),
            jax.ShapeDtypeStruct((len(share_of(strips, 0)), LANES, LANES), jnp.float32),
        ],
        in_specs=[SMEM, VMEM],
        out_specs=[VMEM, VMEM],
        compiler_params=ROOM,
    )(place, filtered)
    partial = call(
        functools.partial(gram_kernel, nz, bands),
        (rows // TILE, TILE, LANES),
        place,
        blocks,
        neighbours,
        scratch=[pltpu.VMEM(split_cells, jnp.float32)],
        scalars=1,
    )
    other = lax.ppermute(own, "band", swap)
    partial = lax.all_to_all(partial.reshape(holders, rows // holders // TILE, TILE, LANES), same_core, 0, 0, tiled=True)
    pieces = call(functools.partial(sum_kernel, float(cells * domains)), partial.shape, partial)
    mine = lax.all_to_all(pieces, same_core, 0, 0, tiled=True)
    theirs = lax.ppermute(mine, "core", swap)
    whole_cells = (strips, cells, LANES)
    parts = pl.pallas_call(
        prepare_kernel,
        out_shape=[jax.ShapeDtypeStruct(whole_cells, jnp.bfloat16)] * 3,
        in_specs=[SMEM] + [VMEM] * 2,
        out_specs=[VMEM] * 3,
        compiler_params=ROOM,
    )(place, own, other)
    result = call(
        finish_kernel,
        (cells, block),
        place,
        mine,
        theirs,
        *parts,
        scratch=[pltpu.VMEM((size, size), jnp.float32)] * 2,
        scalars=1,
    )
    return result.reshape(states.shape)


def with_halo(cells, axis, dim, width):
    count = lax.axis_size(axis)
    size = cells.shape[dim]
    head = lax.slice_in_dim(cells, 0, width, axis=dim)
    tail = lax.slice_in_dim(cells, size - width, size, axis=dim)
    before = lax.ppermute(tail, axis, [(i, (i + 1) % count) for i in range(count)])
    after = lax.ppermute(head, axis, [((i + 1) % count, i) for i in range(count)])
    return jnp.concatenate([before, cells, after], axis=dim)


def apply_ham(field, potential):
    padded_x = with_halo(field, "dx", 0, WIDTH)
    padded_y = with_halo(field, "dy", 1, WIDTH)
    size_x = field.shape[0]
    size_y = field.shape[1]
    lap = 3.0 * coeffs[0] * field
    for shift in range(1, WIDTH + 1):
        near = (
            padded_x[WIDTH + shift : WIDTH + shift + size_x]
            + padded_x[WIDTH - shift : WIDTH - shift + size_x]
            + padded_y[:, WIDTH + shift : WIDTH + shift + size_y]
            + padded_y[:, WIDTH - shift : WIDTH - shift + size_y]
        )
        near = near + jnp.roll(field, shift, 2) + jnp.roll(field, -shift, 2)
        lap = lap + coeffs[shift] * near
    return -0.5 * lap + potential[..., None] * field


def haloed(states, potential):
    prev = states
    cur = (apply_ham(states, potential) - centre_value * states) / half_width
    for _ in range(1, DEGREE):
        nxt = 2.0 * (apply_ham(cur, potential) - centre_value * cur) / half_width - prev
        prev, cur = (cur, nxt)
    block = cur.shape[3]
    cells = cur.shape[0] * cur.shape[1] * cur.shape[2]
    local = cur.reshape(cells, block)
    gathered = lax.all_gather(local, "band", axis=1, tiled=True)
    total = cells * lax.axis_size("dx") * lax.axis_size("dy")
    partial = jnp.dot(gathered.T, gathered, precision=HIGHEST, preferred_element_type=jnp.float32) / total
    correlation = lax.psum(partial, ("dx", "dy"))
    size = correlation.shape[0]
    if size % LANES == 0:
        inverse = call(factor_kernel, (size, size), correlation, scratch=[pltpu.VMEM((size, size), jnp.float32)])
    else:
        factor = jnp.linalg.cholesky(correlation)
        inverse = jax.scipy.linalg.solve_triangular(factor, jnp.eye(size, dtype=jnp.float32), lower=True)
    my_rows = lax.dynamic_slice_in_dim(inverse, lax.axis_index("band") * block, block, 0)
    result = jnp.dot(gathered, my_rows.T, precision=HIGHEST, preferred_element_type=jnp.float32)
    return result.reshape(cur.shape)


def fits_cores(strips, devices):
    rows = {rows_of(strips, core) for core in range(CORES)}
    even = all(sum(i == j for i, j in share_of(strips, core)) % 2 == 0 for core in range(CORES))
    return even and len(rows) == 1 and rows.pop() % (devices // CORES * TILE) == 0


def solution(mesh):
    domains_x, domains_y, bands = (mesh.shape[name] for name in ("dx", "dy", "band"))
    domains = domains_x * domains_y

    def run(states, potential):
        total_x, total_y, nz, size = states.shape
        size_x, size_y, block = total_x // domains_x, total_y // domains_y, size // bands
        if (
            nz == SUBLANES
            and size_y == SUBLANES
            and 2 * nz * size_x <= LANES
            and block * nz == LANES * domains
            and block % LANES == 0
            and bands == 2
            and size_x % bands == 0
            and domains_x % CORES == 0
            and fits_cores(size // LANES, domains * bands)
            and total_x > 2 * WIDTH
            and total_y > 2 * WIDTH
        ):
            devices = mesh.devices.reshape(domains_x // CORES, CORES, domains_y, bands)
            body, over = transposed, jax.sharding.Mesh(devices, ("chip", "core", "dy", "band"))
            x_axis = ("chip", "core")
        else:
            body, over, x_axis = haloed, mesh, "dx"
        spec = P(x_axis, "dy", None, "band")
        step = jax.shard_map(
            body, mesh=over, in_specs=(spec, P(x_axis, "dy", None)), out_specs=spec, check_vma=False
        )
        return step(states, potential)

    return run
```

```python
import functools
import math

import jax
import jax.numpy as jnp
from jax import lax
from jax.experimental import pallas as pl
from jax.experimental.pallas import tpu as pltpu
from jax.sharding import PartitionSpec as P


DEGREE = 3
LANES = 128
SUBLANES = 8
PANEL = 32
PART = 16
CORES = 2
PRODUCTS = 6
TILE = SUBLANES // 2
WHOLE, HALF, QUADRANTS = range(3)

coeffs = (
    -5369.0 / 1800.0,
    12.0 / 7.0,
    -15.0 / 56.0,
    10.0 / 189.0,
    -1.0 / 112.0,
    2.0 / 1925.0,
    -1.0 / 16632.0,
)
WIDTH = len(coeffs) - 1
half_width = 5.0
centre_value = 7.0
VMEM = pl.BlockSpec(memory_space=pltpu.VMEM)
SMEM = pl.BlockSpec(memory_space=pltpu.SMEM)
HBM = pl.BlockSpec(memory_space=pltpu.HBM)
ROOM = pltpu.CompilerParams(vmem_limit_bytes=24 << 20)
HIGHEST = lax.Precision.HIGHEST


def dot(a, b, dims):
    return lax.dot_general(a, b, (dims, ((), ())), precision=HIGHEST, preferred_element_type=jnp.float32)


def split(value):
    high = value.astype(jnp.bfloat16)
    rest = value - high.astype(jnp.float32)
    middle = rest.astype(jnp.bfloat16)
    return high, middle, (rest - middle.astype(jnp.float32)).astype(jnp.bfloat16)


def left_parts(parts):
    high, middle, low = parts
    return [high, high, middle, middle, high, low]


def right_parts(parts):
    high, middle, low = parts
    return [high, middle, high, middle, low, high]


def outer(left, right):
    left = jnp.concatenate(left_parts(left), axis=0)
    right = jnp.concatenate(right_parts(right), axis=0)
    return lax.dot_general(left, right, (((0,), (0,)), ((), ())), preferred_element_type=jnp.float32)


def product(left, right):
    left = jnp.concatenate(left_parts(left), axis=1)
    right = jnp.concatenate(right_parts(right), axis=0)
    return lax.dot_general(left, right, (((1,), (0,)), ((), ())), preferred_element_type=jnp.float32)


def swap_groups(arrays, group):
    count = len(arrays)
    lane = lax.broadcasted_iota(jnp.int32, arrays[0].shape, 1)
    bit = 1
    while bit < count:
        upper = (lane // (group * bit)) % 2 == 1
        out = list(arrays)
        for i in range(count):
            if i & bit == 0:
                low, high = arrays[i], arrays[i | bit]
                out[i] = jnp.where(upper, pltpu.roll(high, group * bit, 1), low)
                out[i | bit] = jnp.where(upper, high, pltpu.roll(low, LANES - group * bit, 1))
        arrays = out
        bit *= 2
    return arrays


def pack_kernel(nz, states_in, potential_in, out_ref, states, potential, arrived):
    halves = range(states.shape[0])
    fetches = [
        pltpu.make_async_copy(states_in.at[:, pl.ds(LANES * half, LANES)], states.at[half], arrived.at[half])
        for half in halves
    ]
    last = pltpu.make_async_copy(potential_in, potential, arrived.at[len(fetches)])
    for fetch in [last] + fetches:
        fetch.start()
    columns = states.shape[1] // nz
    row = lax.broadcasted_iota(jnp.int32, (nz, LANES), 0)
    lane = lax.broadcasted_iota(jnp.int32, (nz, LANES), 1)
    tiles = columns // TILE
    last.wait()
    packed = jnp.zeros((TILE, LANES), jnp.float32)
    for part in range(2):
        wide = jnp.zeros((potential.shape[1], LANES), jnp.float32)
        for x in range(potential.shape[0]):
            spread = jnp.where(lane == row + nz * x + LANES // 2 * part, 1.0, 0.0)
            wide = wide + dot(potential[x], spread, ((1,), (0,)))
        packed = packed + wide[TILE * part : TILE * (part + 1)]
    for i in range(out_ref.shape[0]):
        out_ref[i, tiles] = packed
    for half in halves:
        fetches[half].wait()
        arrays = [states[half, pl.ds(z, columns, stride=nz), :] for z in range(nz)]
        for g, value in enumerate(swap_groups(arrays, LANES // nz)):
            out_ref[half * nz + g, :tiles] = value.reshape(tiles, TILE, LANES)


def filter_kernel(nz, domains_y, size_x, size_y, in_ref, out_ref, field, potential):
    domains = in_ref.shape[0]
    total_x = size_x * (domains // domains_y)
    total_y = size_y * domains_y
    columns = size_x * size_y
    group = LANES // nz
    shares = out_ref.shape[0] // domains
    share = size_x // shares

    def place(i, x):
        return size_x * (i // domains_y) + x, size_y * (i % domains_y)

    def keep(which, x, rows, value):
        field[which, WIDTH + x, rows, :] = value
        if x < WIDTH:
            field[which, WIDTH + total_x + x, rows, :] = value
        if x >= total_x - WIDTH:
            field[which, WIDTH + x - total_x, rows, :] = value

    packed = in_ref[:, columns // TILE].reshape(domains * TILE, LANES)
    source = lax.broadcasted_iota(jnp.int32, (LANES, LANES), 0)
    target = lax.broadcasted_iota(jnp.int32, (LANES, LANES), 1)
    shape = (LANES, 2 * LANES * size_x)
    row = lax.broadcasted_iota(jnp.int32, shape, 0)
    lane = lax.broadcasted_iota(jnp.int32, shape, 1)
    held_at = nz * (lane // LANES // 2) + LANES // 2 * (lane // LANES % 2) + lane % LANES // group
    spread = jnp.where(row == held_at, 1.0, 0.0).astype(jnp.bfloat16)
    spread_all = lax.dot_general(
        jnp.concatenate(split(packed), axis=1),
        jnp.concatenate([spread] * 3, axis=0),
        (((1,), (0,)), ((), ())),
        preferred_element_type=jnp.float32,
    )
    for x in range(size_x):
        values = [spread_all[:, LANES * at : LANES * (at + 1)] for at in (2 * x, 2 * x + 1)]
        for i in range(domains):
            at_x, at_y = place(i, x)
            rows = slice(at_y, at_y + size_y)
            value = jnp.concatenate([part[TILE * i : TILE * (i + 1)] for part in values], axis=0)
            potential[at_x, rows, :] = value - centre_value
            keep(0, at_x, rows, in_ref[i, 2 * x : 2 * x + 2].reshape(size_y, LANES))

    def ring(distance, size):
        value = jnp.zeros(distance.shape, jnp.float32)
        for k in range(1, WIDTH + 1):
            for shift in (k, -k):
                value = value + jnp.where(distance == shift % size, coeffs[k], 0.0)
        return value

    along_z = ring((source // group - target // group + nz) % nz, nz)
    along_z = jnp.where((source - target) % group == 0, along_z, 0.0)
    along_z = along_z + jnp.where(source == target, 3.0 * coeffs[0], 0.0)
    along_z = jnp.concatenate(right_parts(split(along_z)), axis=0)
    shape = (total_y, PRODUCTS * total_y)
    row = lax.broadcasted_iota(jnp.int32, shape, 0)
    lane = lax.broadcasted_iota(jnp.int32, shape, 1)
    ring_y = ring((row - lane % total_y + total_y) % total_y, total_y)
    along_y = jnp.zeros(shape, jnp.float32)
    for part, value in enumerate(left_parts(split(ring_y))):
        along_y = jnp.where(lane // total_y == part, value.astype(jnp.float32), along_y)
    along_y = along_y.astype(jnp.bfloat16)

    together = math.gcd(total_x, 4)
    for step in range(DEGREE):
        now, other = step % 2, (step + 1) % 2
        scale = 1.0 / half_width if step == 0 else 2.0 / half_width
        for x in range(total_x):
            value = field[now, WIDTH + x]
            if x % together == 0:
                parts = [split(field[now, WIDTH + near]) for near in range(x, x + together)]
                sum_z = lax.dot_general(
                    jnp.concatenate([jnp.concatenate(left_parts(part), axis=1) for part in parts], axis=0),
                    along_z,
                    (((1,), (0,)), ((), ())),
                    preferred_element_type=jnp.float32,
                )
                sum_y = lax.dot_general(
                    along_y,
                    jnp.concatenate([jnp.concatenate(right_parts(part), axis=0) for part in parts], axis=1),
                    (((1,), (0,)), ((), ())),
                    preferred_element_type=jnp.float32,
                )
            n = x % together
            lap = sum_z[total_y * n : total_y * (n + 1)] + sum_y[:, LANES * n : LANES * (n + 1)]
            for k in range(1, WIDTH + 1):
                lap = lap + coeffs[k] * (field[now, WIDTH + x + k] + field[now, WIDTH + x - k])
            result = (potential[x] * value - 0.5 * lap) * scale
            if step > 0:
                result = result - field[other, WIDTH + x]
            if step + 1 < DEGREE:
                keep(other, x, slice(None), result)
                continue
            for j in range(domains_y):
                i = x // size_x * domains_y + j
                row = size_y * (x % share)
                out_ref[i * shares + x % size_x // share, row : row + size_y, :] = result[size_y * j : size_y * (j + 1)]


def unpack(nz, bands, in_ref, strip):
    per_band = in_ref.shape[0] // (nz * bands)
    first = nz * (strip % per_band)
    arrays = [in_ref[(first + g) * bands + strip // per_band] for g in range(nz)]
    return swap_groups(arrays, LANES // nz)


def unpack_kernel(nz, bands, in_ref, out_ref):
    for strip in range(out_ref.shape[0]):
        for z, value in enumerate(unpack(nz, bands, in_ref, strip)):
            out_ref[strip, pl.ds(z, in_ref.shape[1], stride=nz), :] = value


def upper_blocks(strips):
    return [(i, j) for i in range(strips) for j in range(i, strips)]


def share_of(strips, core):
    return upper_blocks(strips)[core :: CORES]


def layout(strips, core):
    pairs = share_of(strips, core)
    diagonal = [i for i, j in pairs if i == j]
    return (
        [(WHOLE, LANES, (i, j)) for i, j in pairs if i != j]
        + [(HALF, LANES // 2, (i, i)) for i in diagonal]
        + [(QUADRANTS, LANES // 2, (i, j)) for i, j in zip(diagonal[::2], diagonal[1::2])]
    )


def rows_of(strips, core):
    return sum(rows for _, rows, _ in layout(strips, core))


def gram_kernel(nz, bands, core_ref, own_ref, other_in, out_ref, other_ref):
    strips = own_ref.shape[0]
    unpack_kernel(nz, bands, other_in, other_ref)
    parts = [split(jnp.concatenate([own_ref[strip], other_ref[strip]], axis=0)) for strip in range(strips)]
    for core in range(CORES):

        @pl.when(core_ref[0] == core)
        def _(core=core):
            pairs = share_of(strips, core)
            blocks = {}
            for left in sorted({i for i, _ in pairs}):
                spots = [at for at, (i, _) in enumerate(pairs) if i == left]
                right = [jnp.concatenate([parts[pairs[at][1]][p] for at in spots], axis=1) for p in range(3)]
                value = product([part.T for part in parts[left]], right)
                for n, at in enumerate(spots):
                    blocks[pairs[at]] = value[:, LANES * n : LANES * (n + 1)]
            lane = lax.broadcasted_iota(jnp.int32, (LANES // 2, LANES), 1)
            at = 0
            for kind, rows, (i, j) in layout(strips, core):
                if kind == QUADRANTS:
                    first, second = blocks[i, i][LANES // 2 :], blocks[j, j][LANES // 2 :]
                    value = jnp.where(lane < LANES // 2, pltpu.roll(first, LANES // 2, 1), second)
                else:
                    value = blocks[i, j][:rows]
                out_ref[at : at + rows // TILE] = value.reshape(rows // TILE, TILE, LANES)
                at += rows // TILE


def sum_kernel(total, in_ref, out_ref):
    value = in_ref[0]
    for i in range(1, in_ref.shape[0]):
        value = value + in_ref[i]
    value = value / total
    for i in range(out_ref.shape[0]):
        out_ref[i] = value


def spread_row(value, row):
    return jnp.broadcast_to(value[row : row + 1, :], value.shape)


def eliminate(rows, start):
    rows = list(rows)
    tiles = len(rows)
    sublane = lax.broadcasted_iota(jnp.int32, (SUBLANES, LANES), 0)
    at = lax.broadcasted_iota(jnp.int32, (SUBLANES, LANES), 1) - start
    pivots = [jnp.ones((SUBLANES, LANES), jnp.float32) for _ in range(tiles)]
    for first in range(0, PANEL, PART):
        column = {
            (j, t): jnp.broadcast_to(rows[t][:, start + j : start + j + 1], (SUBLANES, LANES))
            for j in range(first, first + PART)
            for t in range(j // SUBLANES, tiles)
        }
        inside = (at >= first) & (at < first + PART)
        for t in range(tiles):
            rows[t] = jnp.where(inside, jnp.where(at == sublane + SUBLANES * t, 1.0, 0.0), rows[t])
        for k in range(first, first + PART):
            tile, row = k // SUBLANES, k % SUBLANES
            pivot = spread_row(column[k, tile], row)
            pivots[tile] = jnp.where(sublane == row, pivot, pivots[tile])
            over = 1.0 / pivot
            factor = {t: column[k, t] * over for t in range(tile, tiles)}
            for j in range(k + 1, first + PART):
                value = spread_row(column[k, j // SUBLANES], j % SUBLANES)
                for t in range(j // SUBLANES, tiles):
                    column[j, t] = column[j, t] - factor[t] * value
            factor[tile] = jnp.where(sublane > row, factor[tile], 0.0)
            value = spread_row(rows[tile], row)
            for t in range(tile, tiles):
                rows[t] = rows[t] - factor[t] * value
    return [rows[t] * lax.rsqrt(pivots[t]) for t in range(tiles)]


def inverse_of_block(value):
    rest = [value[t : t + SUBLANES] for t in range(0, LANES, SUBLANES)]
    lane = lax.broadcasted_iota(jnp.int32, (SUBLANES, LANES), 1)
    out = []
    for start in range(0, LANES, PANEL):
        end = start + PANEL
        rows = eliminate(rest[start // SUBLANES : end // SUBLANES], start)
        out += [jnp.where(lane < end, row, 0.0) for row in rows]
        if end < LANES:
            parts = split(jnp.concatenate(rows, axis=0))
            update = outer(parts, parts)
            for t in range(end // SUBLANES, LANES // SUBLANES):
                old = jnp.where((lane >= start) & (lane < end), 0.0, rest[t])
                rest[t] = old - update[SUBLANES * t : SUBLANES * (t + 1)]
    return jnp.concatenate(out, axis=0)


def beside(left, right):
    return tuple(jnp.concatenate(pair, axis=1) for pair in zip(left, right))


def inverse_factor(matrix, inverse):
    size = matrix.shape[0]
    for low in range(0, size, LANES):
        high = low + LANES
        rows = slice(low, high)
        block = inverse_of_block(matrix[rows, rows])
        left = split(block)
        inverse[rows, rows] = block
        if high < size:
            inverse[rows, high:] = jnp.zeros((LANES, size - high), jnp.float32)
            following = slice(high, high + LANES)
            above = split(product(left, split(matrix[rows, following])))
            matrix[following, following] = matrix[following, following] - outer(above, above)
            if high + LANES < size:
                above = beside(above, split(product(left, split(matrix[rows, high + LANES :]))))
        below = left
        if low:
            value = product(left, split(matrix[rows, :low]))
            inverse[rows, :low] = value
            below = beside(split(value), left)
        for at in range(high, size, LANES):
            mine = tuple(part[:, at - high : at - high + LANES] for part in above)
            target = slice(at, at + LANES)
            update = outer(mine, below)
            if low:
                matrix[target, :low] = matrix[target, :low] - update[:, :low]
            matrix[target, rows] = -update[:, low:]
            first = max(at, high + LANES)
            if first < size:
                update = outer(mine, tuple(part[:, first - high :] for part in above))
                matrix[target, first:] = matrix[target, first:] - update


def prepare_kernel(place_ref, own_ref, other_ref, *out_refs):
    strips, cells, _ = own_ref.shape
    band = place_ref[1]
    for strip in range(strips):
        for share, value in ((band, own_ref[strip]), (1 - band, other_ref[strip])):
            rows = pl.ds(pl.multiple_of(share * cells, cells), cells)
            for ref, part in zip(out_refs, split(value)):
                ref[strip, rows, :] = part


def finish_kernel(place_ref, mine_ref, theirs_ref, high_ref, middle_ref, low_ref, out_ref, matrix, inverse):
    strips = high_ref.shape[0]
    block = out_ref.shape[1]
    held = mine_ref.shape[1]
    for core in range(CORES):

        @pl.when(place_ref[0] == core)
        def _(core=core):
            for ref, holder in ((mine_ref, core), (theirs_ref, 1 - core)):
                tile = 0
                for kind, rows, (i, j) in layout(strips, holder):
                    for row in range(0, rows, SUBLANES):
                        value = jnp.concatenate([ref[t // held, t % held] for t in (tile, tile + 1)], axis=0)
                        tile += 2
                        targets = [(LANES * i + row, LANES * j, value)]
                        if kind == QUADRANTS:
                            row += LANES // 2
                            targets = [
                                (LANES * i + row, LANES * i, pltpu.roll(value, LANES // 2, 1)),
                                (LANES * j + row, LANES * j, value),
                            ]
                        for top, left, part in targets:
                            matrix[top : top + SUBLANES, left : left + LANES] = part

    inverse_factor(matrix, inverse)
    band = place_ref[1]
    for b in range(strips * LANES // block):

        @pl.when(band == b)
        def _(b=b):
            used = block * (b + 1)
            left = left_parts(
                [
                    jnp.concatenate([ref[s] for s in range(used // LANES)], axis=1)
                    for ref in (high_ref, middle_ref, low_ref)
                ]
            )
            right = right_parts(split(inverse[block * b : used, :used]))
            out_ref[...] = lax.dot_general(
                jnp.concatenate(left, axis=1),
                jnp.concatenate(right, axis=1),
                (((1,), (1,)), ((), ())),
                preferred_element_type=jnp.float32,
            )


def factor_kernel(in_ref, out_ref, matrix):
    matrix[...] = in_ref[...]
    inverse_factor(matrix, out_ref)


def call(kernel, shape, *args, scratch=(), scalars=0):
    specs = [SMEM] * scalars + [VMEM] * (len(args) - scalars)
    return pl.pallas_call(
        kernel,
        out_shape=jax.ShapeDtypeStruct(shape, jnp.float32),
        in_specs=specs,
        out_specs=VMEM,
        scratch_shapes=list(scratch),
        compiler_params=ROOM,
    )(*args)


def transposed(states, potential):
    size_x, size_y, nz, block = states.shape
    domains_y = lax.axis_size("dy")
    domains_x = lax.axis_size("chip") * CORES
    domains = domains_x * domains_y
    bands = lax.axis_size("band")
    cells = size_x * size_y * nz
    columns = size_x * size_y
    area = ("chip", "core", "dy")
    everyone = area + ("band",)
    same_core = ("chip", "dy", "band")
    swap = [(0, 1), (1, 0)]
    place = jnp.stack([lax.axis_index("core"), lax.axis_index("band")]).astype(jnp.int32)

    packed = pl.pallas_call(
        functools.partial(pack_kernel, nz),
        out_shape=jax.ShapeDtypeStruct((domains, columns // TILE + 1, TILE, LANES), jnp.float32),
        in_specs=[HBM, HBM],
        out_specs=VMEM,
        scratch_shapes=[
            pltpu.VMEM((block // LANES, cells, LANES), jnp.float32),
            pltpu.VMEM(potential.shape, jnp.float32),
            pltpu.SemaphoreType.DMA((block // LANES + 1,)),
        ],
        compiler_params=ROOM,
    )(*(pltpu.with_memory_space_constraint(v, pltpu.HBM) for v in (states.reshape(cells, block), potential)))
    packed = lax.all_to_all(packed, area, 0, 0, tiled=True)
    grid = (size_x * domains_x, size_y * domains_y, LANES)
    filtered = call(
        functools.partial(filter_kernel, nz, domains_y, size_x, size_y),
        (domains * bands, columns // bands, LANES),
        packed,
        scratch=[
            pltpu.VMEM((2, grid[0] + 2 * WIDTH) + grid[1:], jnp.float32),
            pltpu.VMEM(grid, jnp.float32),
        ],
    )
    filtered = lax.all_to_all(filtered, everyone, 0, 0, tiled=True)
    size = block * bands
    strips = size // LANES
    rows = rows_of(strips, 0)
    holders = domains * bands // CORES
    neighbours = lax.ppermute(filtered, "core", swap)
    split_cells = (strips, cells // bands, LANES)
    own = call(functools.partial(unpack_kernel, nz, bands), split_cells, filtered)
    partial = call(
        functools.partial(gram_kernel, nz, bands),
        (rows // TILE, TILE, LANES),
        place,
        own,
        neighbours,
        scratch=[pltpu.VMEM(split_cells, jnp.float32)],
        scalars=1,
    )
    other = lax.ppermute(own, "band", swap)
    partial = lax.all_to_all(partial.reshape(holders, rows // holders // TILE, TILE, LANES), same_core, 0, 0, tiled=True)
    pieces = call(functools.partial(sum_kernel, float(cells * domains)), partial.shape, partial)
    mine = lax.all_to_all(pieces, same_core, 0, 0, tiled=True)
    theirs = lax.ppermute(mine, "core", swap)
    whole_cells = (strips, cells, LANES)
    parts = pl.pallas_call(
        prepare_kernel,
        out_shape=[jax.ShapeDtypeStruct(whole_cells, jnp.bfloat16)] * 3,
        in_specs=[SMEM] + [VMEM] * 2,
        out_specs=[VMEM] * 3,
        compiler_params=ROOM,
    )(place, own, other)
    result = call(
        finish_kernel,
        (cells, block),
        place,
        mine,
        theirs,
        *parts,
        scratch=[pltpu.VMEM((size, size), jnp.float32)] * 2,
        scalars=1,
    )
    return result.reshape(states.shape)


def with_halo(cells, axis, dim, width):
    count = lax.axis_size(axis)
    size = cells.shape[dim]
    head = lax.slice_in_dim(cells, 0, width, axis=dim)
    tail = lax.slice_in_dim(cells, size - width, size, axis=dim)
    before = lax.ppermute(tail, axis, [(i, (i + 1) % count) for i in range(count)])
    after = lax.ppermute(head, axis, [((i + 1) % count, i) for i in range(count)])
    return jnp.concatenate([before, cells, after], axis=dim)


def apply_ham(field, potential):
    padded_x = with_halo(field, "dx", 0, WIDTH)
    padded_y = with_halo(field, "dy", 1, WIDTH)
    size_x = field.shape[0]
    size_y = field.shape[1]
    lap = 3.0 * coeffs[0] * field
    for shift in range(1, WIDTH + 1):
        near = (
            padded_x[WIDTH + shift : WIDTH + shift + size_x]
            + padded_x[WIDTH - shift : WIDTH - shift + size_x]
            + padded_y[:, WIDTH + shift : WIDTH + shift + size_y]
            + padded_y[:, WIDTH - shift : WIDTH - shift + size_y]
        )
        near = near + jnp.roll(field, shift, 2) + jnp.roll(field, -shift, 2)
        lap = lap + coeffs[shift] * near
    return -0.5 * lap + potential[..., None] * field


def haloed(states, potential):
    prev = states
    cur = (apply_ham(states, potential) - centre_value * states) / half_width
    for _ in range(1, DEGREE):
        nxt = 2.0 * (apply_ham(cur, potential) - centre_value * cur) / half_width - prev
        prev, cur = (cur, nxt)
    block = cur.shape[3]
    cells = cur.shape[0] * cur.shape[1] * cur.shape[2]
    local = cur.reshape(cells, block)
    gathered = lax.all_gather(local, "band", axis=1, tiled=True)
    total = cells * lax.axis_size("dx") * lax.axis_size("dy")
    partial = jnp.dot(gathered.T, gathered, precision=HIGHEST, preferred_element_type=jnp.float32) / total
    correlation = lax.psum(partial, ("dx", "dy"))
    size = correlation.shape[0]
    if size % LANES == 0:
        inverse = call(factor_kernel, (size, size), correlation, scratch=[pltpu.VMEM((size, size), jnp.float32)])
    else:
        factor = jnp.linalg.cholesky(correlation)
        inverse = jax.scipy.linalg.solve_triangular(factor, jnp.eye(size, dtype=jnp.float32), lower=True)
    my_rows = lax.dynamic_slice_in_dim(inverse, lax.axis_index("band") * block, block, 0)
    result = jnp.dot(gathered, my_rows.T, precision=HIGHEST, preferred_element_type=jnp.float32)
    return result.reshape(cur.shape)


def fits_cores(strips, devices):
    rows = {rows_of(strips, core) for core in range(CORES)}
    even = all(sum(i == j for i, j in share_of(strips, core)) % 2 == 0 for core in range(CORES))
    return even and len(rows) == 1 and rows.pop() % (devices // CORES * TILE) == 0


def solution(mesh):
    domains_x, domains_y, bands = (mesh.shape[name] for name in ("dx", "dy", "band"))
    domains = domains_x * domains_y

    def run(states, potential):
        total_x, total_y, nz, size = states.shape
        size_x, size_y, block = total_x // domains_x, total_y // domains_y, size // bands
        if (
            nz == SUBLANES
            and size_y == SUBLANES
            and 2 * nz * size_x <= LANES
            and block * nz == LANES * domains
            and block % LANES == 0
            and bands == 2
            and size_x % bands == 0
            and domains_x % CORES == 0
            and fits_cores(size // LANES, domains * bands)
            and total_x > 2 * WIDTH
            and total_y > 2 * WIDTH
        ):
            devices = mesh.devices.reshape(domains_x // CORES, CORES, domains_y, bands)
            body, over = transposed, jax.sharding.Mesh(devices, ("chip", "core", "dy", "band"))
            x_axis = ("chip", "core")
        else:
            body, over, x_axis = haloed, mesh, "dx"
        spec = P(x_axis, "dy", None, "band")
        step = jax.shard_map(
            body, mesh=over, in_specs=(spec, P(x_axis, "dy", None)), out_specs=spec, check_vma=False
        )
        return step(states, potential)

    return run
```

```python
import functools
import math

import jax
import jax.numpy as jnp
from jax import lax
from jax.experimental import pallas as pl
from jax.experimental.pallas import tpu as pltpu
from jax.sharding import PartitionSpec as P


DEGREE = 3
LANES = 128
SUBLANES = 8
PANEL = 32
PART = 16
CORES = 2
PRODUCTS = 6
TILE = SUBLANES // 2
WHOLE, HALF, QUADRANTS = range(3)

coeffs = (
    -5369.0 / 1800.0,
    12.0 / 7.0,
    -15.0 / 56.0,
    10.0 / 189.0,
    -1.0 / 112.0,
    2.0 / 1925.0,
    -1.0 / 16632.0,
)
WIDTH = len(coeffs) - 1
half_width = 5.0
centre_value = 7.0
VMEM = pl.BlockSpec(memory_space=pltpu.VMEM)
SMEM = pl.BlockSpec(memory_space=pltpu.SMEM)
HBM = pl.BlockSpec(memory_space=pltpu.HBM)
ROOM = pltpu.CompilerParams(vmem_limit_bytes=24 << 20)
HIGHEST = lax.Precision.HIGHEST


def dot(a, b, dims):
    return lax.dot_general(a, b, (dims, ((), ())), precision=HIGHEST, preferred_element_type=jnp.float32)


def split(value):
    high = value.astype(jnp.bfloat16)
    rest = value - high.astype(jnp.float32)
    middle = rest.astype(jnp.bfloat16)
    return high, middle, (rest - middle.astype(jnp.float32)).astype(jnp.bfloat16)


def left_parts(parts):
    high, middle, low = parts
    return [high, high, middle, middle, high, low]


def right_parts(parts):
    high, middle, low = parts
    return [high, middle, high, middle, low, high]


def outer(left, right):
    left = jnp.concatenate(left_parts(left), axis=0)
    right = jnp.concatenate(right_parts(right), axis=0)
    return lax.dot_general(left, right, (((0,), (0,)), ((), ())), preferred_element_type=jnp.float32)


def product(left, right):
    left = jnp.concatenate(left_parts(left), axis=1)
    right = jnp.concatenate(right_parts(right), axis=0)
    return lax.dot_general(left, right, (((1,), (0,)), ((), ())), preferred_element_type=jnp.float32)


def swap_groups(arrays, group):
    count = len(arrays)
    lane = lax.broadcasted_iota(jnp.int32, arrays[0].shape, 1)
    bit = 1
    while bit < count:
        upper = (lane // (group * bit)) % 2 == 1
        out = list(arrays)
        for i in range(count):
            if i & bit == 0:
                low, high = arrays[i], arrays[i | bit]
                out[i] = jnp.where(upper, pltpu.roll(high, group * bit, 1), low)
                out[i | bit] = jnp.where(upper, high, pltpu.roll(low, LANES - group * bit, 1))
        arrays = out
        bit *= 2
    return arrays


def pack_kernel(nz, states_in, potential_in, out_ref, states, potential, arrived):
    halves = range(states.shape[0])
    fetches = [
        pltpu.make_async_copy(states_in.at[:, pl.ds(LANES * half, LANES)], states.at[half], arrived.at[half])
        for half in halves
    ]
    last = pltpu.make_async_copy(potential_in, potential, arrived.at[len(fetches)])
    for fetch in [last] + fetches:
        fetch.start()
    columns = states.shape[1] // nz
    row = lax.broadcasted_iota(jnp.int32, (nz, LANES), 0)
    lane = lax.broadcasted_iota(jnp.int32, (nz, LANES), 1)
    tiles = columns // TILE
    last.wait()
    size_x, size_y, _ = potential.shape
    wide = dot(potential[...].reshape(size_x * size_y, nz), jnp.where(lane % nz == row, 1.0, 0.0), ((1,), (0,)))
    packed = jnp.zeros((size_y, LANES), jnp.float32)
    for x in range(size_x):
        packed = jnp.where(lane % (LANES // 2) // nz == x, wide[size_y * x : size_y * (x + 1)], packed)
    packed = jnp.where(lane[:TILE] < LANES // 2, packed[:TILE], packed[TILE:])
    for i in range(out_ref.shape[0]):
        out_ref[i, tiles] = packed
    for half in halves:
        fetches[half].wait()
        arrays = [states[half, pl.ds(z, columns, stride=nz), :] for z in range(nz)]
        for g, value in enumerate(swap_groups(arrays, LANES // nz)):
            out_ref[half * nz + g, :tiles] = value.reshape(tiles, TILE, LANES)


def filter_kernel(nz, domains_y, size_x, size_y, in_ref, out_ref, field, potential):
    domains = in_ref.shape[0]
    total_x = size_x * (domains // domains_y)
    total_y = size_y * domains_y
    columns = size_x * size_y
    group = LANES // nz
    shares = out_ref.shape[0] // domains
    share = size_x // shares

    def place(i, x):
        return size_x * (i // domains_y) + x, size_y * (i % domains_y)

    def keep(which, x, rows, value):
        field[which, WIDTH + x, rows, :] = value
        if x < WIDTH:
            field[which, WIDTH + total_x + x, rows, :] = value
        if x >= total_x - WIDTH:
            field[which, WIDTH + x - total_x, rows, :] = value

    packed = in_ref[:, columns // TILE].reshape(domains * TILE, LANES)
    source = lax.broadcasted_iota(jnp.int32, (LANES, LANES), 0)
    target = lax.broadcasted_iota(jnp.int32, (LANES, LANES), 1)
    shape = (LANES, 2 * LANES * size_x)
    row = lax.broadcasted_iota(jnp.int32, shape, 0)
    lane = lax.broadcasted_iota(jnp.int32, shape, 1)
    held_at = nz * (lane // LANES // 2) + LANES // 2 * (lane // LANES % 2) + lane % LANES // group
    spread = jnp.where(row == held_at, 1.0, 0.0).astype(jnp.bfloat16)
    spread_all = lax.dot_general(
        jnp.concatenate(split(packed), axis=1),
        jnp.concatenate([spread] * 3, axis=0),
        (((1,), (0,)), ((), ())),
        preferred_element_type=jnp.float32,
    )
    for x in range(size_x):
        values = [spread_all[:, LANES * at : LANES * (at + 1)] for at in (2 * x, 2 * x + 1)]
        for i in range(domains):
            at_x, at_y = place(i, x)
            rows = slice(at_y, at_y + size_y)
            value = jnp.concatenate([part[TILE * i : TILE * (i + 1)] for part in values], axis=0)
            potential[at_x, rows, :] = value - centre_value
            keep(0, at_x, rows, in_ref[i, 2 * x : 2 * x + 2].reshape(size_y, LANES))

    def ring(distance, size):
        value = jnp.zeros(distance.shape, jnp.float32)
        for k in range(1, WIDTH + 1):
            for shift in (k, -k):
                value = value + jnp.where(distance == shift % size, coeffs[k], 0.0)
        return value

    along_z = ring((source // group - target // group + nz) % nz, nz)
    along_z = jnp.where((source - target) % group == 0, along_z, 0.0)
    along_z = along_z + jnp.where(source == target, 3.0 * coeffs[0], 0.0)
    along_z = jnp.concatenate(right_parts(split(along_z)), axis=0)
    shape = (total_y, PRODUCTS * total_y)
    row = lax.broadcasted_iota(jnp.int32, shape, 0)
    lane = lax.broadcasted_iota(jnp.int32, shape, 1)
    ring_y = ring((row - lane % total_y + total_y) % total_y, total_y)
    along_y = jnp.zeros(shape, jnp.float32)
    for part, value in enumerate(left_parts(split(ring_y))):
        along_y = jnp.where(lane // total_y == part, value.astype(jnp.float32), along_y)
    along_y = along_y.astype(jnp.bfloat16)

    together = math.gcd(total_x, 4)
    for step in range(DEGREE):
        now, other = step % 2, (step + 1) % 2
        scale = 1.0 / half_width if step == 0 else 2.0 / half_width
        for x in range(total_x):
            value = field[now, WIDTH + x]
            if x % together == 0:
                parts = [split(field[now, WIDTH + near]) for near in range(x, x + together)]
                sum_z = lax.dot_general(
                    jnp.concatenate([jnp.concatenate(left_parts(part), axis=1) for part in parts], axis=0),
                    along_z,
                    (((1,), (0,)), ((), ())),
                    preferred_element_type=jnp.float32,
                )
                sum_y = lax.dot_general(
                    along_y,
                    jnp.concatenate([jnp.concatenate(right_parts(part), axis=0) for part in parts], axis=1),
                    (((1,), (0,)), ((), ())),
                    preferred_element_type=jnp.float32,
                )
            n = x % together
            lap = sum_z[total_y * n : total_y * (n + 1)] + sum_y[:, LANES * n : LANES * (n + 1)]
            for k in range(1, WIDTH + 1):
                lap = lap + coeffs[k] * (field[now, WIDTH + x + k] + field[now, WIDTH + x - k])
            result = (potential[x] * value - 0.5 * lap) * scale
            if step > 0:
                result = result - field[other, WIDTH + x]
            if step + 1 < DEGREE:
                keep(other, x, slice(None), result)
                continue
            for j in range(domains_y):
                i = x // size_x * domains_y + j
                row = size_y * (x % share)
                out_ref[i * shares + x % size_x // share, row : row + size_y, :] = result[size_y * j : size_y * (j + 1)]


def unpack(nz, bands, in_ref, strip):
    per_band = in_ref.shape[0] // (nz * bands)
    first = nz * (strip % per_band)
    arrays = [in_ref[(first + g) * bands + strip // per_band] for g in range(nz)]
    return swap_groups(arrays, LANES // nz)


def unpack_kernel(nz, bands, in_ref, out_ref):
    for strip in range(out_ref.shape[0]):
        for z, value in enumerate(unpack(nz, bands, in_ref, strip)):
            out_ref[strip, pl.ds(z, in_ref.shape[1], stride=nz), :] = value


def upper_blocks(strips):
    return [(i, j) for i in range(strips) for j in range(i, strips)]


def share_of(strips, core):
    return upper_blocks(strips)[core :: CORES]


def layout(strips, core):
    pairs = share_of(strips, core)
    diagonal = [i for i, j in pairs if i == j]
    return (
        [(WHOLE, LANES, (i, j)) for i, j in pairs if i != j]
        + [(HALF, LANES // 2, (i, i)) for i in diagonal]
        + [(QUADRANTS, LANES // 2, (i, j)) for i, j in zip(diagonal[::2], diagonal[1::2])]
    )


def rows_of(strips, core):
    return sum(rows for _, rows, _ in layout(strips, core))


def gram_kernel(nz, bands, core_ref, own_ref, other_in, out_ref, other_ref):
    strips = own_ref.shape[0]
    unpack_kernel(nz, bands, other_in, other_ref)
    parts = [split(jnp.concatenate([own_ref[strip], other_ref[strip]], axis=0)) for strip in range(strips)]
    for core in range(CORES):

        @pl.when(core_ref[0] == core)
        def _(core=core):
            pairs = share_of(strips, core)
            blocks = {}
            for left in sorted({i for i, _ in pairs}):
                spots = [at for at, (i, _) in enumerate(pairs) if i == left]
                right = [jnp.concatenate([parts[pairs[at][1]][p] for at in spots], axis=1) for p in range(3)]
                value = product([part.T for part in parts[left]], right)
                for n, at in enumerate(spots):
                    blocks[pairs[at]] = value[:, LANES * n : LANES * (n + 1)]
            lane = lax.broadcasted_iota(jnp.int32, (LANES // 2, LANES), 1)
            at = 0
            for kind, rows, (i, j) in layout(strips, core):
                if kind == QUADRANTS:
                    first, second = blocks[i, i][LANES // 2 :], blocks[j, j][LANES // 2 :]
                    value = jnp.where(lane < LANES // 2, pltpu.roll(first, LANES // 2, 1), second)
                else:
                    value = blocks[i, j][:rows]
                out_ref[at : at + rows // TILE] = value.reshape(rows // TILE, TILE, LANES)
                at += rows // TILE


def sum_kernel(total, in_ref, out_ref):
    value = in_ref[0]
    for i in range(1, in_ref.shape[0]):
        value = value + in_ref[i]
    value = value / total
    for i in range(out_ref.shape[0]):
        out_ref[i] = value


def spread_row(value, row):
    return jnp.broadcast_to(value[row : row + 1, :], value.shape)


def eliminate(rows, start):
    rows = list(rows)
    tiles = len(rows)
    sublane = lax.broadcasted_iota(jnp.int32, (SUBLANES, LANES), 0)
    at = lax.broadcasted_iota(jnp.int32, (SUBLANES, LANES), 1) - start
    pivots = [jnp.ones((SUBLANES, LANES), jnp.float32) for _ in range(tiles)]
    for first in range(0, PANEL, PART):
        column = {
            (j, t): jnp.broadcast_to(rows[t][:, start + j : start + j + 1], (SUBLANES, LANES))
            for j in range(first, first + PART)
            for t in range(j // SUBLANES, tiles)
        }
        inside = (at >= first) & (at < first + PART)
        for t in range(tiles):
            rows[t] = jnp.where(inside, jnp.where(at == sublane + SUBLANES * t, 1.0, 0.0), rows[t])
        for k in range(first, first + PART):
            tile, row = k // SUBLANES, k % SUBLANES
            pivot = spread_row(column[k, tile], row)
            pivots[tile] = jnp.where(sublane == row, pivot, pivots[tile])
            over = 1.0 / pivot
            factor = {t: column[k, t] * over for t in range(tile, tiles)}
            for j in range(k + 1, first + PART):
                value = spread_row(column[k, j // SUBLANES], j % SUBLANES)
                for t in range(j // SUBLANES, tiles):
                    column[j, t] = column[j, t] - factor[t] * value
            factor[tile] = jnp.where(sublane > row, factor[tile], 0.0)
            value = spread_row(rows[tile], row)
            for t in range(tile, tiles):
                rows[t] = rows[t] - factor[t] * value
    return [rows[t] * lax.rsqrt(pivots[t]) for t in range(tiles)]


def inverse_of_block(value):
    rest = [value[t : t + SUBLANES] for t in range(0, LANES, SUBLANES)]
    lane = lax.broadcasted_iota(jnp.int32, (SUBLANES, LANES), 1)
    out = []
    for start in range(0, LANES, PANEL):
        end = start + PANEL
        rows = eliminate(rest[start // SUBLANES : end // SUBLANES], start)
        out += [jnp.where(lane < end, row, 0.0) for row in rows]
        if end < LANES:
            parts = split(jnp.concatenate(rows, axis=0))
            update = outer(parts, parts)
            for t in range(end // SUBLANES, LANES // SUBLANES):
                old = jnp.where((lane >= start) & (lane < end), 0.0, rest[t])
                rest[t] = old - update[SUBLANES * t : SUBLANES * (t + 1)]
    return jnp.concatenate(out, axis=0)


def beside(left, right):
    return tuple(jnp.concatenate(pair, axis=1) for pair in zip(left, right))


def inverse_factor(matrix, inverse):
    size = matrix.shape[0]
    for low in range(0, size, LANES):
        high = low + LANES
        rows = slice(low, high)
        block = inverse_of_block(matrix[rows, rows])
        left = split(block)
        inverse[rows, rows] = block
        if high < size:
            inverse[rows, high:] = jnp.zeros((LANES, size - high), jnp.float32)
            following = slice(high, high + LANES)
            above = split(product(left, split(matrix[rows, following])))
            matrix[following, following] = matrix[following, following] - outer(above, above)
            if high + LANES < size:
                above = beside(above, split(product(left, split(matrix[rows, high + LANES :]))))
        below = left
        if low:
            value = product(left, split(matrix[rows, :low]))
            inverse[rows, :low] = value
            below = beside(split(value), left)
        for at in range(high, size, LANES):
            mine = tuple(part[:, at - high : at - high + LANES] for part in above)
            target = slice(at, at + LANES)
            update = outer(mine, below)
            if low:
                matrix[target, :low] = matrix[target, :low] - update[:, :low]
            matrix[target, rows] = -update[:, low:]
            first = max(at, high + LANES)
            if first < size:
                update = outer(mine, tuple(part[:, first - high :] for part in above))
                matrix[target, first:] = matrix[target, first:] - update


def prepare_kernel(place_ref, own_ref, other_ref, *out_refs):
    strips, cells, _ = own_ref.shape
    band = place_ref[1]
    for strip in range(strips):
        for share, value in ((band, own_ref[strip]), (1 - band, other_ref[strip])):
            rows = pl.ds(pl.multiple_of(share * cells, cells), cells)
            for ref, part in zip(out_refs, split(value)):
                ref[strip, rows, :] = part


def finish_kernel(place_ref, mine_ref, theirs_ref, high_ref, middle_ref, low_ref, out_ref, matrix, inverse):
    strips = high_ref.shape[0]
    block = out_ref.shape[1]
    held = mine_ref.shape[1]
    for core in range(CORES):

        @pl.when(place_ref[0] == core)
        def _(core=core):
            for ref, holder in ((mine_ref, core), (theirs_ref, 1 - core)):
                tile = 0
                for kind, rows, (i, j) in layout(strips, holder):
                    for row in range(0, rows, SUBLANES):
                        value = jnp.concatenate([ref[t // held, t % held] for t in (tile, tile + 1)], axis=0)
                        tile += 2
                        targets = [(LANES * i + row, LANES * j, value)]
                        if kind == QUADRANTS:
                            row += LANES // 2
                            targets = [
                                (LANES * i + row, LANES * i, pltpu.roll(value, LANES // 2, 1)),
                                (LANES * j + row, LANES * j, value),
                            ]
                        for top, left, part in targets:
                            matrix[top : top + SUBLANES, left : left + LANES] = part

    inverse_factor(matrix, inverse)
    band = place_ref[1]
    for b in range(strips * LANES // block):

        @pl.when(band == b)
        def _(b=b):
            used = block * (b + 1)
            left = left_parts(
                [
                    jnp.concatenate([ref[s] for s in range(used // LANES)], axis=1)
                    for ref in (high_ref, middle_ref, low_ref)
                ]
            )
            right = right_parts(split(inverse[block * b : used, :used]))
            out_ref[...] = lax.dot_general(
                jnp.concatenate(left, axis=1),
                jnp.concatenate(right, axis=1),
                (((1,), (1,)), ((), ())),
                preferred_element_type=jnp.float32,
            )


def factor_kernel(in_ref, out_ref, matrix):
    matrix[...] = in_ref[...]
    inverse_factor(matrix, out_ref)


def call(kernel, shape, *args, scratch=(), scalars=0):
    specs = [SMEM] * scalars + [VMEM] * (len(args) - scalars)
    return pl.pallas_call(
        kernel,
        out_shape=jax.ShapeDtypeStruct(shape, jnp.float32),
        in_specs=specs,
        out_specs=VMEM,
        scratch_shapes=list(scratch),
        compiler_params=ROOM,
    )(*args)


def transposed(states, potential):
    size_x, size_y, nz, block = states.shape
    domains_y = lax.axis_size("dy")
    domains_x = lax.axis_size("chip") * CORES
    domains = domains_x * domains_y
    bands = lax.axis_size("band")
    cells = size_x * size_y * nz
    columns = size_x * size_y
    area = ("chip", "core", "dy")
    everyone = area + ("band",)
    same_core = ("chip", "dy", "band")
    swap = [(0, 1), (1, 0)]
    place = jnp.stack([lax.axis_index("core"), lax.axis_index("band")]).astype(jnp.int32)

    packed = pl.pallas_call(
        functools.partial(pack_kernel, nz),
        out_shape=jax.ShapeDtypeStruct((domains, columns // TILE + 1, TILE, LANES), jnp.float32),
        in_specs=[HBM, HBM],
        out_specs=VMEM,
        scratch_shapes=[
            pltpu.VMEM((block // LANES, cells, LANES), jnp.float32),
            pltpu.VMEM(potential.shape, jnp.float32),
            pltpu.SemaphoreType.DMA((block // LANES + 1,)),
        ],
        compiler_params=ROOM,
    )(*(pltpu.with_memory_space_constraint(v, pltpu.HBM) for v in (states.reshape(cells, block), potential)))
    packed = lax.all_to_all(packed, area, 0, 0, tiled=True)
    grid = (size_x * domains_x, size_y * domains_y, LANES)
    filtered = call(
        functools.partial(filter_kernel, nz, domains_y, size_x, size_y),
        (domains * bands, columns // bands, LANES),
        packed,
        scratch=[
            pltpu.VMEM((2, grid[0] + 2 * WIDTH) + grid[1:], jnp.float32),
            pltpu.VMEM(grid, jnp.float32),
        ],
    )
    filtered = lax.all_to_all(filtered, everyone, 0, 0, tiled=True)
    size = block * bands
    strips = size // LANES
    rows = rows_of(strips, 0)
    holders = domains * bands // CORES
    neighbours = lax.ppermute(filtered, "core", swap)
    split_cells = (strips, cells // bands, LANES)
    own = call(functools.partial(unpack_kernel, nz, bands), split_cells, filtered)
    partial = call(
        functools.partial(gram_kernel, nz, bands),
        (rows // TILE, TILE, LANES),
        place,
        own,
        neighbours,
        scratch=[pltpu.VMEM(split_cells, jnp.float32)],
        scalars=1,
    )
    other = lax.ppermute(own, "band", swap)
    partial = lax.all_to_all(partial.reshape(holders, rows // holders // TILE, TILE, LANES), same_core, 0, 0, tiled=True)
    pieces = call(functools.partial(sum_kernel, float(cells * domains)), partial.shape, partial)
    mine = lax.all_to_all(pieces, same_core, 0, 0, tiled=True)
    theirs = lax.ppermute(mine, "core", swap)
    whole_cells = (strips, cells, LANES)
    parts = pl.pallas_call(
        prepare_kernel,
        out_shape=[jax.ShapeDtypeStruct(whole_cells, jnp.bfloat16)] * 3,
        in_specs=[SMEM] + [VMEM] * 2,
        out_specs=[VMEM] * 3,
        compiler_params=ROOM,
    )(place, own, other)
    result = call(
        finish_kernel,
        (cells, block),
        place,
        mine,
        theirs,
        *parts,
        scratch=[pltpu.VMEM((size, size), jnp.float32)] * 2,
        scalars=1,
    )
    return result.reshape(states.shape)


def with_halo(cells, axis, dim, width):
    count = lax.axis_size(axis)
    size = cells.shape[dim]
    head = lax.slice_in_dim(cells, 0, width, axis=dim)
    tail = lax.slice_in_dim(cells, size - width, size, axis=dim)
    before = lax.ppermute(tail, axis, [(i, (i + 1) % count) for i in range(count)])
    after = lax.ppermute(head, axis, [((i + 1) % count, i) for i in range(count)])
    return jnp.concatenate([before, cells, after], axis=dim)


def apply_ham(field, potential):
    padded_x = with_halo(field, "dx", 0, WIDTH)
    padded_y = with_halo(field, "dy", 1, WIDTH)
    size_x = field.shape[0]
    size_y = field.shape[1]
    lap = 3.0 * coeffs[0] * field
    for shift in range(1, WIDTH + 1):
        near = (
            padded_x[WIDTH + shift : WIDTH + shift + size_x]
            + padded_x[WIDTH - shift : WIDTH - shift + size_x]
            + padded_y[:, WIDTH + shift : WIDTH + shift + size_y]
            + padded_y[:, WIDTH - shift : WIDTH - shift + size_y]
        )
        near = near + jnp.roll(field, shift, 2) + jnp.roll(field, -shift, 2)
        lap = lap + coeffs[shift] * near
    return -0.5 * lap + potential[..., None] * field


def haloed(states, potential):
    prev = states
    cur = (apply_ham(states, potential) - centre_value * states) / half_width
    for _ in range(1, DEGREE):
        nxt = 2.0 * (apply_ham(cur, potential) - centre_value * cur) / half_width - prev
        prev, cur = (cur, nxt)
    block = cur.shape[3]
    cells = cur.shape[0] * cur.shape[1] * cur.shape[2]
    local = cur.reshape(cells, block)
    gathered = lax.all_gather(local, "band", axis=1, tiled=True)
    total = cells * lax.axis_size("dx") * lax.axis_size("dy")
    partial = jnp.dot(gathered.T, gathered, precision=HIGHEST, preferred_element_type=jnp.float32) / total
    correlation = lax.psum(partial, ("dx", "dy"))
    size = correlation.shape[0]
    if size % LANES == 0:
        inverse = call(factor_kernel, (size, size), correlation, scratch=[pltpu.VMEM((size, size), jnp.float32)])
    else:
        factor = jnp.linalg.cholesky(correlation)
        inverse = jax.scipy.linalg.solve_triangular(factor, jnp.eye(size, dtype=jnp.float32), lower=True)
    my_rows = lax.dynamic_slice_in_dim(inverse, lax.axis_index("band") * block, block, 0)
    result = jnp.dot(gathered, my_rows.T, precision=HIGHEST, preferred_element_type=jnp.float32)
    return result.reshape(cur.shape)


def fits_cores(strips, devices):
    rows = {rows_of(strips, core) for core in range(CORES)}
    even = all(sum(i == j for i, j in share_of(strips, core)) % 2 == 0 for core in range(CORES))
    return even and len(rows) == 1 and rows.pop() % (devices // CORES * TILE) == 0


def solution(mesh):
    domains_x, domains_y, bands = (mesh.shape[name] for name in ("dx", "dy", "band"))
    domains = domains_x * domains_y

    def run(states, potential):
        total_x, total_y, nz, size = states.shape
        size_x, size_y, block = total_x // domains_x, total_y // domains_y, size // bands
        if (
            nz == SUBLANES
            and size_y == SUBLANES
            and 2 * nz * size_x <= LANES
            and block * nz == LANES * domains
            and block % LANES == 0
            and bands == 2
            and size_x % bands == 0
            and domains_x % CORES == 0
            and fits_cores(size // LANES, domains * bands)
            and total_x > 2 * WIDTH
            and total_y > 2 * WIDTH
        ):
            devices = mesh.devices.reshape(domains_x // CORES, CORES, domains_y, bands)
            body, over = transposed, jax.sharding.Mesh(devices, ("chip", "core", "dy", "band"))
            x_axis = ("chip", "core")
        else:
            body, over, x_axis = haloed, mesh, "dx"
        spec = P(x_axis, "dy", None, "band")
        step = jax.shard_map(
            body, mesh=over, in_specs=(spec, P(x_axis, "dy", None)), out_specs=spec, check_vma=False
        )
        return step(states, potential)

    return run
```
